32 devices in a mesh: row: 4 (over y, x), col: 8 (over z, core).
Axes of the slice: x: 2, y: 2, z: 4, core: 2. Of those that a mesh axis runs over, the one named last changes fastest.
Arguments:
- layer_input: bfloat16 [8192, 2048], P(('row', 'col')), may hold values from -6 to 6
- per_layer_input: bfloat16 [8192, 256], P(('row', 'col')), may hold values from -6 to 6
- out_cotangent: bfloat16 [8192, 2048], P(('row', 'col')), may hold values from -6 to 6
- seq_lengths: int32 [4, 3], P('row'), may hold values from 1 to 1024, 2048 in all within a row
- query_weight: bfloat16 [2048, 2048], P('row', 'col'), may hold values from -0.125 to 0.125
- key_weight: bfloat16 [2048, 512], P('row', 'col'), may hold values from -0.125 to 0.125
- value_weight: bfloat16 [2048, 512], P('row', 'col'), may hold values from -0.125 to 0.125
- out_weight: bfloat16 [2048, 2048], P('row', 'col'), may hold values from -0.125 to 0.125
- gate_weight: bfloat16 [2048, 8192], P('row', 'col'), may hold values from -0.125 to 0.125
- up_weight: bfloat16 [2048, 8192], P('row', 'col'), may hold values from -0.125 to 0.125
- down_weight: bfloat16 [2048, 8192], P('row', 'col'), may hold values from -0.0625 to 0.0625
- laurel_down: bfloat16 [2048, 64], P(('row', 'col')), may hold values from -0.125 to 0.125
- laurel_up: bfloat16 [2048, 64], P(('row', 'col')), may hold values from -0.75 to 0.75
- per_layer_gate: bfloat16 [2048, 256], P(('row', 'col')), may hold values from -0.125 to 0.125
- per_layer_projection: bfloat16 [2048, 256], P(('row', 'col')), may hold values from -0.375 to 0.375
- input_gain: bfloat16 [2048], P(('row', 'col')), may hold values from 0.099609375 to 1.8984375
- query_gain: bfloat16 [256], P(('row', 'col')), may hold values from 0.099609375 to 1.8984375
- key_gain: bfloat16 [256], P(('row', 'col')), may hold values from 0.099609375 to 1.8984375
- attention_gain: bfloat16 [2048], P(('row', 'col')), may hold values from 0.099609375 to 1.8984375
- laurel_gain: bfloat16 [2048], P(('row', 'col')), may hold values from 0.099609375 to 1.8984375
- pre_feed_gain: bfloat16 [2048], P(('row', 'col')), may hold values from 0.099609375 to 1.8984375
- post_feed_gain: bfloat16 [2048], P(('row', 'col')), may hold values from 0.099609375 to 1.8984375
- per_layer_gain: bfloat16 [2048], P(('row', 'col')), may hold values from 0.099609375 to 1.8984375
Outputs:
- layer_output: bfloat16 [8192, 2048], P(('row', 'col'))
- input_grad: bfloat16 [8192, 2048], P(('row', 'col'))
- per_layer_grad: bfloat16 [8192, 256], P(('row', 'col'))
- query_weight_grad: float32 [2048, 2048], P('row', 'col')
- key_weight_grad: float32 [2048, 512], P('row', 'col')
- value_weight_grad: float32 [2048, 512], P('row', 'col')
- out_weight_grad: float32 [2048, 2048], P('row', 'col')
- gate_weight_grad: float32 [2048, 8192], P('row', 'col')
- up_weight_grad: float32 [2048, 8192], P('row', 'col')
- down_weight_grad: float32 [2048, 8192], P('row', 'col')
- laurel_down_grad: float32 [2048, 64], P(('row', 'col'))
- laurel_up_grad: float32 [2048, 64], P(('row', 'col'))
- per_layer_gate_grad: float32 [2048, 256], P(('row', 'col'))
- per_layer_projection_grad: float32 [2048, 256], P(('row', 'col'))
- input_gain_grad: float32 [2048], P(('row', 'col'))
- query_gain_grad: float32 [256], P(('row', 'col'))
- key_gain_grad: float32 [256], P(('row', 'col'))
- attention_gain_grad: float32 [2048], P(('row', 'col'))
- laurel_gain_grad: float32 [2048], P(('row', 'col'))
- pre_feed_gain_grad: float32 [2048], P(('row', 'col'))
- post_feed_gain_grad: float32 [2048], P(('row', 'col'))
- per_layer_gain_grad: float32 [2048], P(('row', 'col'))
The draws below stay inside these ranges and needn't reach their ends.
Inputs may be any that keep to these rules, and one draw needn't show every extreme that they name: `seq_lengths`: row r holds the lengths of the 3 sequences of row group r in token order; they sum to 2048, and the longest is exactly 1024.
All inputs are finite; a program needn't handle non-finite values.
Results may differ from the reference program's by a relative error of at most 0.025.
Values may be sent and summed in bfloat16 or wider, within the bound.
No kernel may reach another device: no remote copies, remote signals or barrier semaphores. Data moves between devices by JAX's collectives and lax.ppermute only.
A program may use at most 320 MiB of HBM per device.

```python
import math
import jax
import jax.numpy as jnp
import numpy as np
from jax import lax

D = 2048
HEADS = 8
KV_HEADS = 2
HEAD = 256
FF = 8192
RANK = 64
PLE = 256
BLOCK = 256
TOK_ROW = 2048
TOKENS = 8192
SEQS = 3
LONGEST = 1024
N_ROW = 4


def level_of(rng, shape, cuts, low, largest):
    def one(dim, parts):
        heights = jax.random.uniform(jax.random.fold_in(jax.random.fold_in(rng, 6), dim), (parts,), jnp.float32, low / len(cuts), largest / len(cuts))
        return jnp.repeat(jnp.exp(heights), shape[dim] // parts).reshape((-1,) + (1,) * (len(shape) - dim - 1))

    level = one(*cuts[0])
    for cut in cuts[1:]:
        level = level * one(*cut)
    return level


def profile(count, total, limit, slope):
    weights = [(1 << 20) // math.isqrt(rank ** slope) + 1 for rank in range(2, count + 1)]
    rest, given = total - limit - (count - 1), [1] * (count - 1)
    while rest > 0:
        free = [i for i in range(count - 1) if given[i] < limit]
        pool, remaining = sum([weights[i] for i in free]), rest
        for i in free:
            extra = min(limit - given[i], max(1, remaining * weights[i] // pool), rest)
            given[i] = given[i] + extra
            rest = rest - extra
    return np.array([limit] + given)


def ragged_sizes(rng, number_of, total, limit, slope):
    if number_of == 2:
        one = jax.random.randint(rng, (), max(1, total - limit), min(limit, total - 1) + 1)
        return jnp.stack([one, total - one])
    sizes = jnp.asarray(profile(number_of, total, limit, slope), jnp.int32)
    twos = (number_of - 1) // 2
    donor, sink = sizes[1:1 + 2 * twos:2], sizes[2:2 + 2 * twos:2]
    room = jnp.minimum(donor - 1, limit - sink)
    shifted = jax.random.randint(jax.random.fold_in(rng, 1), (twos,), 0, 1 << 20) % (room + 1)
    sizes = sizes.at[1:1 + 2 * twos:2].set(donor - shifted).at[2:2 + 2 * twos:2].set(sink + shifted)
    return sizes[jax.random.permutation(jax.random.fold_in(rng, 2), number_of)]


def scatter_about(stream_key, shape, width, bound, cuts=(), held_as=jnp.bfloat16):
    array = width * jax.random.normal(stream_key, shape, jnp.float32)
    if cuts:
        array = array * level_of(stream_key, shape, cuts, -0.22, 0.18)
    return jnp.clip(array, -bound, bound).astype(held_as)


def setup_inputs(seed: int = 0) -> dict:
    splits = jax.random.split(jax.random.key(seed), 24)
    return {
        "layer_input": scatter_about(splits[0], (TOKENS, D), 1.0, 6.0, ((0, 32),)),
        "per_layer_input": scatter_about(splits[1], (TOKENS, PLE), 1.0, 6.0, ((0, 32),)),
        "out_cotangent": scatter_about(splits[2], (TOKENS, D), 1.0, 6.0, ((0, 32),)),
        "seq_lengths": jax.vmap(lambda own: ragged_sizes(own, SEQS, TOK_ROW, LONGEST, 1))(jax.random.split(splits[3], N_ROW)).reshape((N_ROW, SEQS)).astype(jnp.int32),
        "query_weight": scatter_about(splits[4], (D, HEADS * HEAD), D ** -0.5, 0.125, ((0, 4), (1, 8))),
        "key_weight": scatter_about(splits[5], (D, KV_HEADS * HEAD), D ** -0.5, 0.125, ((0, 4), (1, 8))),
        "value_weight": scatter_about(splits[6], (D, KV_HEADS * HEAD), D ** -0.5, 0.125, ((0, 4), (1, 8))),
        "out_weight": scatter_about(splits[7], (D, HEADS * HEAD), (HEADS * HEAD) ** -0.5, 0.125, ((0, 4), (1, 8))),
        "gate_weight": scatter_about(splits[8], (D, FF), D ** -0.5, 0.125, ((0, 4), (1, 8))),
        "up_weight": scatter_about(splits[9], (D, FF), D ** -0.5, 0.125, ((0, 4), (1, 8))),
        "down_weight": scatter_about(splits[10], (D, FF), FF ** -0.5, 0.0625, ((0, 4), (1, 8))),
        "laurel_down": scatter_about(splits[11], (D, RANK), D ** -0.5, 0.125, ((0, 32),)),
        "laurel_up": scatter_about(splits[12], (D, RANK), RANK ** -0.5, 0.75, ((0, 32),)),
        "per_layer_gate": scatter_about(splits[13], (D, PLE), D ** -0.5, 0.125, ((0, 32),)),
        "per_layer_projection": scatter_about(splits[14], (D, PLE), PLE ** -0.5, 0.375, ((0, 32),)),
        "input_gain": jnp.clip(1.0 + 0.18 * jax.random.normal(splits[15], (D,), jnp.float32), 0.099609375, 1.8984375).astype(jnp.bfloat16),
        "query_gain": jnp.clip(1.0 + 0.18 * jax.random.normal(splits[16], (HEAD,), jnp.float32), 0.099609375, 1.8984375).astype(jnp.bfloat16),
        "key_gain": jnp.clip(1.0 + 0.18 * jax.random.normal(splits[17], (HEAD,), jnp.float32), 0.099609375, 1.8984375).astype(jnp.bfloat16),
        "attention_gain": jnp.clip(1.0 + 0.18 * jax.random.normal(splits[18], (D,), jnp.float32), 0.099609375, 1.8984375).astype(jnp.bfloat16),
        "laurel_gain": jnp.clip(1.0 + 0.18 * jax.random.normal(splits[19], (D,), jnp.float32), 0.099609375, 1.8984375).astype(jnp.bfloat16),
        "pre_feed_gain": jnp.clip(1.0 + 0.18 * jax.random.normal(splits[20], (D,), jnp.float32), 0.099609375, 1.8984375).astype(jnp.bfloat16),
        "post_feed_gain": jnp.clip(1.0 + 0.18 * jax.random.normal(splits[21], (D,), jnp.float32), 0.099609375, 1.8984375).astype(jnp.bfloat16),
        "per_layer_gain": jnp.clip(1.0 + 0.18 * jax.random.normal(splits[22], (D,), jnp.float32), 0.099609375, 1.8984375).astype(jnp.bfloat16),
    }


NORM_EPS = 1e-06
ROOT_HALF = 0.7071067811865476
ROPE_THETA = 1000000.0
NEGATIVE = -1e+30
PRECISE = lax.Precision.HIGHEST

@jax.custom_vjp
def low(v):
    return lax.optimization_barrier(v.astype(jnp.bfloat16)).astype(jnp.float32)

@jax.custom_vjp
def low_back(v):
    return v

def low_keep(v):
    return (low(v), None)

def low_pass(kept, grad):
    return (grad,)

def back_keep(v):
    return (v, None)

def back_low(kept, grad):
    return (low(grad),)
low.defvjp(low_keep, low_pass)
low_back.defvjp(back_keep, back_low)

def matmul(left, right):
    return jnp.dot(left, right, precision=PRECISE, preferred_element_type=jnp.float32)

def matmul_t(left, right):
    return lax.dot_general(left, right, (((1,), (1,)), ((), ())), precision=PRECISE, preferred_element_type=jnp.float32)

def rms_scale(values, scale_gain):
    return values * lax.rsqrt(lax.optimization_barrier(jnp.mean(values * values, axis=-1, keepdims=True)) + NORM_EPS) * scale_gain

def rms_plain(values):
    return values * lax.rsqrt(lax.optimization_barrier(jnp.mean(values * values, axis=-1, keepdims=True)) + NORM_EPS)

def rotate(values, position):
    half_width = values.shape[-1] // 2
    steps_up = jnp.arange(half_width, dtype=jnp.float32)
    frequency = jnp.exp(steps_up * (-2.0 * math.log(ROPE_THETA) / values.shape[-1]))
    angle_grid = position.astype(jnp.float32)[:, None] * frequency[None, :]
    cosine = jnp.cos(angle_grid)[:, None, :]
    sine_part = jnp.sin(angle_grid)[:, None, :]
    first_half = values[..., :half_width]
    second_half = values[..., half_width:]
    return jnp.concatenate([first_half * cosine - second_half * sine_part, second_half * cosine + first_half * sine_part], axis=-1)

def head_prepare(projected, head_gain, position):
    shaped = projected.reshape(projected.shape[0], -1, HEAD)
    return rotate(rms_scale(shaped, head_gain), position)

def placement_info(lengths, token_count):
    finish = jnp.cumsum(lengths).astype(jnp.int32)
    begins = (finish - lengths).astype(jnp.int32)
    tokens_at = jnp.arange(token_count, dtype=jnp.int32)
    segment = lax.optimization_barrier(jnp.sum((tokens_at[:, None] >= finish[None, :]).astype(jnp.int32), axis=1)).astype(jnp.int32)
    chosen = segment[:, None] == jnp.arange(lengths.shape[0], dtype=jnp.int32)[None, :]
    offset = lax.optimization_barrier(jnp.sum(jnp.where(chosen, begins[None, :], 0), axis=1)).astype(jnp.int32)
    return (segment, (tokens_at - offset).astype(jnp.int32))

def geglu(gate_in, up_in):
    return jax.nn.gelu(gate_in, approximate=True) * up_in

def attend(query_rot, key_rot, values, segment, position):
    token_count = query_rot.shape[0]
    block_rows = min(512, token_count)
    score_scale = 1.0 / math.sqrt(HEAD)
    query_blocks = query_rot.reshape(token_count // block_rows, block_rows, KV_HEADS, HEADS // KV_HEADS, HEAD)
    segment_blocks = segment.reshape(token_count // block_rows, block_rows)
    position_blocks = position.reshape(token_count // block_rows, block_rows)
    key_block = position // BLOCK

    def one_block(pieces):
        query_block, query_segment, query_position = pieces
        scores = jnp.einsum('qhgd,khd->hgqk', query_block, key_rot, precision=PRECISE, preferred_element_type=jnp.float32)
        scores = low_back(scores * score_scale)
        allowed = (query_segment[:, None] == segment[None, :]) & (key_block[None, :] <= (query_position // BLOCK)[:, None])
        scores = jnp.where(allowed[None, None], scores, NEGATIVE)
        weights = low(jax.nn.softmax(scores, axis=-1))
        return jnp.einsum('hgqk,khd->qhgd', weights, values, precision=PRECISE, preferred_element_type=jnp.float32)
    outputs = lax.map(jax.checkpoint(one_block), (query_blocks, segment_blocks, position_blocks))
    return outputs.reshape(token_count, HEADS * HEAD)

def layer_group(params, inputs, embeds, lengths):
    query_weight, key_weight, value_weight, out_weight, gate_weight, up_weight, down_weight, laurel_down, laurel_up, per_layer_gate, per_layer_projection, input_gain, query_gain, key_gain, attention_gain, laurel_gain, pre_feed_gain, post_feed_gain, per_layer_gain = params
    token_count = inputs.shape[0]
    segment, position = placement_info(lengths, token_count)
    normed = low(rms_scale(inputs, input_gain))
    query = low(low_back(matmul(normed, query_weight)))
    key_proj = low(low_back(matmul(normed, key_weight)))
    value_proj = low(low_back(matmul(normed, value_weight)))
    query_rot = low(head_prepare(query, query_gain, position))
    key_rot = low(head_prepare(key_proj, key_gain, position))
    value_normed = low(rms_plain(value_proj.reshape(token_count, KV_HEADS, HEAD)))
    query_rot = query_rot.reshape(token_count, KV_HEADS, HEADS // KV_HEADS, HEAD)
    attended = attend(query_rot, key_rot, value_normed, segment, position)
    attended = low(low_back(attended))
    attention_out = low_back(matmul_t(attended, out_weight))
    laurel_mid = low(low_back(matmul(normed, laurel_down)))
    laurel_out = low_back(matmul_t(laurel_mid, laurel_up))
    mixed = (inputs + rms_scale(attention_out, attention_gain) + normed + rms_scale(laurel_out, laurel_gain)) * ROOT_HALF
    feed_in = low(rms_scale(mixed, pre_feed_gain))
    gate = low_back(matmul(feed_in, gate_weight))
    up_part = low_back(matmul(feed_in, up_weight))
    hidden = low(geglu(gate, up_part))
    down_out = low_back(matmul_t(hidden, down_weight))
    after_feed = mixed + rms_scale(down_out, post_feed_gain)
    after_low = low(after_feed)
    per_pre = low_back(matmul(after_low, per_layer_gate))
    per_hidden = low(geglu(per_pre, embeds))
    per_out = low_back(matmul_t(per_hidden, per_layer_projection))
    return after_feed + rms_scale(per_out, per_layer_gain)

def reference(layer_input, per_layer_input, out_cotangent, seq_lengths, query_weight, key_weight, value_weight, out_weight, gate_weight, up_weight, down_weight, laurel_down, laurel_up, per_layer_gate, per_layer_projection, input_gain, query_gain, key_gain, attention_gain, laurel_gain, pre_feed_gain, post_feed_gain, per_layer_gain):
    supplied = (query_weight, key_weight, value_weight, out_weight, gate_weight, up_weight, down_weight, laurel_down, laurel_up, per_layer_gate, per_layer_projection, input_gain, query_gain, key_gain, attention_gain, laurel_gain, pre_feed_gain, post_feed_gain, per_layer_gain)
    params = tuple((weight_item.astype(jnp.float32) for weight_item in supplied))
    inputs = layer_input.astype(jnp.float32).reshape(N_ROW, TOK_ROW, D)
    embeds = per_layer_input.astype(jnp.float32).reshape(N_ROW, TOK_ROW, PLE)
    cotangent = out_cotangent.astype(jnp.float32).reshape(N_ROW, TOK_ROW, D)

    def forward(weight_set, group_inputs, group_embeds):

        def one_group(pieces):
            return layer_group(weight_set, pieces[0], pieces[1], pieces[2])
        return lax.map(jax.checkpoint(one_group), (group_inputs, group_embeds, seq_lengths))
    outputs, pull_back = jax.vjp(forward, params, inputs, embeds)
    gradients, input_part, embed_part = pull_back(cotangent)
    return (outputs.reshape(TOKENS, D).astype(jnp.bfloat16), input_part.reshape(TOKENS, D).astype(jnp.bfloat16), embed_part.reshape(TOKENS, PLE).astype(jnp.bfloat16), gradients[0], gradients[1], gradients[2], gradients[3], gradients[4], gradients[5], gradients[6], gradients[7], gradients[8], gradients[9], gradients[10], gradients[11], gradients[12], gradients[13], gradients[14], gradients[15], gradients[16], gradients[17], gradients[18])
```

```python
from functools import partial
import math

import jax
import jax.numpy as jnp
from jax import lax
from jax.experimental import pallas as pl
from jax.experimental.pallas import tpu as pltpu
from jax.sharding import PartitionSpec as P

HEADS = 8
KV_HEADS = 2
HEAD = 256
BLOCK = 256


NORM_EPS = 1e-06
ROOT_HALF = 0.7071067811865476
ROPE_THETA = 1000000.0


def rms_scale(values, scale_gain):
    return (
        values
        * lax.rsqrt(jnp.mean(values * values, axis=-1, keepdims=True) + NORM_EPS)
        * scale_gain
    )


def rms_plain(values):
    return values * lax.rsqrt(jnp.mean(values * values, axis=-1, keepdims=True) + NORM_EPS)


def rotate(values, position):
    half_width = values.shape[-1] // 2
    steps_up = jnp.arange(half_width, dtype=jnp.float32)
    frequency = jnp.exp(steps_up * (-2.0 * math.log(ROPE_THETA) / values.shape[-1]))
    angle_grid = position.astype(jnp.float32)[:, None] * frequency[None, :]
    cosine = jnp.cos(angle_grid)[:, None, :]
    sine_part = jnp.sin(angle_grid)[:, None, :]
    first_half = values[..., :half_width]
    second_half = values[..., half_width:]
    return jnp.concatenate(
        [
            first_half * cosine - second_half * sine_part,
            second_half * cosine + first_half * sine_part,
        ],
        axis=-1,
    )


def head_prepare(projected, head_gain, position):
    shaped = projected.reshape(projected.shape[0], -1, HEAD)
    return rotate(rms_scale(shaped, head_gain), position)


def placement_info(lengths, tokens_at):
    finish = jnp.cumsum(lengths)
    begins = finish - lengths
    segment = jnp.sum((tokens_at[:, None] >= finish[None, :]).astype(jnp.int32), axis=1)
    chosen = segment[:, None] == jnp.arange(lengths.shape[0], dtype=jnp.int32)[None, :]
    begin = jnp.sum(jnp.where(chosen, begins[None, :], 0), axis=1)
    end = jnp.sum(jnp.where(chosen, finish[None, :], 0), axis=1)
    position = tokens_at - begin
    reach = jnp.minimum(end, begin + (position // BLOCK + 1) * BLOCK)
    return (position, begin, reach)


def geglu(gate_in, up_in):
    return jax.nn.gelu(gate_in, approximate=True) * up_in


def residual_mix(inputs, attention_out, normed, laurel_out, attention_gain, laurel_gain, pre_gain):
    mixed = (
        inputs
        + rms_scale(attention_out, attention_gain)
        + normed
        + rms_scale(laurel_out, laurel_gain)
    ) * ROOT_HALF
    return (mixed, rms_scale(mixed, pre_gain))


def feed_mix(mixed, down_out, post_gain):
    return mixed + rms_scale(down_out, post_gain)


def final_mix(after_feed, per_out, final_gain):
    return after_feed + rms_scale(per_out, final_gain)


def product(left, right):
    return jnp.dot(left, right, preferred_element_type=jnp.float32)


def product_t(left, right):
    return lax.dot_general(
        left, right, (((1,), (1,)), ((), ())), preferred_element_type=jnp.float32
    )


def product_tn(left, right):
    return lax.dot_general(
        left, right, (((0,), (0,)), ((), ())), preferred_element_type=jnp.float32
    )


def hop(values, axis, mask):
    size = lax.axis_size(axis)
    return lax.ppermute(values, axis, [(i, i ^ mask) for i in range(size)])


def after(values, *others):
    return lax.optimization_barrier((values,) + others)[0]


def xor_blocks(values, me, count):
    width = values.shape[-1] // count
    blocks = [values[..., i * width : (i + 1) * width] for i in range(count)]
    bit = 1
    while bit < count:
        flip = (me & bit) != 0
        blocks = [jnp.where(flip, blocks[i ^ bit], blocks[i]) for i in range(count)]
        bit *= 2
    return jnp.concatenate(blocks, axis=-1)


def xor_gather(piece, axis, count, unit):
    if count == 4:
        half = piece.shape[0] // 2
        near = hop(piece, axis, unit)
        far = hop(piece, axis, 2 * unit)
        upper = hop(near[:half], axis, 2 * unit)
        lower = hop(far[half:], axis, unit)
        return [piece, near, far, jnp.concatenate([upper, lower], axis=0)]
    pieces = [piece]
    bit = 1
    while bit < count:
        pieces = pieces + [hop(one, axis, bit * unit) for one in pieces]
        bit *= 2
    return pieces


def add_low(left, right):
    return (left.astype(jnp.float32) + right.astype(jnp.float32)).astype(jnp.bfloat16)


def xor_scatter(parts, axis, unit):
    count = len(parts)
    if count == 4:
        half = parts[0].shape[0] // 2
        upper = hop(parts[3][:half], axis, 2 * unit)
        lower = hop(parts[3][half:], axis, unit)
        near_low = hop(parts[1][half:], axis, unit)
        far_up = hop(parts[2][:half], axis, 2 * unit)
        near_up = hop(add_low(parts[1][:half], upper), axis, unit)
        far_low = hop(add_low(parts[2][half:], lower), axis, 2 * unit)
        own = parts[0].astype(jnp.float32)
        top = own[:half] + near_up.astype(jnp.float32) + far_up.astype(jnp.float32)
        bottom = own[half:] + near_low.astype(jnp.float32) + far_low.astype(jnp.float32)
        return jnp.concatenate([top, bottom], axis=0)
    bit = count // 2
    while bit > 0:
        parts = [add_low(parts[j], hop(parts[j + bit], axis, bit * unit)) for j in range(bit)]
        bit //= 2
    return parts[0].astype(jnp.float32)


def gather_cols(shard, pairs, row_total, dep=None):
    along = xor_gather(shard, "col", pairs, 2)
    height = shard.shape[0]
    stacked = jnp.concatenate(along, axis=0)
    if dep is not None:
        stacked = after(stacked, dep)
    mine = xor_gather(stacked, "row", row_total, 1)
    other = [hop(one, "col", 1) for one in mine]
    rows = []
    for r in range(row_total):
        blocks = []
        for z in range(pairs):
            for side in (mine, other):
                blocks.append(side[r][z * height : (z + 1) * height])
        rows.append(jnp.concatenate(blocks, axis=1))
    return jnp.concatenate(rows, axis=0), mine[-1]


def gather_rows(shard, row_total, dep):
    pieces = xor_gather(after(shard, dep), "row", row_total, 1)
    return jnp.concatenate(pieces, axis=0), pieces[-1]


def scatter_rows(total, row_total):
    height = total.shape[0] // row_total
    return xor_scatter([total[r * height : (r + 1) * height] for r in range(row_total)], "row", 1)


def scatter_cols(total, row_total, pairs):
    mine = scatter_rows(total, row_total).astype(jnp.bfloat16)
    width = mine.shape[1] // pairs
    return xor_scatter([mine[:, z * width : (z + 1) * width] for z in range(pairs)], "col", 2)


def pair_columns(columns, count):
    width = columns.shape[1] // count
    keep = [columns[:, j * width : (j + 1) * width] for j in range(0, count, 2)]
    give = [columns[:, j * width : (j + 1) * width] for j in range(1, count, 2)]
    other = hop(jnp.concatenate(give, axis=1), "col", 1)
    return jnp.concatenate([jnp.concatenate(keep, axis=1), other], axis=0)


def pair_rows(own):
    return jnp.concatenate([own, hop(own, "col", 1)], axis=0)


def attend_body(span_ref, window_ref, query_ref, key_ref, value_ref, out_ref, inverse_ref, sums, weights):
    rows = query_ref.shape[0]
    low_edge = window_ref[:, 0:1]
    high_edge = window_ref[:, 1:2]
    query = query_ref[...]
    sums[...] = jnp.zeros_like(sums)
    weights[...] = jnp.zeros_like(weights)

    def one_tile(tile, carry):
        scores = lax.dot_general(
            query, key_ref[tile], (((1,), (1,)), ((), ())), preferred_element_type=jnp.float32
        )
        place = tile * rows + lax.broadcasted_iota(jnp.int32, scores.shape, 1)
        exps = jnp.where((place >= low_edge) & (place < high_edge), jnp.exp(scores), 0.0)
        part = exps[:, :128]
        for start in range(128, rows, 128):
            part = part + exps[:, start : start + 128]
        weights[...] += part
        sums[...] += jnp.dot(
            exps.astype(jnp.bfloat16), value_ref[tile], preferred_element_type=jnp.float32
        )
        return carry

    lax.fori_loop(span_ref[0], span_ref[1], one_tile, 0)
    inverse = 1.0 / jnp.sum(weights[...], axis=1, keepdims=True)
    out_ref[...] = (sums[...] * inverse).astype(jnp.bfloat16)
    inverse_ref[...] = jnp.broadcast_to(inverse, inverse_ref.shape)


def attend(span, window, query, gathered):
    rows, width = query.shape
    tiles = gathered.shape[0]
    groups = HEADS // KV_HEADS
    half = pl.BlockSpec((rows, HEAD), lambda h, s: (0, h))
    flops = 4 * rows * rows * tiles * width
    return pl.pallas_call(
        attend_body,
        out_shape=(
            jax.ShapeDtypeStruct((rows, width), jnp.bfloat16),
            jax.ShapeDtypeStruct((rows, HEADS * 128), jnp.float32),
        ),
        grid_spec=pltpu.PrefetchScalarGridSpec(
            num_scalar_prefetch=1,
            grid=(HEADS,),
            in_specs=[
                pl.BlockSpec((rows, 2), lambda h, s: (0, 0)),
                half,
                pl.BlockSpec((tiles, None, rows, HEAD), lambda h, s: (0, 0, 0, h // groups)),
                pl.BlockSpec((tiles, None, rows, HEAD), lambda h, s: (0, 1, 0, h // groups)),
            ],
            out_specs=(half, pl.BlockSpec((rows, 128), lambda h, s: (0, h))),
            scratch_shapes=[
                pltpu.VMEM((rows, HEAD), jnp.float32),
                pltpu.VMEM((rows, 128), jnp.float32),
            ],
        ),
        cost_estimate=pl.CostEstimate(
            flops=flops, transcendentals=rows * rows * tiles * HEADS, bytes_accessed=8 * rows * width
        ),
        name="attend",
    )(span, window, query, gathered, gathered)


def attend_back_body(
    span_ref, window_ref, query_ref, key_ref, value_ref, grad_ref, out_ref, inverse_ref,
    query_grad_ref, pair_grad_ref, query_sum, key_sum, value_sum,
):
    rows = query_ref.shape[0]
    groups = HEADS // KV_HEADS
    head = pl.program_id(0)
    low_edge = window_ref[0:1, :]
    high_edge = window_ref[1:2, :]
    query = query_ref[...]
    grad_wide = grad_ref[...].astype(jnp.float32)
    inverse = inverse_ref[:, 0:1]
    delta = jnp.sum(grad_wide * out_ref[...].astype(jnp.float32), axis=1, keepdims=True) * inverse
    delta_row = jnp.transpose(jnp.broadcast_to(delta, (rows, 128)))[0:1, :]
    grad_scaled = (grad_wide * inverse).astype(jnp.bfloat16)
    query_sum[...] = jnp.zeros_like(query_sum)

    @pl.when(lax.rem(head, groups) == 0)
    def _():
        key_sum[...] = jnp.zeros_like(key_sum)
        value_sum[...] = jnp.zeros_like(value_sum)

    def one_tile(tile, carry):
        keys = key_ref[tile]
        contract_last = (((1,), (1,)), ((), ()))
        scores = lax.dot_general(keys, query, contract_last, preferred_element_type=jnp.float32)
        place = tile * rows + lax.broadcasted_iota(jnp.int32, scores.shape, 0)
        exps = jnp.where((place >= low_edge) & (place < high_edge), jnp.exp(scores), 0.0)
        prob_grad = lax.dot_general(
            value_ref[tile], grad_scaled, contract_last, preferred_element_type=jnp.float32
        )
        score_grad = (exps * (prob_grad - delta_row)).astype(jnp.bfloat16)
        key_sum[tile] += jnp.dot(score_grad, query, preferred_element_type=jnp.float32)
        value_sum[tile] += jnp.dot(
            exps.astype(jnp.bfloat16), grad_scaled, preferred_element_type=jnp.float32
        )
        query_sum[...] += lax.dot_general(
            score_grad, keys, (((0,), (0,)), ((), ())), preferred_element_type=jnp.float32
        )
        return carry

    lax.fori_loop(span_ref[0], span_ref[1], one_tile, 0)
    query_grad_ref[...] = query_sum[...] * (1.0 / math.sqrt(HEAD))

    @pl.when(lax.rem(head, groups) == groups - 1)
    def _():
        pair_grad_ref[:, 0] = key_sum[...].astype(jnp.bfloat16)
        pair_grad_ref[:, 1] = value_sum[...].astype(jnp.bfloat16)


def attend_back(span, window, query, gathered, grad, out, inverse):
    rows, width = query.shape
    tiles = gathered.shape[0]
    groups = HEADS // KV_HEADS
    half = pl.BlockSpec((rows, HEAD), lambda h, s: (0, h))
    return pl.pallas_call(
        attend_back_body,
        out_shape=(
            jax.ShapeDtypeStruct((rows, width), jnp.float32),
            jax.ShapeDtypeStruct(gathered.shape, jnp.bfloat16),
        ),
        grid_spec=pltpu.PrefetchScalarGridSpec(
            num_scalar_prefetch=1,
            grid=(HEADS,),
            in_specs=[
                pl.BlockSpec((2, rows), lambda h, s: (0, 0)),
                half,
                pl.BlockSpec((tiles, None, rows, HEAD), lambda h, s: (0, 0, 0, h // groups)),
                pl.BlockSpec((tiles, None, rows, HEAD), lambda h, s: (0, 1, 0, h // groups)),
                half,
                half,
                pl.BlockSpec((rows, 128), lambda h, s: (0, h)),
            ],
            out_specs=(
                half,
                pl.BlockSpec((tiles, 2, rows, HEAD), lambda h, s: (0, 0, 0, h // groups)),
            ),
            scratch_shapes=[
                pltpu.VMEM((rows, HEAD), jnp.float32),
                pltpu.VMEM((tiles, rows, HEAD), jnp.float32),
                pltpu.VMEM((tiles, rows, HEAD), jnp.float32),
            ],
        ),
        cost_estimate=pl.CostEstimate(
            flops=10 * rows * rows * tiles * width,
            transcendentals=rows * rows * tiles * HEADS,
            bytes_accessed=16 * rows * width,
        ),
        name="attend_back",
    )(span, window, query, gathered, gathered, grad, out, inverse)


def local(
    layer_input,
    per_layer_input,
    out_cotangent,
    seq_lengths,
    query_weight,
    key_weight,
    value_weight,
    out_weight,
    gate_weight,
    up_weight,
    down_weight,
    laurel_down,
    laurel_up,
    per_layer_gate,
    per_layer_projection,
    input_gain,
    query_gain,
    key_gain,
    attention_gain,
    laurel_gain,
    pre_feed_gain,
    post_feed_gain,
    per_layer_gain,
):
    rows, width = layer_input.shape
    row_total = lax.axis_size("row")
    col_total = lax.axis_size("col")
    pairs = col_total // 2
    me_row = lax.axis_index("row")
    me_col = lax.axis_index("col")
    rank = laurel_down.shape[1]
    embed = per_layer_gate.shape[1]
    kv_width = key_weight.shape[1]
    feed_width = gate_weight.shape[1]
    low = jnp.bfloat16
    wide = jnp.float32

    kv_all, kv_last = gather_cols(
        jnp.concatenate([key_weight, value_weight], axis=1), pairs, row_total
    )
    query_all, query_last = gather_cols(query_weight, pairs, row_total, kv_last)

    small_rows = laurel_down.shape[0]
    head_part = query_gain.shape[0]
    gains_own = jnp.concatenate(
        [
            input_gain,
            attention_gain,
            laurel_gain,
            pre_feed_gain,
            post_feed_gain,
            per_layer_gain,
            query_gain,
            key_gain,
        ]
    )
    gain_total = gains_own.shape[0]
    matrices_own = jnp.concatenate(
        [laurel_down, laurel_up, per_layer_gate, per_layer_projection], axis=1
    )
    small_width = matrices_own.shape[1]
    gains_block = jnp.pad(gains_own[None, :], ((0, 15), (0, small_width - gain_total)))
    small_own = jnp.concatenate([matrices_own, gains_block], axis=0)
    small_group = lax.all_gather(small_own, "col", axis=0, tiled=True)
    small_pieces = xor_gather(small_group, "row", row_total, 1)
    small_pieces = [one.reshape(col_total, small_rows + 16, small_width) for one in small_pieces]
    matrices = jnp.concatenate(
        [one[:, :small_rows].reshape(-1, small_width) for one in small_pieces], axis=0
    )
    laurel_down_all = matrices[:, :rank]
    laurel_up_all = matrices[:, rank : 2 * rank]
    layer_gate_all = matrices[:, 2 * rank : 2 * rank + embed]
    layer_proj_all = matrices[:, 2 * rank + embed :]
    gain_rows = [one[:, small_rows, :].astype(wide) for one in small_pieces]
    gain_list = [
        jnp.concatenate(
            [one[:, i * small_rows : (i + 1) * small_rows].reshape(-1) for one in gain_rows]
        )
        for i in range(6)
    ]
    head_gains = []
    for i in range(2):
        start = 6 * small_rows + i * head_part
        rel = jnp.concatenate([one[:, start : start + head_part].reshape(-1) for one in gain_rows])
        head_gains.append(xor_blocks(rel, me_row, row_total))

    out_all, out_last = gather_cols(out_weight, pairs, row_total, query_last)
    feed_all, feed_last = gather_rows(
        jnp.concatenate([gate_weight, up_weight], axis=1), row_total, out_last
    )
    down_all, down_last = gather_rows(down_weight, row_total, feed_last)

    tokens_at = me_col * rows + jnp.arange(rows, dtype=jnp.int32)
    position, begin, reach = placement_info(seq_lengths[0], tokens_at)
    window = jnp.stack([begin, reach])
    span = jnp.stack([jnp.min(begin) // rows, (jnp.max(reach) + rows - 1) // rows])
    inputs = xor_blocks(layer_input, me_row, row_total).astype(wide)
    cotangent = xor_blocks(out_cotangent, me_row, row_total).astype(wide)
    normed, input_pull = jax.vjp(rms_scale, inputs, gain_list[0])
    normed_low = normed.astype(low)
    kv_own = xor_blocks(product(normed_low, kv_all).astype(low), me_col, col_total)
    kv_own = kv_own.reshape(rows, col_total, 2 * kv_width)
    key_own = kv_own[:, :, :kv_width].reshape(rows, KV_HEADS * HEAD)
    value_own = kv_own[:, :, kv_width:].reshape(rows, KV_HEADS * HEAD)
    key_rot, key_pull = jax.vjp(
        partial(head_prepare, position=position), key_own.astype(wide), head_gains[1]
    )
    value_normed, value_pull = jax.vjp(
        rms_plain, value_own.astype(wide).reshape(rows, KV_HEADS, HEAD)
    )
    pair_own = jnp.stack(
        [
            key_rot.astype(low).reshape(rows, KV_HEADS * HEAD),
            value_normed.astype(low).reshape(rows, KV_HEADS * HEAD),
        ]
    )
    pair_all = lax.all_gather(pair_own, "col", axis=0, tiled=True)
    pair_all = pair_all.reshape(col_total, 2, rows, KV_HEADS * HEAD)
    query_own = xor_blocks(product(normed_low, query_all).astype(low), me_col, col_total)
    query_rot, query_pull = jax.vjp(
        partial(head_prepare, position=position), query_own.astype(wide), head_gains[0]
    )
    query_scaled = query_rot.astype(low).reshape(rows, HEADS * HEAD) * low(1.0 / math.sqrt(HEAD))
    attended, inverse = attend(span, jnp.transpose(window), query_scaled, pair_all)
    attended_rel = xor_blocks(attended, me_col, col_total)
    attention_out = product_t(attended_rel, out_all)
    laurel_mid = product(normed_low, laurel_down_all).astype(low)
    laurel_out = product_t(laurel_mid, laurel_up_all)
    (mixed, feed_in), mix_pull = jax.vjp(
        residual_mix,
        inputs,
        attention_out,
        normed_low.astype(wide),
        laurel_out,
        gain_list[1],
        gain_list[2],
        gain_list[3],
    )
    feed_low = feed_in.astype(low)
    feed_tokens = lax.all_gather(feed_low, "col", axis=0, tiled=True)
    gate_up = product(feed_tokens, feed_all).astype(low)
    gate = gate_up[:, :feed_width].astype(wide)
    up = gate_up[:, feed_width:].astype(wide)
    hidden, hidden_pull = jax.vjp(geglu, gate, up)
    hidden_low = hidden.astype(low)
    down_out = lax.psum_scatter(
        product_t(hidden_low, down_all).astype(low), "col", scatter_dimension=0, tiled=True
    ).astype(wide)
    after_feed, feed_pull = jax.vjp(feed_mix, mixed, down_out, gain_list[4])
    after_low = after_feed.astype(low)
    per_pre = product(after_low, layer_gate_all)
    per_hidden, per_pull = jax.vjp(geglu, per_pre, per_layer_input.astype(wide))
    per_low = per_hidden.astype(low)
    per_out = product_t(per_low, layer_proj_all)
    output, final_pull = jax.vjp(final_mix, after_feed, per_out, gain_list[5])
    after_grad, per_out_grad, final_gain_grad = final_pull(cotangent)
    per_out_low = per_out_grad.astype(low)
    per_hidden_grad = product(per_out_low, layer_proj_all)
    layer_proj_grad = product_tn(per_out_low, per_low)
    per_pre_grad, embed_grad = per_pull(per_hidden_grad)
    per_pre_low = per_pre_grad.astype(low)
    after_grad = after_grad + product_t(per_pre_low, layer_gate_all)
    layer_gate_grad = product_tn(after_low, per_pre_low)
    mixed_grad, down_grad, post_gain_grad = feed_pull(after_grad)
    down_low = down_grad.astype(low)
    down_tokens = lax.all_gather(down_low, "col", axis=0, tiled=True)
    hidden_grad = product(down_tokens, down_all)
    gate_grad, up_grad = hidden_pull(hidden_grad)
    feed_grad_low = jnp.concatenate([gate_grad.astype(low), up_grad.astype(low)], axis=1)
    feed_in_grad = lax.psum_scatter(
        product_t(feed_grad_low, feed_all).astype(low), "col", scatter_dimension=0, tiled=True
    ).astype(wide)
    down_total = product_tn(down_tokens, hidden_low).astype(low)
    down_weight_grad = scatter_rows(down_total, row_total)
    feed_total = product_tn(feed_tokens, feed_grad_low).astype(low)
    feed_weight_grad = scatter_rows(feed_total, row_total)
    (
        inputs_grad,
        attention_grad,
        normed_grad,
        laurel_out_grad,
        attention_gain_grad,
        laurel_gain_grad,
        pre_gain_grad,
    ) = mix_pull((mixed_grad, feed_in_grad))
    attention_low = attention_grad.astype(low)
    attended_grad = xor_blocks(product(attention_low, out_all).astype(low), me_col, col_total)
    query_rot_grad, pair_parts = attend_back(
        span, window, query_scaled, pair_all, attended_grad, attended, inverse
    )
    pair_sum = lax.psum_scatter(
        pair_parts.reshape(2 * col_total, rows, KV_HEADS * HEAD),
        "col",
        scatter_dimension=0,
        tiled=True,
    ).astype(wide)
    out_total = product_tn(pair_rows(attention_low), pair_columns(attended_rel, col_total))
    out_weight_grad = scatter_cols(out_total.astype(low), row_total, pairs)
    normed_pair = pair_rows(normed_low)
    query_grad, query_gain_grad = query_pull(query_rot_grad.reshape(rows, HEADS, HEAD))
    query_rel = xor_blocks(query_grad.astype(low), me_col, col_total)
    query_total = product_tn(normed_pair, pair_columns(query_rel, col_total))
    query_weight_grad = scatter_cols(query_total.astype(low), row_total, pairs)

    laurel_out_low = laurel_out_grad.astype(low)
    laurel_mid_grad = product(laurel_out_low, laurel_up_all)
    laurel_up_grad = product_tn(laurel_out_low, laurel_mid)
    laurel_mid_low = laurel_mid_grad.astype(low)
    laurel_down_grad = product_tn(normed_low, laurel_mid_low)
    small_total = jnp.concatenate(
        [laurel_down_grad, laurel_up_grad, layer_gate_grad, layer_proj_grad], axis=1
    ).astype(low)
    small_total = small_total.reshape(row_total, col_total, small_rows, small_width)
    small_total = jnp.transpose(small_total, (1, 0, 2, 3)).reshape(-1, small_width)
    small_summed = lax.psum_scatter(small_total, "col", scatter_dimension=0, tiled=True)
    small_grad = scatter_rows(small_summed, row_total)

    normed_grad = (
        normed_grad
        + product_t(laurel_mid_low, laurel_down_all)
        + product_t(query_rel, query_all)
    )
    key_grad, key_gain_grad = key_pull(pair_sum[0].reshape(rows, KV_HEADS, HEAD))
    (value_grad,) = value_pull(pair_sum[1].reshape(rows, KV_HEADS, HEAD))
    kv_grad = jnp.concatenate(
        [
            key_grad.astype(low).reshape(rows, col_total, kv_width),
            value_grad.astype(low).reshape(rows, col_total, kv_width),
        ],
        axis=2,
    ).reshape(rows, col_total * 2 * kv_width)
    kv_rel = xor_blocks(kv_grad, me_col, col_total)
    kv_total = product_tn(normed_pair, pair_columns(kv_rel, col_total))
    kv_weight_grad = scatter_cols(kv_total.astype(low), row_total, pairs)
    normed_grad = normed_grad + product_t(kv_rel, kv_all)
    input_part, input_gain_grad = input_pull(normed_grad)
    input_total = xor_blocks((inputs_grad + input_part).astype(low), me_row, row_total)

    wide_gains = [
        input_gain_grad,
        attention_gain_grad,
        laurel_gain_grad,
        pre_gain_grad,
        post_gain_grad,
        final_gain_grad,
    ]
    gain_parts = [
        xor_blocks(one, me_row, row_total).reshape(row_total, col_total, small_rows)
        for one in wide_gains
    ] + [
        one.reshape(row_total, col_total, head_part) for one in (query_gain_grad, key_gain_grad)
    ]
    gain_sums = jnp.transpose(jnp.concatenate(gain_parts, axis=2), (1, 0, 2))
    gain_sums = gain_sums.reshape(col_total, row_total * gain_total)
    gain_sums = jnp.sum(lax.all_to_all(gain_sums, "col", 0, 0, tiled=True), axis=0)
    gain_sums = gain_sums.reshape(row_total, gain_total)
    gain_sums = jnp.sum(lax.all_to_all(gain_sums, "row", 0, 0, tiled=True), axis=0)
    gain_out = [gain_sums[i * small_rows : (i + 1) * small_rows] for i in range(6)]
    head_out = gain_sums[6 * small_rows :]
    return (
        xor_blocks(output.astype(low), me_row, row_total),
        input_total,
        embed_grad.astype(low),
        query_weight_grad,
        kv_weight_grad[:, :kv_width],
        kv_weight_grad[:, kv_width:],
        out_weight_grad,
        feed_weight_grad[:, :feed_width],
        feed_weight_grad[:, feed_width:],
        down_weight_grad,
        small_grad[:, :rank],
        small_grad[:, rank : 2 * rank],
        small_grad[:, 2 * rank : 2 * rank + embed],
        small_grad[:, 2 * rank + embed :],
        gain_out[0],
        head_out[:head_part],
        head_out[head_part:],
        gain_out[1],
        gain_out[2],
        gain_out[3],
        gain_out[4],
        gain_out[5],
    )


def solution(mesh):
    in_specs = (
        P(("row", "col"), None),
        P(("row", "col"), None),
        P(("row", "col"), None),
        P("row", None),
        P("row", "col"),
        P("row", "col"),
        P("row", "col"),
        P("row", "col"),
        P("row", "col"),
        P("row", "col"),
        P("row", "col"),
        P(("row", "col"), None),
        P(("row", "col"), None),
        P(("row", "col"), None),
        P(("row", "col"), None),
        P(("row", "col")),
        P(("row", "col")),
        P(("row", "col")),
        P(("row", "col")),
        P(("row", "col")),
        P(("row", "col")),
        P(("row", "col")),
        P(("row", "col")),
    )
    out_specs = (
        P(("row", "col"), None),
        P(("row", "col"), None),
        P(("row", "col"), None),
        P("row", "col"),
        P("row", "col"),
        P("row", "col"),
        P("row", "col"),
        P("row", "col"),
        P("row", "col"),
        P("row", "col"),
        P(("row", "col"), None),
        P(("row", "col"), None),
        P(("row", "col"), None),
        P(("row", "col"), None),
        P(("row", "col")),
        P(("row", "col")),
        P(("row", "col")),
        P(("row", "col")),
        P(("row", "col")),
        P(("row", "col")),
        P(("row", "col")),
        P(("row", "col")),
    )
    return jax.shard_map(local, mesh=mesh, in_specs=in_specs, out_specs=out_specs, check_vma=False)
```

```python
from functools import partial
import math

import jax
import jax.numpy as jnp
from jax import lax
from jax.experimental import pallas as pl
from jax.experimental.pallas import tpu as pltpu
from jax.sharding import PartitionSpec as P


HEADS = 8
KV_HEADS = 2
HEAD = 256
BLOCK = 256
ROW = "row"
COL = "col"


NORM_EPS = 1e-06
ROOT_HALF = 0.7071067811865476
ROPE_THETA = 1000000.0


def rms_scale(values, scale_gain):
    return (
        values
        * lax.rsqrt(jnp.mean(values * values, axis=-1, keepdims=True) + NORM_EPS)
        * scale_gain
    )


def angles(position):
    half_width = HEAD // 2
    steps_up = jnp.arange(half_width, dtype=jnp.float32)
    frequency = jnp.exp(steps_up * (-2.0 * math.log(ROPE_THETA) / HEAD))
    angle_grid = position.astype(jnp.float32)[:, None] * frequency[None, :]
    return (jnp.cos(angle_grid), jnp.sin(angle_grid))


def turn(values, cosine, sine_part):
    half_width = HEAD // 2
    first_half = values[:, :half_width]
    second_half = values[:, half_width:]
    return jnp.concatenate(
        [
            first_half * cosine - second_half * sine_part,
            second_half * cosine + first_half * sine_part,
        ],
        axis=1,
    )


def inverse_rms(values):
    return lax.rsqrt(jnp.mean(values * values, axis=1, keepdims=True) + NORM_EPS)


def norm_back(values, inverse, grad):
    return inverse * (
        grad - values * (inverse * inverse * jnp.mean(grad * values, axis=1, keepdims=True))
    )


def query_body(scale, query_ref, gain_ref, cosine_ref, sine_ref, out_ref):
    for head in range(query_ref.shape[1] // HEAD):
        span = slice(head * HEAD, (head + 1) * HEAD)
        values = query_ref[:, span].astype(jnp.float32)
        normed = values * inverse_rms(values) * gain_ref[...]
        turned = turn(normed, cosine_ref[...], sine_ref[...]).astype(jnp.bfloat16)
        out_ref[:, span] = turned * jnp.bfloat16(scale)


def query_back_body(query_ref, grad_ref, gain_ref, cosine_ref, sine_ref, out_ref, gain_grad_ref):
    total = jnp.zeros((1, HEAD), jnp.float32)
    for head in range(query_ref.shape[1] // HEAD):
        span = slice(head * HEAD, (head + 1) * HEAD)
        values = query_ref[:, span].astype(jnp.float32)
        inverse = inverse_rms(values)
        grad = turn(grad_ref[:, span], cosine_ref[...], -sine_ref[...])
        total = total + jnp.sum(grad * values * inverse, axis=0, keepdims=True)
        out_ref[:, span] = norm_back(values, inverse, grad * gain_ref[...]).astype(jnp.bfloat16)
    gain_grad_ref[...] = total


def head_of(columns, head, kind, count):
    width = columns.shape[1] // count // 2
    per_head = HEAD // width
    parts = [
        columns[:, (2 * c + kind) * width : (2 * c + kind + 1) * width]
        for c in range(head * per_head, (head + 1) * per_head)
    ]
    return jnp.concatenate(parts, axis=1)


def pair_body(count, columns_ref, gain_ref, cosine_ref, sine_ref, out_ref):
    columns = columns_ref[...].astype(jnp.float32)
    for head in range(KV_HEADS):
        span = slice(head * HEAD, (head + 1) * HEAD)
        keys = head_of(columns, head, 0, count)
        normed = keys * inverse_rms(keys) * gain_ref[...]
        out_ref[0, :, span] = turn(normed, cosine_ref[...], sine_ref[...]).astype(jnp.bfloat16)
        values = head_of(columns, head, 1, count)
        out_ref[1, :, span] = (values * inverse_rms(values)).astype(jnp.bfloat16)


def pair_back_body(
    count, columns_ref, grad_ref, gain_ref, cosine_ref, sine_ref, out_ref, gain_grad_ref
):
    columns = columns_ref[...].astype(jnp.float32)
    width = columns.shape[1] // count // 2
    total = jnp.zeros((1, HEAD), jnp.float32)
    pieces = []
    for head in range(KV_HEADS):
        span = slice(head * HEAD, (head + 1) * HEAD)
        keys = head_of(columns, head, 0, count)
        inverse = inverse_rms(keys)
        grad = grad_ref[0, :, span].astype(jnp.float32)
        grad = turn(grad, cosine_ref[...], -sine_ref[...])
        total = total + jnp.sum(grad * keys * inverse, axis=0, keepdims=True)
        key_grad = norm_back(keys, inverse, grad * gain_ref[...])
        values = head_of(columns, head, 1, count)
        value_grad = norm_back(
            values, inverse_rms(values), grad_ref[1, :, span].astype(jnp.float32)
        )
        for c in range(HEAD // width):
            pieces.append(key_grad[:, c * width : (c + 1) * width])
            pieces.append(value_grad[:, c * width : (c + 1) * width])
    out_ref[...] = jnp.concatenate(pieces, axis=1).astype(jnp.bfloat16)
    gain_grad_ref[...] = total


def small_call(body, shapes, *operands):
    size = 4 * sum(one.size for one in operands)
    return pl.pallas_call(
        body,
        out_shape=shapes,
        cost_estimate=pl.CostEstimate(flops=4 * size, transcendentals=0, bytes_accessed=size),
    )(*operands)


def placement_info(lengths, tokens_at):
    finish = jnp.cumsum(lengths)
    begins = finish - lengths
    segment = jnp.sum((tokens_at[:, None] >= finish[None, :]).astype(jnp.int32), axis=1)
    chosen = segment[:, None] == jnp.arange(lengths.shape[0], dtype=jnp.int32)[None, :]
    begin = jnp.sum(jnp.where(chosen, begins[None, :], 0), axis=1)
    end = jnp.sum(jnp.where(chosen, finish[None, :], 0), axis=1)
    position = tokens_at - begin
    reach = jnp.minimum(end, begin + (position // BLOCK + 1) * BLOCK)
    return (position, begin, reach)


def geglu(gate_in, up_in):
    return jax.nn.gelu(gate_in, approximate=True) * up_in


def residual_mix(inputs, attention_out, normed, laurel_out, attention_gain, laurel_gain, pre_gain):
    mixed = (
        inputs
        + rms_scale(attention_out, attention_gain)
        + normed
        + rms_scale(laurel_out, laurel_gain)
    ) * ROOT_HALF
    return (mixed, rms_scale(mixed, pre_gain))


def feed_mix(mixed, down_out, post_gain):
    return mixed + rms_scale(down_out, post_gain)


def final_mix(after_feed, per_out, final_gain):
    return after_feed + rms_scale(per_out, final_gain)


def product(left, right):
    return jnp.dot(left, right, preferred_element_type=jnp.float32)


def product_t(left, right):
    return lax.dot_general(
        left, right, (((1,), (1,)), ((), ())), preferred_element_type=jnp.float32
    )


def product_tn(left, right):
    return lax.dot_general(
        left, right, (((0,), (0,)), ((), ())), preferred_element_type=jnp.float32
    )


def hop(values, axis, mask):
    size = lax.axis_size(axis)
    return lax.ppermute(values, axis, [(i, i ^ mask) for i in range(size)])


def split_hop(values, even_mask, odd_mask):
    size = lax.axis_size(ROW) * lax.axis_size(COL)
    pairs = [(i, i ^ (odd_mask if i % 2 else even_mask)) for i in range(size)]
    return lax.ppermute(values, (ROW, COL), pairs)


def after(values, *others):
    return lax.optimization_barrier((values,) + others)[0]


def xor_blocks(values, me, count):
    width = values.shape[-1] // count
    blocks = [values[..., i * width : (i + 1) * width] for i in range(count)]
    bit = 1
    while bit < count:
        flip = (me & bit) != 0
        blocks = [jnp.where(flip, blocks[i ^ bit], blocks[i]) for i in range(count)]
        bit *= 2
    return jnp.concatenate(blocks, axis=-1)


def unit_of(axis):
    return lax.axis_size(COL) if axis == ROW else 2


def direct_gather(piece, axis, count):
    unit = 1 if axis == ROW else 2
    return [piece] + [hop(piece, axis, j * unit) for j in range(1, count)]


def xor_gather(piece, axis, count, middle=None):
    unit = 1 if axis == ROW else 2
    if count == 4:
        near = hop(piece, axis, unit)
        far = hop(piece, axis, 2 * unit)
        odd = lax.axis_index(COL) % 2 == 1
        flat = unit_of(axis)
        chosen_far, chosen_near = far, near
        if middle is not None:
            chosen_far, chosen_near = after(far, middle), after(near, middle)
        across = split_hop(jnp.where(odd, chosen_far, chosen_near), 2 * flat, flat)
        return [piece, near, far, across]
    pieces = [piece]
    bit = 1
    while bit < count:
        pieces = pieces + [hop(one, axis, bit * unit) for one in pieces]
        bit *= 2
    return pieces


def add_low(left, right):
    return (left.astype(jnp.float32) + right.astype(jnp.float32)).astype(jnp.bfloat16)


def xor_scatter(parts, axis, late=None, last=None, marks=None):
    count = parts.shape[0]
    unit = 1 if axis == ROW else 2
    if marks is not None and count != 4:
        marks.append(parts[0])
    if count == 4:
        odd = lax.axis_index(COL) % 2 == 1
        flat = unit_of(axis)
        across = split_hop(parts[3], 2 * flat, flat)
        early = split_hop(jnp.where(odd, parts[1], parts[2]), 2 * flat, flat)
        if late is not None:
            across = after(across, late)
        rest = add_low(jnp.where(odd, parts[2], parts[1]), across)
        if marks is not None:
            marks.append(rest)
        rest = split_hop(rest, flat, 2 * flat)
        if last is not None:
            rest = after(rest, last)
            early = after(early, last)
        return parts[0].astype(jnp.float32) + early.astype(jnp.float32) + rest.astype(jnp.float32)
    parts = [parts[j] for j in range(count)]
    bit = count // 2
    while bit > 0:
        parts = [add_low(parts[j], hop(parts[j + bit], axis, bit * unit)) for j in range(bit)]
        bit //= 2
    return parts[0].astype(jnp.float32)


def scatter_rows(total, row_total, late=None, last=None, marks=None):
    parts = total.reshape(row_total, -1, total.shape[1])
    return xor_scatter(parts, ROW, late, last, marks)


def scatter_cols(total, row_total, pairs, late=None, last=None, marks=None):
    mine = scatter_rows(total, row_total, late, last, marks).astype(jnp.bfloat16)
    width = mine.shape[1] // pairs
    parts = jnp.stack([mine[:, z * width : (z + 1) * width] for z in range(pairs)])
    return xor_scatter(parts, COL, None, None, marks)


def deal_rows_body(pairs, me_ref, block_ref, keep_ref, give_ref):
    for z in range(pairs):
        keep_ref[z] = block_ref[lax.bitwise_xor(me_ref[0], 2 * z)]
        give_ref[z] = block_ref[lax.bitwise_xor(me_ref[0], 2 * z + 1)]


def scatter_small(me, total, row_total, col_total):
    pairs = col_total // 2
    width = total.shape[1]
    blocks = total.reshape(row_total, col_total, -1, width)
    height = blocks.shape[2]
    half = jax.ShapeDtypeStruct((row_total, pairs, height, width), total.dtype)
    out_block = pl.BlockSpec((None, pairs, height, width), lambda r, s: (r, 0, 0, 0))
    keep, give = pl.pallas_call(
        partial(deal_rows_body, pairs),
        out_shape=(half, half),
        grid_spec=pltpu.PrefetchScalarGridSpec(
            num_scalar_prefetch=1,
            grid=(row_total,),
            in_specs=[
                pl.BlockSpec((None, col_total, height, width), lambda r, s: (r, 0, 0, 0))
            ],
            out_specs=(out_block, out_block),
        ),
        cost_estimate=pl.CostEstimate(
            flops=0, transcendentals=0, bytes_accessed=4 * total.size
        ),
    )(me, blocks)
    both = add_low(keep, hop(give, COL, 1)).reshape(row_total, pairs * height, width)
    mine = xor_scatter(both, ROW).astype(jnp.bfloat16)
    return xor_scatter(mine.reshape(pairs, height, width), COL)


def stack_body(*refs):
    for i, ref in enumerate(refs[:-1]):
        refs[-1][i] = ref[...]


def stack_pieces(pieces):
    shape = (len(pieces),) + pieces[0].shape
    return pl.pallas_call(
        stack_body,
        out_shape=jax.ShapeDtypeStruct(shape, pieces[0].dtype),
        cost_estimate=pl.CostEstimate(
            flops=0, transcendentals=0, bytes_accessed=4 * math.prod(shape)
        ),
    )(*pieces)


def gather_weight(shard, pairs, row_total, direct, first=None, second=None, middle=None):
    along = direct_gather(shard if first is None else after(shard, first), COL, pairs)
    stacked = stack_pieces(along)
    if second is not None:
        stacked = after(stacked, second)
    if direct:
        mine = direct_gather(stacked, ROW, row_total)
    else:
        mine = xor_gather(stacked, ROW, row_total, middle)
    return (mine, [hop(one, COL, 1) for one in mine]), along[-1], mine[-1]


def place_body(pairs, me_ref, own_ref, other_ref, out_ref):
    for z in range(pairs):
        out_ref[lax.bitwise_xor(me_ref[0], 2 * z)] = own_ref[z]
        out_ref[lax.bitwise_xor(me_ref[0], 2 * z + 1)] = other_ref[z]


def over_col(me, own, pairs):
    stacked = stack_pieces(direct_gather(own, COL, pairs))
    other = hop(stacked, COL, 1)
    vmem = pl.BlockSpec(memory_space=pltpu.VMEM)
    return pl.pallas_call(
        partial(place_body, pairs),
        out_shape=jax.ShapeDtypeStruct((2 * pairs,) + own.shape, own.dtype),
        in_specs=[pl.BlockSpec(memory_space=pltpu.SMEM), vmem, vmem],
    )(me, stacked, other)


def block_of(ref, index, width):
    if len(ref.shape) == 3:
        return ref.at[index]
    return ref.at[:, pl.ds(pl.multiple_of(index * width, 128), width)]


def blocked(values, count):
    rows = values.shape[0]
    width = values.shape[1] // count
    if width % 128 == 0:
        return values
    return jnp.transpose(values.reshape(rows, count, width), (1, 0, 2))


def project_body(me_ref, left_ref, *refs):
    pieces, out_ref = refs[:-1], refs[-1]
    row_total = len(pieces) // 2
    pairs, height, width = pieces[0].shape
    for z in range(pairs):
        for core in range(2):
            total = None
            for r in range(row_total):
                part = jnp.dot(
                    left_ref[:, r * height : (r + 1) * height],
                    pieces[core * row_total + r][z],
                    preferred_element_type=jnp.float32,
                )
                total = part if total is None else total + part
            out = block_of(out_ref, lax.bitwise_xor(me_ref[0], 2 * z + core), width)
            out[...] = total.astype(out_ref.dtype)


def contract_body(me_ref, left_ref, *refs):
    pieces, out_ref = refs[:-1], refs[-1]
    row_total = len(pieces) // 2
    pairs, height, width = pieces[0].shape
    for r in range(row_total):
        total = None
        for z in range(pairs):
            for core in range(2):
                block = block_of(left_ref, lax.bitwise_xor(me_ref[0], 2 * z + core), width)
                part = lax.dot_general(
                    block[...],
                    pieces[core * row_total + r][z],
                    (((1,), (1,)), ((), ())),
                    preferred_element_type=jnp.float32,
                )
                total = part if total is None else total + part
        out_ref[:, r * height : (r + 1) * height] = total


def whole_call(body, shape, dtype, flops, me, left, pieces):
    mine, other = pieces
    operands = [left, *mine, *other]
    size = sum(one.size for one in operands) * 2
    vmem = pl.BlockSpec(memory_space=pltpu.VMEM)
    return pl.pallas_call(
        body,
        out_shape=jax.ShapeDtypeStruct(shape, dtype),
        in_specs=[pl.BlockSpec(memory_space=pltpu.SMEM)] + [vmem] * len(operands),
        out_specs=vmem,
        cost_estimate=pl.CostEstimate(flops=flops, transcendentals=0, bytes_accessed=size),
    )(me, *operands)


def project(me, left, pieces):
    pairs, _, width = pieces[0][0].shape
    rows = left.shape[0]
    shape = (rows, 2 * pairs * width) if width % 128 == 0 else (2 * pairs, rows, width)
    flops = 4 * rows * left.shape[1] * pairs * width
    out = whole_call(project_body, shape, jnp.bfloat16, flops, me, left, pieces)
    if len(shape) == 3:
        out = jnp.transpose(out, (1, 0, 2)).reshape(rows, 2 * pairs * width)
    return out


def contract(me, left, pieces):
    pairs, height, _ = pieces[0][0].shape
    shape = (left.shape[0], len(pieces[0]) * height)
    flops = 2 * left.size * shape[1]
    left = blocked(left, 2 * pairs)
    return whole_call(contract_body, shape, jnp.float32, flops, me, left, pieces)


def deal_body(pairs, me_ref, columns_ref, keep_ref, give_ref):
    width = keep_ref.shape[1] // pairs
    for z in range(pairs):
        span = slice(z * width, (z + 1) * width)
        for core, out_ref in enumerate((keep_ref, give_ref)):
            index = lax.bitwise_xor(me_ref[0], 2 * z + core)
            out_ref[:, span] = block_of(columns_ref, index, width)[...]


def pair_columns(me, columns, count):
    rows, width = columns.shape
    half = jax.ShapeDtypeStruct((rows, width // 2), columns.dtype)
    values = blocked(columns, count)
    keep, give = pl.pallas_call(
        partial(deal_body, count // 2),
        out_shape=(half, half),
        in_specs=[
            pl.BlockSpec(memory_space=pltpu.SMEM),
            pl.BlockSpec(memory_space=pltpu.VMEM),
        ],
        cost_estimate=pl.CostEstimate(
            flops=0, transcendentals=0, bytes_accessed=4 * rows * width
        ),
    )(me, values)
    return jnp.concatenate([keep, hop(give, COL, 1)], axis=0)


def pair_rows(own):
    return jnp.concatenate([own, hop(own, COL, 1)], axis=0)


def attend_body(span_ref, window_ref, query_ref, key_ref, value_ref, out_ref, inverse_ref, sums, weights):
    rows = query_ref.shape[0]
    low_edge = window_ref[:, 0:1]
    high_edge = window_ref[:, 1:2]
    query = query_ref[...]
    sums[...] = jnp.zeros_like(sums)
    weights[...] = jnp.zeros_like(weights)

    def one_tile(tile, carry):
        scores = lax.dot_general(
            query, key_ref[tile], (((1,), (1,)), ((), ())), preferred_element_type=jnp.float32
        )
        place = tile * rows + lax.broadcasted_iota(jnp.int32, scores.shape, 1)
        exps = jnp.where((place >= low_edge) & (place < high_edge), jnp.exp(scores), 0.0)
        part = exps[:, :128]
        for start in range(128, rows, 128):
            part = part + exps[:, start : start + 128]
        weights[...] += part
        sums[...] += jnp.dot(
            exps.astype(jnp.bfloat16), value_ref[tile], preferred_element_type=jnp.float32
        )
        return carry

    lax.fori_loop(span_ref[0], span_ref[1], one_tile, 0)
    inverse = 1.0 / jnp.sum(weights[...], axis=1, keepdims=True)
    out_ref[...] = (sums[...] * inverse).astype(jnp.bfloat16)
    inverse_ref[...] = jnp.broadcast_to(inverse, inverse_ref.shape)


def attend(span, window, query, gathered):
    rows, width = query.shape
    tiles = gathered.shape[0]
    groups = HEADS // KV_HEADS
    half = pl.BlockSpec((rows, HEAD), lambda h, s: (0, h))
    flops = 4 * rows * rows * tiles * width
    return pl.pallas_call(
        attend_body,
        out_shape=(
            jax.ShapeDtypeStruct((rows, width), jnp.bfloat16),
            jax.ShapeDtypeStruct((rows, HEADS * 128), jnp.float32),
        ),
        grid_spec=pltpu.PrefetchScalarGridSpec(
            num_scalar_prefetch=1,
            grid=(HEADS,),
            in_specs=[
                pl.BlockSpec((rows, 2), lambda h, s: (0, 0)),
                half,
                pl.BlockSpec((tiles, None, rows, HEAD), lambda h, s: (0, 0, 0, h // groups)),
                pl.BlockSpec((tiles, None, rows, HEAD), lambda h, s: (0, 1, 0, h // groups)),
            ],
            out_specs=(half, pl.BlockSpec((rows, 128), lambda h, s: (0, h))),
            scratch_shapes=[
                pltpu.VMEM((rows, HEAD), jnp.float32),
                pltpu.VMEM((rows, 128), jnp.float32),
            ],
        ),
        cost_estimate=pl.CostEstimate(
            flops=flops, transcendentals=rows * rows * tiles * HEADS, bytes_accessed=8 * rows * width
        ),
    )(span, window, query, gathered, gathered)


def attend_back_body(
    span_ref, window_ref, query_ref, key_ref, value_ref, grad_ref, out_ref, inverse_ref,
    query_grad_ref, pair_grad_ref, query_sum, key_sum, value_sum,
):
    rows = query_ref.shape[0]
    groups = HEADS // KV_HEADS
    head = pl.program_id(0)
    low_edge = window_ref[0:1, :]
    high_edge = window_ref[1:2, :]
    query = query_ref[...]
    grad_wide = grad_ref[...].astype(jnp.float32)
    inverse = inverse_ref[:, 0:1]
    delta = jnp.sum(grad_wide * out_ref[...].astype(jnp.float32), axis=1, keepdims=True) * inverse
    delta_row = jnp.transpose(jnp.broadcast_to(delta, (rows, 128)))[0:1, :]
    grad_scaled = (grad_wide * inverse).astype(jnp.bfloat16)
    query_sum[...] = jnp.zeros_like(query_sum)

    @pl.when(lax.rem(head, groups) == 0)
    def _():
        key_sum[...] = jnp.zeros_like(key_sum)
        value_sum[...] = jnp.zeros_like(value_sum)

    def one_tile(tile, carry):
        keys = key_ref[tile]
        contract_last = (((1,), (1,)), ((), ()))
        scores = lax.dot_general(keys, query, contract_last, preferred_element_type=jnp.float32)
        place = tile * rows + lax.broadcasted_iota(jnp.int32, scores.shape, 0)
        exps = jnp.where((place >= low_edge) & (place < high_edge), jnp.exp(scores), 0.0)
        prob_grad = lax.dot_general(
            value_ref[tile], grad_scaled, contract_last, preferred_element_type=jnp.float32
        )
        score_grad = (exps * (prob_grad - delta_row)).astype(jnp.bfloat16)
        key_sum[tile] += jnp.dot(score_grad, query, preferred_element_type=jnp.float32)
        value_sum[tile] += jnp.dot(
            exps.astype(jnp.bfloat16), grad_scaled, preferred_element_type=jnp.float32
        )
        query_sum[...] += lax.dot_general(
            score_grad, keys, (((0,), (0,)), ((), ())), preferred_element_type=jnp.float32
        )
        return carry

    lax.fori_loop(span_ref[0], span_ref[1], one_tile, 0)
    query_grad_ref[...] = query_sum[...] * (1.0 / math.sqrt(HEAD))

    @pl.when(lax.rem(head, groups) == groups - 1)
    def _():
        pair_grad_ref[:, 0] = key_sum[...].astype(jnp.bfloat16)
        pair_grad_ref[:, 1] = value_sum[...].astype(jnp.bfloat16)


def attend_back(span, window, query, gathered, grad, out, inverse):
    rows, width = query.shape
    tiles = gathered.shape[0]
    groups = HEADS // KV_HEADS
    half = pl.BlockSpec((rows, HEAD), lambda h, s: (0, h))
    return pl.pallas_call(
        attend_back_body,
        out_shape=(
            jax.ShapeDtypeStruct((rows, width), jnp.float32),
            jax.ShapeDtypeStruct(gathered.shape, jnp.bfloat16),
        ),
        grid_spec=pltpu.PrefetchScalarGridSpec(
            num_scalar_prefetch=1,
            grid=(HEADS,),
            in_specs=[
                pl.BlockSpec((2, rows), lambda h, s: (0, 0)),
                half,
                pl.BlockSpec((tiles, None, rows, HEAD), lambda h, s: (0, 0, 0, h // groups)),
                pl.BlockSpec((tiles, None, rows, HEAD), lambda h, s: (0, 1, 0, h // groups)),
                half,
                half,
                pl.BlockSpec((rows, 128), lambda h, s: (0, h)),
            ],
            out_specs=(
                half,
                pl.BlockSpec((tiles, 2, rows, HEAD), lambda h, s: (0, 0, 0, h // groups)),
            ),
            scratch_shapes=[
                pltpu.VMEM((rows, HEAD), jnp.float32),
                pltpu.VMEM((tiles, rows, HEAD), jnp.float32),
                pltpu.VMEM((tiles, rows, HEAD), jnp.float32),
            ],
        ),
        cost_estimate=pl.CostEstimate(
            flops=10 * rows * rows * tiles * width,
            transcendentals=rows * rows * tiles * HEADS,
            bytes_accessed=16 * rows * width,
        ),
    )(span, window, query, gathered, gathered, grad, out, inverse)


def local(
    layer_input,
    per_layer_input,
    out_cotangent,
    seq_lengths,
    query_weight,
    key_weight,
    value_weight,
    out_weight,
    gate_weight,
    up_weight,
    down_weight,
    laurel_down,
    laurel_up,
    per_layer_gate,
    per_layer_projection,
    input_gain,
    query_gain,
    key_gain,
    attention_gain,
    laurel_gain,
    pre_feed_gain,
    post_feed_gain,
    per_layer_gain,
):
    rows, width = layer_input.shape
    row_total = lax.axis_size(ROW)
    col_total = lax.axis_size(COL)
    pairs = col_total // 2
    me_row = lax.axis_index(ROW)
    me_col = lax.axis_index(COL)
    rank = laurel_down.shape[1]
    embed = per_layer_gate.shape[1]
    kv_width = key_weight.shape[1]
    feed_width = gate_weight.shape[1]
    low = jnp.bfloat16
    wide = jnp.float32

    me = me_col.astype(jnp.int32).reshape(1)
    small_rows = laurel_down.shape[0]
    head_part = query_gain.shape[0]

    gains_own = jnp.concatenate(
        [
            input_gain,
            attention_gain,
            laurel_gain,
            pre_feed_gain,
            post_feed_gain,
            per_layer_gain,
            query_gain,
            key_gain,
        ]
    )
    gain_total = gains_own.shape[0]
    laurel_own = jnp.concatenate([laurel_down, laurel_up], axis=1)
    line = laurel_own.shape[1]
    gain_lines = -(-gain_total // line)
    gains_block = jnp.pad(gains_own, (0, gain_lines * line - gain_total)).reshape(gain_lines, line)
    first_own = jnp.concatenate(
        [laurel_own, jnp.pad(gains_block, ((0, 16 - gain_lines), (0, 0)))], axis=0
    )

    spread = jnp.broadcast_to(first_own[None], (col_total,) + first_own.shape)
    first_group = lax.all_to_all(spread, COL, 0, 0, tiled=True)
    first_all = jnp.stack(direct_gather(first_group, ROW, row_total))
    laurel_all = first_all[:, :, :small_rows].reshape(-1, line)
    laurel_down_all = laurel_all[:, :rank]
    laurel_up_all = laurel_all[:, rank:]
    gain_rows = first_all[:, :, small_rows : small_rows + gain_lines].astype(wide)
    gain_rows = gain_rows.reshape(row_total, col_total, gain_lines * line)
    gains = gain_rows[:, :, : 6 * small_rows].reshape(row_total, col_total, 6, small_rows)
    gains = jnp.transpose(gains, (2, 0, 1, 3)).reshape(6, width)
    gain_list = [gains[i] for i in range(6)]
    head_gains = []
    for i in range(2):
        start = 6 * small_rows + i * head_part
        rel = gain_rows[:, :, start : start + head_part].reshape(-1)
        head_gains.append(xor_blocks(rel, me_row, row_total))

    kv_pieces, kv_first, kv_last = gather_weight(
        jnp.concatenate([key_weight, value_weight], axis=1), pairs, row_total, True
    )
    query_pieces, _, query_last = gather_weight(
        query_weight, pairs, row_total, False, kv_first, kv_last
    )
    tokens_at = me_col * rows + jnp.arange(rows, dtype=jnp.int32)
    position, begin, reach = placement_info(seq_lengths[0], tokens_at)
    window = jnp.stack([begin, reach])
    span = jnp.stack([jnp.min(begin) // rows, (jnp.max(reach) + rows - 1) // rows])
    inputs = xor_blocks(layer_input, me_row, row_total).astype(wide)
    cotangent = xor_blocks(out_cotangent, me_row, row_total).astype(wide)
    normed, input_pull = jax.vjp(rms_scale, inputs, gain_list[0])
    normed_low = normed.astype(low)
    cosine, sine_part = angles(position)
    query_gain_row = head_gains[0].reshape(1, HEAD)
    key_gain_row = head_gains[1].reshape(1, HEAD)
    kv_own = project(me, normed_low, kv_pieces)
    pair_own = small_call(
        partial(pair_body, col_total),
        jax.ShapeDtypeStruct((2, rows, KV_HEADS * HEAD), low),
        kv_own,
        key_gain_row,
        cosine,
        sine_part,
    )
    pair_all = lax.all_gather(pair_own, COL, axis=0, tiled=True)
    pair_all = pair_all.reshape(col_total, 2, rows, KV_HEADS * HEAD)
    query_own = project(me, normed_low, query_pieces)
    query_scaled = small_call(
        partial(query_body, 1.0 / math.sqrt(HEAD)),
        jax.ShapeDtypeStruct((rows, HEADS * HEAD), low),
        query_own,
        query_gain_row,
        cosine,
        sine_part,
    )
    out_pieces, _, out_last = gather_weight(
        out_weight, pairs, row_total, False, kv_first, query_last, query_own
    )
    attended, inverse = attend(span, jnp.transpose(window), query_scaled, pair_all)
    attention_out = contract(me, attended, out_pieces)
    laurel_mid = product(normed_low, laurel_down_all).astype(low)
    laurel_out = product_t(laurel_mid, laurel_up_all)
    (mixed, feed_in), mix_pull = jax.vjp(
        residual_mix,
        inputs,
        attention_out,
        normed_low.astype(wide),
        laurel_out,
        gain_list[1],
        gain_list[2],
        gain_list[3],
    )
    feed_low = feed_in.astype(low)
    feed_pieces = xor_gather(
        after(jnp.concatenate([gate_weight, up_weight], axis=1), out_last), ROW, row_total, feed_low
    )
    down_pieces = xor_gather(down_weight, ROW, row_total, feed_pieces[-1])
    layer_own = jnp.concatenate([per_layer_gate, per_layer_projection], axis=1)
    layer_group = over_col(me, after(layer_own, feed_low), pairs)
    layer_pieces = direct_gather(after(layer_group, down_pieces[-1]), ROW, row_total)
    layer_all = jnp.concatenate([one.reshape(-1, 2 * embed) for one in layer_pieces], axis=0)
    layer_gate_all = layer_all[:, :embed]
    layer_proj_all = layer_all[:, embed:]
    feed_all = jnp.concatenate(feed_pieces, axis=0)
    down_all = jnp.concatenate(down_pieces, axis=0)
    halves = 2
    part_rows = rows // halves
    feed_tokens, hidden_pulls, hidden_lows, down_outs = [], [], [], []
    done = None
    for h in range(halves):
        tokens = lax.all_gather(
            feed_low[h * part_rows : (h + 1) * part_rows], COL, axis=0, tiled=True
        )
        tokens = tokens if done is None else after(tokens, done)
        gate_up = product(tokens, feed_all).astype(low)
        hidden, hidden_pull = jax.vjp(
            geglu, gate_up[:, :feed_width].astype(wide), gate_up[:, feed_width:].astype(wide)
        )
        hidden_low = hidden.astype(low)
        done = product_t(hidden_low, down_all).astype(low)
        down_outs.append(lax.psum_scatter(done, COL, scatter_dimension=0, tiled=True))
        feed_tokens.append(tokens)
        hidden_pulls.append(hidden_pull)
        hidden_lows.append(hidden_low)
    down_out = jnp.concatenate(down_outs, axis=0).astype(wide)
    after_feed, feed_pull = jax.vjp(feed_mix, mixed, down_out, gain_list[4])
    after_low = after_feed.astype(low)
    per_pre = product(after_low, layer_gate_all)
    per_hidden, per_pull = jax.vjp(geglu, per_pre, per_layer_input.astype(wide))
    per_low = per_hidden.astype(low)
    per_out = product_t(per_low, layer_proj_all)
    output, final_pull = jax.vjp(final_mix, after_feed, per_out, gain_list[5])
    after_grad, per_out_grad, final_gain_grad = final_pull(cotangent)
    per_out_low = per_out_grad.astype(low)
    per_hidden_grad = product(per_out_low, layer_proj_all)
    layer_proj_grad = product_tn(per_out_low, per_low)
    per_pre_grad, embed_grad = per_pull(per_hidden_grad)
    per_pre_low = per_pre_grad.astype(low)
    after_grad = after_grad + product_t(per_pre_low, layer_gate_all)
    layer_gate_grad = product_tn(after_low, per_pre_low)
    mixed_grad, down_grad, post_gain_grad = feed_pull(after_grad)
    down_low = down_grad.astype(low)
    layer_grad = scatter_small(
        me,
        after(jnp.concatenate([layer_gate_grad, layer_proj_grad], axis=1).astype(low), down_low),
        row_total,
        col_total,
    )
    attended_pair = pair_columns(me, after(attended, down_low), col_total)
    normed_pair = pair_rows(after(normed_low, down_low))
    down_tokens, feed_grads, feed_in_grads = [], [], []
    done = None
    for h in range(halves):
        tokens = lax.all_gather(
            down_low[h * part_rows : (h + 1) * part_rows], COL, axis=0, tiled=True
        )
        if done is None:
            tokens, layer_grad, attended_pair, normed_pair = lax.optimization_barrier(
                (tokens, layer_grad, attended_pair, normed_pair)
            )
        else:
            tokens = after(tokens, done)
        hidden_grad = product(tokens, down_all)
        gate_grad, up_grad = hidden_pulls[h](hidden_grad)
        feed_grad_low = jnp.concatenate([gate_grad.astype(low), up_grad.astype(low)], axis=1)
        done = product_t(feed_grad_low, feed_all).astype(low)
        feed_in_grads.append(lax.psum_scatter(done, COL, scatter_dimension=0, tiled=True))
        down_tokens.append(tokens)
        feed_grads.append(feed_grad_low)
    feed_in_grad = jnp.concatenate(feed_in_grads, axis=0).astype(wide)
    down_total = sum(
        product_tn(after(down_tokens[h], done), hidden_lows[h]) for h in range(halves)
    ).astype(low)
    feed_total = sum(
        product_tn(after(feed_tokens[h], down_total), feed_grads[h]) for h in range(halves)
    ).astype(low)
    (
        inputs_grad,
        attention_grad,
        normed_grad,
        laurel_out_grad,
        attention_gain_grad,
        laurel_gain_grad,
        pre_gain_grad,
    ) = mix_pull((mixed_grad, feed_in_grad))
    attention_low = attention_grad.astype(low)
    attended_grad = project(me, attention_low, out_pieces)
    query_rot_grad, pair_parts = attend_back(
        span, window, query_scaled, pair_all, attended_grad, attended, inverse
    )
    pair_sum = lax.psum_scatter(
        pair_parts.reshape(2 * col_total, rows, KV_HEADS * HEAD),
        COL,
        scatter_dimension=0,
        tiled=True,
    )
    attention_pair = pair_rows(attention_low)
    out_total = product_tn(after(attention_pair, pair_parts), attended_pair).astype(low)
    query_rot_grad = after(query_rot_grad, out_total)
    gain_row = jax.ShapeDtypeStruct((1, HEAD), wide)
    query_low, query_gain_grad = small_call(
        query_back_body,
        (jax.ShapeDtypeStruct((rows, HEADS * HEAD), low), gain_row),
        query_own,
        query_rot_grad,
        query_gain_row,
        cosine,
        sine_part,
    )
    query_total = product_tn(
        after(normed_pair, out_total), pair_columns(me, query_low, col_total)
    ).astype(low)
    query_part = contract(me, after(query_low, query_total), query_pieces)

    laurel_out_low = after(laurel_out_grad.astype(low), query_total)
    laurel_mid_grad = product(laurel_out_low, laurel_up_all)
    laurel_up_grad = product_tn(laurel_out_low, laurel_mid)
    laurel_mid_low = laurel_mid_grad.astype(low)
    laurel_down_grad = product_tn(normed_low, laurel_mid_low)
    small_total = jnp.concatenate([laurel_down_grad, laurel_up_grad], axis=1)
    normed_grad = normed_grad + product_t(laurel_mid_low, laurel_down_all) + query_part
    pair_sum = after(pair_sum, normed_grad, small_total)
    kv_grad, key_gain_grad = small_call(
        partial(pair_back_body, col_total),
        (jax.ShapeDtypeStruct(kv_own.shape, low), gain_row),
        kv_own,
        pair_sum,
        key_gain_row,
        cosine,
        sine_part,
    )
    kv_total = product_tn(normed_pair, pair_columns(me, kv_grad, col_total)).astype(low)
    marks = []
    normed_grad = normed_grad + contract(me, after(kv_grad, kv_total), kv_pieces)
    kv_weight_grad = scatter_cols(kv_total, row_total, pairs, normed_grad, None, marks)
    mark = marks[0]
    query_marks = []
    query_weight_grad = scatter_cols(query_total, row_total, pairs, mark, mark, query_marks)
    out_weight_grad = scatter_cols(out_total, row_total, pairs, query_part, mark)
    down_weight_grad = scatter_rows(down_total, row_total, feed_total, query_marks[0])
    feed_weight_grad = scatter_rows(feed_total, row_total, attended_grad, marks[-1])
    input_part, input_gain_grad = input_pull(after(normed_grad, mark))
    input_total = xor_blocks((inputs_grad + input_part).astype(low), me_row, row_total)

    wide_gains = jnp.stack(
        [
            input_gain_grad,
            attention_gain_grad,
            laurel_gain_grad,
            pre_gain_grad,
            post_gain_grad,
            final_gain_grad,
        ]
    ).reshape(6, row_total, col_total, small_rows)
    wide_gains = jnp.transpose(wide_gains, (2, 1, 0, 3)).reshape(col_total, row_total, -1)
    both_gains = jnp.concatenate([query_gain_grad, key_gain_grad], axis=0)
    both_gains = xor_blocks(both_gains, me_row, row_total)
    both_gains = both_gains.reshape(2, row_total, col_total, head_part)
    both_gains = jnp.transpose(both_gains, (2, 1, 0, 3)).reshape(col_total, row_total, -1)
    gain_sums = jnp.concatenate([wide_gains, both_gains], axis=2)
    gain_sums = jnp.pad(gain_sums, ((0, 0), (0, 0), (0, gain_lines * line - gain_total)))
    gain_sums = gain_sums.reshape(col_total, row_total, gain_lines, line)
    laurel_parts = jnp.transpose(
        small_total.reshape(row_total, col_total, small_rows, line), (1, 0, 2, 3)
    )
    sums = jnp.concatenate([laurel_parts, gain_sums], axis=2)
    sums = lax.all_to_all(after(sums, query_marks[0]), COL, 0, 0, tiled=True)
    sums = jnp.sum(after(sums, query_marks[-1]), axis=0)
    sums = sums[0] + sum(hop(sums[j], ROW, j) for j in range(1, row_total))
    laurel_grad = sums[:small_rows]
    gain_sums = sums[small_rows:].reshape(-1)
    gain_out = [gain_sums[i * small_rows : (i + 1) * small_rows] for i in range(6)]
    head_out = gain_sums[6 * small_rows : gain_total]
    return (
        xor_blocks(output.astype(low), me_row, row_total),
        input_total,
        embed_grad.astype(low),
        query_weight_grad,
        kv_weight_grad[:, :kv_width],
        kv_weight_grad[:, kv_width:],
        out_weight_grad,
        feed_weight_grad[:, :feed_width],
        feed_weight_grad[:, feed_width:],
        down_weight_grad,
        laurel_grad[:, :rank],
        laurel_grad[:, rank:],
        layer_grad[:, :embed],
        layer_grad[:, embed:],
        gain_out[0],
        head_out[:head_part],
        head_out[head_part:],
        gain_out[1],
        gain_out[2],
        gain_out[3],
        gain_out[4],
        gain_out[5],
    )


def solution(mesh):
    in_specs = (
        P((ROW, COL), None),
        P((ROW, COL), None),
        P((ROW, COL), None),
        P(ROW, None),
        P(ROW, COL),
        P(ROW, COL),
        P(ROW, COL),
        P(ROW, COL),
        P(ROW, COL),
        P(ROW, COL),
        P(ROW, COL),
        P((ROW, COL), None),
        P((ROW, COL), None),
        P((ROW, COL), None),
        P((ROW, COL), None),
        P((ROW, COL)),
        P((ROW, COL)),
        P((ROW, COL)),
        P((ROW, COL)),
        P((ROW, COL)),
        P((ROW, COL)),
        P((ROW, COL)),
        P((ROW, COL)),
    )
    out_specs = (
        P((ROW, COL), None),
        P((ROW, COL), None),
        P((ROW, COL), None),
        P(ROW, COL),
        P(ROW, COL),
        P(ROW, COL),
        P(ROW, COL),
        P(ROW, COL),
        P(ROW, COL),
        P(ROW, COL),
        P((ROW, COL), None),
        P((ROW, COL), None),
        P((ROW, COL), None),
        P((ROW, COL), None),
        P((ROW, COL)),
        P((ROW, COL)),
        P((ROW, COL)),
        P((ROW, COL)),
        P((ROW, COL)),
        P((ROW, COL)),
        P((ROW, COL)),
        P((ROW, COL)),
    )

    return jax.shard_map(local, mesh=mesh, in_specs=in_specs, out_specs=out_specs, check_vma=False)
```

```python
from functools import partial
import math

import jax
import jax.numpy as jnp
from jax import lax
from jax.experimental import pallas as pl
from jax.experimental.pallas import tpu as pltpu
from jax.sharding import PartitionSpec as P


HEADS = 8
KV_HEADS = 2
HEAD = 256
BLOCK = 256
ROW = "row"
COL = "col"


NORM_EPS = 1e-06
ROOT_HALF = 0.7071067811865476
ROPE_THETA = 1000000.0


def rms_scale(values, scale_gain):
    return (
        values
        * lax.rsqrt(jnp.mean(values * values, axis=-1, keepdims=True) + NORM_EPS)
        * scale_gain
    )


def angles(position):
    half_width = HEAD // 2
    steps_up = jnp.arange(half_width, dtype=jnp.float32)
    frequency = jnp.exp(steps_up * (-2.0 * math.log(ROPE_THETA) / HEAD))
    angle_grid = position.astype(jnp.float32)[:, None] * frequency[None, :]
    return (jnp.cos(angle_grid), jnp.sin(angle_grid))


def turn(values, cosine, sine_part):
    half_width = HEAD // 2
    first_half = values[:, :half_width]
    second_half = values[:, half_width:]
    return jnp.concatenate(
        [
            first_half * cosine - second_half * sine_part,
            second_half * cosine + first_half * sine_part,
        ],
        axis=1,
    )


def inverse_rms(values):
    return lax.rsqrt(jnp.mean(values * values, axis=1, keepdims=True) + NORM_EPS)


def norm_back(values, inverse, grad):
    return inverse * (
        grad - values * (inverse * inverse * jnp.mean(grad * values, axis=1, keepdims=True))
    )


def query_body(scale, query_ref, gain_ref, cosine_ref, sine_ref, out_ref):
    for head in range(query_ref.shape[1] // HEAD):
        span = slice(head * HEAD, (head + 1) * HEAD)
        values = query_ref[:, span].astype(jnp.float32)
        normed = values * inverse_rms(values) * gain_ref[...]
        turned = turn(normed, cosine_ref[...], sine_ref[...]).astype(jnp.bfloat16)
        out_ref[:, span] = turned * jnp.bfloat16(scale)


def query_back_body(query_ref, grad_ref, gain_ref, cosine_ref, sine_ref, out_ref, gain_grad_ref):
    total = jnp.zeros((1, HEAD), jnp.float32)
    for head in range(query_ref.shape[1] // HEAD):
        span = slice(head * HEAD, (head + 1) * HEAD)
        values = query_ref[:, span].astype(jnp.float32)
        inverse = inverse_rms(values)
        grad = turn(grad_ref[:, span], cosine_ref[...], -sine_ref[...])
        total = total + jnp.sum(grad * values * inverse, axis=0, keepdims=True)
        out_ref[:, span] = norm_back(values, inverse, grad * gain_ref[...]).astype(jnp.bfloat16)
    gain_grad_ref[...] = total


def head_of(columns, head, kind, count):
    width = columns.shape[1] // count // 2
    per_head = HEAD // width
    parts = [
        columns[:, (2 * c + kind) * width : (2 * c + kind + 1) * width]
        for c in range(head * per_head, (head + 1) * per_head)
    ]
    return jnp.concatenate(parts, axis=1)


def pair_body(count, columns_ref, gain_ref, cosine_ref, sine_ref, out_ref):
    columns = columns_ref[...].astype(jnp.float32)
    for head in range(KV_HEADS):
        span = slice(head * HEAD, (head + 1) * HEAD)
        keys = head_of(columns, head, 0, count)
        normed = keys * inverse_rms(keys) * gain_ref[...]
        out_ref[0, :, span] = turn(normed, cosine_ref[...], sine_ref[...]).astype(jnp.bfloat16)
        values = head_of(columns, head, 1, count)
        out_ref[1, :, span] = (values * inverse_rms(values)).astype(jnp.bfloat16)


def pair_back_body(
    count, columns_ref, grad_ref, gain_ref, cosine_ref, sine_ref, out_ref, gain_grad_ref
):
    columns = columns_ref[...].astype(jnp.float32)
    width = columns.shape[1] // count // 2
    total = jnp.zeros((1, HEAD), jnp.float32)
    pieces = []
    for head in range(KV_HEADS):
        span = slice(head * HEAD, (head + 1) * HEAD)
        keys = head_of(columns, head, 0, count)
        inverse = inverse_rms(keys)
        grad = grad_ref[0, :, span].astype(jnp.float32)
        grad = turn(grad, cosine_ref[...], -sine_ref[...])
        total = total + jnp.sum(grad * keys * inverse, axis=0, keepdims=True)
        key_grad = norm_back(keys, inverse, grad * gain_ref[...])
        values = head_of(columns, head, 1, count)
        value_grad = norm_back(
            values, inverse_rms(values), grad_ref[1, :, span].astype(jnp.float32)
        )
        for c in range(HEAD // width):
            pieces.append(key_grad[:, c * width : (c + 1) * width])
            pieces.append(value_grad[:, c * width : (c + 1) * width])
    out_ref[...] = jnp.concatenate(pieces, axis=1).astype(jnp.bfloat16)
    gain_grad_ref[...] = total


def small_call(body, shapes, *operands):
    size = 4 * sum(one.size for one in operands)
    return pl.pallas_call(
        body,
        out_shape=shapes,
        cost_estimate=pl.CostEstimate(flops=4 * size, transcendentals=0, bytes_accessed=size),
    )(*operands)


def placement_info(lengths, tokens_at):
    finish = jnp.cumsum(lengths)
    begins = finish - lengths
    segment = jnp.sum((tokens_at[:, None] >= finish[None, :]).astype(jnp.int32), axis=1)
    chosen = segment[:, None] == jnp.arange(lengths.shape[0], dtype=jnp.int32)[None, :]
    begin = jnp.sum(jnp.where(chosen, begins[None, :], 0), axis=1)
    end = jnp.sum(jnp.where(chosen, finish[None, :], 0), axis=1)
    position = tokens_at - begin
    reach = jnp.minimum(end, begin + (position // BLOCK + 1) * BLOCK)
    return (position, begin, reach)


def geglu(gate_in, up_in):
    return jax.nn.gelu(gate_in, approximate=True) * up_in


def residual_mix(inputs, attention_out, normed, laurel_out, attention_gain, laurel_gain, pre_gain):
    mixed = (
        inputs
        + rms_scale(attention_out, attention_gain)
        + normed
        + rms_scale(laurel_out, laurel_gain)
    ) * ROOT_HALF
    return (mixed, rms_scale(mixed, pre_gain))


def feed_mix(mixed, down_out, post_gain):
    return mixed + rms_scale(down_out, post_gain)


def final_mix(after_feed, per_out, final_gain):
    return after_feed + rms_scale(per_out, final_gain)


def product(left, right):
    return jnp.dot(left, right, preferred_element_type=jnp.float32)


def product_t(left, right):
    return lax.dot_general(
        left, right, (((1,), (1,)), ((), ())), preferred_element_type=jnp.float32
    )


def product_tn(left, right):
    return lax.dot_general(
        left, right, (((0,), (0,)), ((), ())), preferred_element_type=jnp.float32
    )


def hop(values, axis, mask):
    size = lax.axis_size(axis)
    return lax.ppermute(values, axis, [(i, i ^ mask) for i in range(size)])


def split_hop(values, even_mask, odd_mask):
    size = lax.axis_size(ROW) * lax.axis_size(COL)
    pairs = [(i, i ^ (odd_mask if i % 2 else even_mask)) for i in range(size)]
    return lax.ppermute(values, (ROW, COL), pairs)


def after(values, *others):
    return lax.optimization_barrier((values,) + others)[0]


def xor_blocks(values, me, count):
    width = values.shape[-1] // count
    blocks = [values[..., i * width : (i + 1) * width] for i in range(count)]
    bit = 1
    while bit < count:
        flip = (me & bit) != 0
        blocks = [jnp.where(flip, blocks[i ^ bit], blocks[i]) for i in range(count)]
        bit *= 2
    return jnp.concatenate(blocks, axis=-1)


def unit_of(axis):
    return lax.axis_size(COL) if axis == ROW else 2


def direct_gather(piece, axis, count):
    unit = 1 if axis == ROW else 2
    return [piece] + [hop(piece, axis, j * unit) for j in range(1, count)]


def xor_gather(piece, axis, count, middle=None):
    unit = 1 if axis == ROW else 2
    if count == 4:
        near = hop(piece, axis, unit)
        far = hop(piece, axis, 2 * unit)
        odd = lax.axis_index(COL) % 2 == 1
        flat = unit_of(axis)
        chosen_far, chosen_near = far, near
        if middle is not None:
            chosen_far, chosen_near = after(far, middle), after(near, middle)
        across = split_hop(jnp.where(odd, chosen_far, chosen_near), 2 * flat, flat)
        return [piece, near, far, across]
    pieces = [piece]
    bit = 1
    while bit < count:
        pieces = pieces + [hop(one, axis, bit * unit) for one in pieces]
        bit *= 2
    return pieces


def add_low(left, right):
    return (left.astype(jnp.float32) + right.astype(jnp.float32)).astype(jnp.bfloat16)


def xor_scatter(parts, axis, late=None, last=None, marks=None):
    count = parts.shape[0]
    unit = 1 if axis == ROW else 2
    if marks is not None and count != 4:
        marks.append(parts[0])
    if count == 4:
        odd = lax.axis_index(COL) % 2 == 1
        flat = unit_of(axis)
        across = split_hop(parts[3], 2 * flat, flat)
        early = split_hop(jnp.where(odd, parts[1], parts[2]), 2 * flat, flat)
        if late is not None:
            across = after(across, late)
        rest = add_low(jnp.where(odd, parts[2], parts[1]), across)
        if marks is not None:
            marks.append(rest)
        rest = split_hop(rest, flat, 2 * flat)
        if last is not None:
            rest = after(rest, last)
            early = after(early, last)
        return parts[0].astype(jnp.float32) + early.astype(jnp.float32) + rest.astype(jnp.float32)
    parts = [parts[j] for j in range(count)]
    bit = count // 2
    while bit > 0:
        parts = [add_low(parts[j], hop(parts[j + bit], axis, bit * unit)) for j in range(bit)]
        bit //= 2
    return parts[0].astype(jnp.float32)


def scatter_rows(total, row_total, late=None, last=None, marks=None):
    parts = total.reshape(row_total, -1, total.shape[1])
    return xor_scatter(parts, ROW, late, last, marks)


def scatter_cols(total, row_total, pairs, late=None, last=None, marks=None):
    mine = scatter_rows(total, row_total, late, last, marks).astype(jnp.bfloat16)
    width = mine.shape[1] // pairs
    parts = jnp.stack([mine[:, z * width : (z + 1) * width] for z in range(pairs)])
    return xor_scatter(parts, COL, None, None, marks)


def deal_rows_body(pairs, me_ref, block_ref, keep_ref, give_ref):
    for z in range(pairs):
        keep_ref[z] = block_ref[lax.bitwise_xor(me_ref[0], 2 * z)]
        give_ref[z] = block_ref[lax.bitwise_xor(me_ref[0], 2 * z + 1)]


def scatter_small(me, total, row_total, col_total):
    pairs = col_total // 2
    width = total.shape[1]
    blocks = total.reshape(row_total, col_total, -1, width)
    height = blocks.shape[2]
    half = jax.ShapeDtypeStruct((row_total, pairs, height, width), total.dtype)
    out_block = pl.BlockSpec((None, pairs, height, width), lambda r, s: (r, 0, 0, 0))
    keep, give = pl.pallas_call(
        partial(deal_rows_body, pairs),
        out_shape=(half, half),
        grid_spec=pltpu.PrefetchScalarGridSpec(
            num_scalar_prefetch=1,
            grid=(row_total,),
            in_specs=[
                pl.BlockSpec((None, col_total, height, width), lambda r, s: (r, 0, 0, 0))
            ],
            out_specs=(out_block, out_block),
        ),
        cost_estimate=pl.CostEstimate(
            flops=0, transcendentals=0, bytes_accessed=4 * total.size
        ),
    )(me, blocks)
    both = add_low(keep, hop(give, COL, 1)).reshape(row_total, pairs * height, width)
    mine = xor_scatter(both, ROW).astype(jnp.bfloat16)
    return xor_scatter(mine.reshape(pairs, height, width), COL)


def stack_body(*refs):
    for i, ref in enumerate(refs[:-1]):
        refs[-1][i] = ref[...]


def stack_pieces(pieces):
    shape = (len(pieces),) + pieces[0].shape
    return pl.pallas_call(
        stack_body,
        out_shape=jax.ShapeDtypeStruct(shape, pieces[0].dtype),
        cost_estimate=pl.CostEstimate(
            flops=0, transcendentals=0, bytes_accessed=4 * math.prod(shape)
        ),
    )(*pieces)


def gather_weight(shard, pairs, row_total, direct, first=None, second=None, middle=None):
    along = direct_gather(shard if first is None else after(shard, first), COL, pairs)
    stacked = stack_pieces(along)
    if second is not None:
        stacked = after(stacked, second)
    if direct:
        mine = direct_gather(stacked, ROW, row_total)
    else:
        mine = xor_gather(stacked, ROW, row_total, middle)
    other = [hop(one, COL, 1) for one in mine]
    return (mine, other), along[-1], mine[-1]


def place_body(pairs, me_ref, own_ref, other_ref, out_ref):
    for z in range(pairs):
        out_ref[lax.bitwise_xor(me_ref[0], 2 * z)] = own_ref[z]
        out_ref[lax.bitwise_xor(me_ref[0], 2 * z + 1)] = other_ref[z]


def over_col(me, own, pairs):
    stacked = stack_pieces(direct_gather(own, COL, pairs))
    other = hop(stacked, COL, 1)
    vmem = pl.BlockSpec(memory_space=pltpu.VMEM)
    return pl.pallas_call(
        partial(place_body, pairs),
        out_shape=jax.ShapeDtypeStruct((2 * pairs,) + own.shape, own.dtype),
        in_specs=[pl.BlockSpec(memory_space=pltpu.SMEM), vmem, vmem],
    )(me, stacked, other)


def block_of(ref, index, width):
    if len(ref.shape) == 3:
        return ref.at[index]
    return ref.at[:, pl.ds(pl.multiple_of(index * width, 128), width)]


def blocked(values, count):
    rows = values.shape[0]
    width = values.shape[1] // count
    if width % 128 == 0:
        return values
    return jnp.transpose(values.reshape(rows, count, width), (1, 0, 2))


def project_body(me_ref, left_ref, *refs):
    pieces, out_ref = refs[:-1], refs[-1]
    row_total = len(pieces) // 2
    pairs, height, width = pieces[0].shape
    for z in range(pairs):
        for core in range(2):
            total = None
            for r in range(row_total):
                part = jnp.dot(
                    left_ref[:, r * height : (r + 1) * height],
                    pieces[core * row_total + r][z],
                    preferred_element_type=jnp.float32,
                )
                total = part if total is None else total + part
            out = block_of(out_ref, lax.bitwise_xor(me_ref[0], 2 * z + core), width)
            out[...] = total.astype(out_ref.dtype)


def contract_body(me_ref, left_ref, *refs):
    pieces, out_ref = refs[:-1], refs[-1]
    row_total = len(pieces) // 2
    pairs, height, width = pieces[0].shape
    for r in range(row_total):
        total = None
        for z in range(pairs):
            for core in range(2):
                block = block_of(left_ref, lax.bitwise_xor(me_ref[0], 2 * z + core), width)
                part = lax.dot_general(
                    block[...],
                    pieces[core * row_total + r][z],
                    (((1,), (1,)), ((), ())),
                    preferred_element_type=jnp.float32,
                )
                total = part if total is None else total + part
        out_ref[:, r * height : (r + 1) * height] = total


def whole_call(body, shape, dtype, flops, me, left, pieces):
    mine, other = pieces
    operands = [left, *mine, *other]
    size = sum(one.size for one in operands) * 2
    vmem = pl.BlockSpec(memory_space=pltpu.VMEM)
    return pl.pallas_call(
        body,
        out_shape=jax.ShapeDtypeStruct(shape, dtype),
        in_specs=[pl.BlockSpec(memory_space=pltpu.SMEM)] + [vmem] * len(operands),
        out_specs=vmem,
        cost_estimate=pl.CostEstimate(flops=flops, transcendentals=0, bytes_accessed=size),
    )(me, *operands)


def project(me, left, pieces):
    pairs, _, width = pieces[0][0].shape
    rows = left.shape[0]
    shape = (rows, 2 * pairs * width) if width % 128 == 0 else (2 * pairs, rows, width)
    flops = 4 * rows * left.shape[1] * pairs * width
    out = whole_call(project_body, shape, jnp.bfloat16, flops, me, left, pieces)
    if len(shape) == 3:
        out = jnp.transpose(out, (1, 0, 2)).reshape(rows, 2 * pairs * width)
    return out


def contract(me, left, pieces):
    pairs, height, _ = pieces[0][0].shape
    shape = (left.shape[0], len(pieces[0]) * height)
    flops = 2 * left.size * shape[1]
    left = blocked(left, 2 * pairs)
    return whole_call(contract_body, shape, jnp.float32, flops, me, left, pieces)


def deal_body(pairs, me_ref, columns_ref, keep_ref, give_ref):
    width = keep_ref.shape[1] // pairs
    for z in range(pairs):
        span = slice(z * width, (z + 1) * width)
        for core, out_ref in enumerate((keep_ref, give_ref)):
            index = lax.bitwise_xor(me_ref[0], 2 * z + core)
            out_ref[:, span] = block_of(columns_ref, index, width)[...]


def pair_columns(me, columns, count):
    rows, width = columns.shape
    half = jax.ShapeDtypeStruct((rows, width // 2), columns.dtype)
    values = blocked(columns, count)
    keep, give = pl.pallas_call(
        partial(deal_body, count // 2),
        out_shape=(half, half),
        in_specs=[
            pl.BlockSpec(memory_space=pltpu.SMEM),
            pl.BlockSpec(memory_space=pltpu.VMEM),
        ],
        cost_estimate=pl.CostEstimate(
            flops=0, transcendentals=0, bytes_accessed=4 * rows * width
        ),
    )(me, values)
    return jnp.concatenate([keep, hop(give, COL, 1)], axis=0)


def pair_rows(own):
    return jnp.concatenate([own, hop(own, COL, 1)], axis=0)


def attend_body(span_ref, window_ref, query_ref, key_ref, value_ref, out_ref, inverse_ref, sums, weights):
    rows = query_ref.shape[0]
    low_edge = window_ref[:, 0:1]
    high_edge = window_ref[:, 1:2]
    query = query_ref[...]
    sums[...] = jnp.zeros_like(sums)
    weights[...] = jnp.zeros_like(weights)

    def one_tile(tile, carry):
        scores = lax.dot_general(
            query, key_ref[tile], (((1,), (1,)), ((), ())), preferred_element_type=jnp.float32
        )
        place = tile * rows + lax.broadcasted_iota(jnp.int32, scores.shape, 1)
        exps = jnp.where((place >= low_edge) & (place < high_edge), jnp.exp(scores), 0.0)
        part = exps[:, :128]
        for start in range(128, rows, 128):
            part = part + exps[:, start : start + 128]
        weights[...] += part
        sums[...] += jnp.dot(
            exps.astype(jnp.bfloat16), value_ref[tile], preferred_element_type=jnp.float32
        )
        return carry

    lax.fori_loop(span_ref[0], span_ref[1], one_tile, 0)
    inverse = 1.0 / jnp.sum(weights[...], axis=1, keepdims=True)
    out_ref[...] = (sums[...] * inverse).astype(jnp.bfloat16)
    inverse_ref[...] = jnp.broadcast_to(inverse, inverse_ref.shape)


def attend(span, window, query, gathered):
    rows, width = query.shape
    tiles = gathered.shape[0]
    groups = HEADS // KV_HEADS
    half = pl.BlockSpec((rows, HEAD), lambda h, s: (0, h))
    flops = 4 * rows * rows * tiles * width
    return pl.pallas_call(
        attend_body,
        out_shape=(
            jax.ShapeDtypeStruct((rows, width), jnp.bfloat16),
            jax.ShapeDtypeStruct((rows, HEADS * 128), jnp.float32),
        ),
        grid_spec=pltpu.PrefetchScalarGridSpec(
            num_scalar_prefetch=1,
            grid=(HEADS,),
            in_specs=[
                pl.BlockSpec((rows, 2), lambda h, s: (0, 0)),
                half,
                pl.BlockSpec((tiles, None, rows, HEAD), lambda h, s: (0, 0, 0, h // groups)),
                pl.BlockSpec((tiles, None, rows, HEAD), lambda h, s: (0, 1, 0, h // groups)),
            ],
            out_specs=(half, pl.BlockSpec((rows, 128), lambda h, s: (0, h))),
            scratch_shapes=[
                pltpu.VMEM((rows, HEAD), jnp.float32),
                pltpu.VMEM((rows, 128), jnp.float32),
            ],
        ),
        cost_estimate=pl.CostEstimate(
            flops=flops, transcendentals=rows * rows * tiles * HEADS, bytes_accessed=8 * rows * width
        ),
    )(span, window, query, gathered, gathered)


def attend_back_body(
    span_ref, window_ref, query_ref, key_ref, value_ref, grad_ref, out_ref, inverse_ref,
    query_grad_ref, pair_grad_ref, query_sum, key_sum, value_sum,
):
    rows = query_ref.shape[0]
    groups = HEADS // KV_HEADS
    head = pl.program_id(0)
    low_edge = window_ref[0:1, :]
    high_edge = window_ref[1:2, :]
    query = query_ref[...]
    grad_wide = grad_ref[...].astype(jnp.float32)
    inverse = inverse_ref[:, 0:1]
    delta = jnp.sum(grad_wide * out_ref[...].astype(jnp.float32), axis=1, keepdims=True) * inverse
    delta_row = jnp.transpose(jnp.broadcast_to(delta, (rows, 128)))[0:1, :]
    grad_scaled = (grad_wide * inverse).astype(jnp.bfloat16)
    query_sum[...] = jnp.zeros_like(query_sum)

    @pl.when(lax.rem(head, groups) == 0)
    def _():
        key_sum[...] = jnp.zeros_like(key_sum)
        value_sum[...] = jnp.zeros_like(value_sum)

    def one_tile(tile, carry):
        keys = key_ref[tile]
        contract_last = (((1,), (1,)), ((), ()))
        scores = lax.dot_general(keys, query, contract_last, preferred_element_type=jnp.float32)
        place = tile * rows + lax.broadcasted_iota(jnp.int32, scores.shape, 0)
        exps = jnp.where((place >= low_edge) & (place < high_edge), jnp.exp(scores), 0.0)
        prob_grad = lax.dot_general(
            value_ref[tile], grad_scaled, contract_last, preferred_element_type=jnp.float32
        )
        score_grad = (exps * (prob_grad - delta_row)).astype(jnp.bfloat16)
        key_sum[tile] += jnp.dot(score_grad, query, preferred_element_type=jnp.float32)
        value_sum[tile] += jnp.dot(
            exps.astype(jnp.bfloat16), grad_scaled, preferred_element_type=jnp.float32
        )
        query_sum[...] += lax.dot_general(
            score_grad, keys, (((0,), (0,)), ((), ())), preferred_element_type=jnp.float32
        )
        return carry

    lax.fori_loop(span_ref[0], span_ref[1], one_tile, 0)
    query_grad_ref[...] = query_sum[...] * (1.0 / math.sqrt(HEAD))

    @pl.when(lax.rem(head, groups) == groups - 1)
    def _():
        pair_grad_ref[:, 0] = key_sum[...].astype(jnp.bfloat16)
        pair_grad_ref[:, 1] = value_sum[...].astype(jnp.bfloat16)


def attend_back(span, window, query, gathered, grad, out, inverse):
    rows, width = query.shape
    tiles = gathered.shape[0]
    groups = HEADS // KV_HEADS
    half = pl.BlockSpec((rows, HEAD), lambda h, s: (0, h))
    return pl.pallas_call(
        attend_back_body,
        out_shape=(
            jax.ShapeDtypeStruct((rows, width), jnp.float32),
            jax.ShapeDtypeStruct(gathered.shape, jnp.bfloat16),
        ),
        grid_spec=pltpu.PrefetchScalarGridSpec(
            num_scalar_prefetch=1,
            grid=(HEADS,),
            in_specs=[
                pl.BlockSpec((2, rows), lambda h, s: (0, 0)),
                half,
                pl.BlockSpec((tiles, None, rows, HEAD), lambda h, s: (0, 0, 0, h // groups)),
                pl.BlockSpec((tiles, None, rows, HEAD), lambda h, s: (0, 1, 0, h // groups)),
                half,
                half,
                pl.BlockSpec((rows, 128), lambda h, s: (0, h)),
            ],
            out_specs=(
                half,
                pl.BlockSpec((tiles, 2, rows, HEAD), lambda h, s: (0, 0, 0, h // groups)),
            ),
            scratch_shapes=[
                pltpu.VMEM((rows, HEAD), jnp.float32),
                pltpu.VMEM((tiles, rows, HEAD), jnp.float32),
                pltpu.VMEM((tiles, rows, HEAD), jnp.float32),
            ],
        ),
        cost_estimate=pl.CostEstimate(
            flops=10 * rows * rows * tiles * width,
            transcendentals=rows * rows * tiles * HEADS,
            bytes_accessed=16 * rows * width,
        ),
    )(span, window, query, gathered, gathered, grad, out, inverse)


def local(
    layer_input,
    per_layer_input,
    out_cotangent,
    seq_lengths,
    query_weight,
    key_weight,
    value_weight,
    out_weight,
    gate_weight,
    up_weight,
    down_weight,
    laurel_down,
    laurel_up,
    per_layer_gate,
    per_layer_projection,
    input_gain,
    query_gain,
    key_gain,
    attention_gain,
    laurel_gain,
    pre_feed_gain,
    post_feed_gain,
    per_layer_gain,
):
    rows, width = layer_input.shape
    row_total = lax.axis_size(ROW)
    col_total = lax.axis_size(COL)
    pairs = col_total // 2
    me_row = lax.axis_index(ROW)
    me_col = lax.axis_index(COL)
    rank = laurel_down.shape[1]
    embed = per_layer_gate.shape[1]
    kv_width = key_weight.shape[1]
    feed_width = gate_weight.shape[1]
    low = jnp.bfloat16
    wide = jnp.float32

    me = me_col.astype(jnp.int32).reshape(1)
    small_rows = laurel_down.shape[0]
    head_part = query_gain.shape[0]

    gains_own = jnp.concatenate(
        [
            input_gain,
            attention_gain,
            laurel_gain,
            pre_feed_gain,
            post_feed_gain,
            per_layer_gain,
            query_gain,
            key_gain,
        ]
    )
    gain_total = gains_own.shape[0]
    laurel_own = jnp.concatenate([laurel_down, laurel_up], axis=1)
    line = laurel_own.shape[1]
    gain_lines = -(-gain_total // line)
    gains_block = jnp.pad(gains_own, (0, gain_lines * line - gain_total)).reshape(gain_lines, line)
    first_own = jnp.concatenate(
        [laurel_own, jnp.pad(gains_block, ((0, 16 - gain_lines), (0, 0)))], axis=0
    )

    spread = jnp.broadcast_to(first_own[None], (col_total,) + first_own.shape)
    first_group = lax.all_to_all(spread, COL, 0, 0, tiled=True)
    first_all = jnp.stack(direct_gather(first_group, ROW, row_total))
    laurel_all = first_all[:, :, :small_rows].reshape(-1, line)
    laurel_down_all = laurel_all[:, :rank]
    laurel_up_all = laurel_all[:, rank:]
    gain_rows = first_all[:, :, small_rows : small_rows + gain_lines].astype(wide)
    gain_rows = gain_rows.reshape(row_total, col_total, gain_lines * line)
    gains = gain_rows[:, :, : 6 * small_rows].reshape(row_total, col_total, 6, small_rows)
    gains = jnp.transpose(gains, (2, 0, 1, 3)).reshape(6, width)
    gain_list = [gains[i] for i in range(6)]
    head_gains = []
    for i in range(2):
        start = 6 * small_rows + i * head_part
        rel = gain_rows[:, :, start : start + head_part].reshape(-1)
        head_gains.append(xor_blocks(rel, me_row, row_total))

    kv_pieces, kv_first, kv_last = gather_weight(
        jnp.concatenate([key_weight, value_weight], axis=1), pairs, row_total, True
    )
    query_pieces, _, query_last = gather_weight(
        query_weight, pairs, row_total, False, kv_first, kv_last
    )
    tokens_at = me_col * rows + jnp.arange(rows, dtype=jnp.int32)
    position, begin, reach = placement_info(seq_lengths[0], tokens_at)
    window = jnp.stack([begin, reach])
    span = jnp.stack([jnp.min(begin) // rows, (jnp.max(reach) + rows - 1) // rows])
    inputs = xor_blocks(layer_input, me_row, row_total).astype(wide)
    cotangent = xor_blocks(out_cotangent, me_row, row_total).astype(wide)
    normed, input_pull = jax.vjp(rms_scale, inputs, gain_list[0])
    normed_low = normed.astype(low)
    cosine, sine_part = angles(position)
    query_gain_row = head_gains[0].reshape(1, HEAD)
    key_gain_row = head_gains[1].reshape(1, HEAD)
    kv_own = project(me, normed_low, kv_pieces)
    pair_own = small_call(
        partial(pair_body, col_total),
        jax.ShapeDtypeStruct((2, rows, KV_HEADS * HEAD), low),
        kv_own,
        key_gain_row,
        cosine,
        sine_part,
    )
    pair_all = lax.all_gather(pair_own, COL, axis=0, tiled=True)
    pair_all = pair_all.reshape(col_total, 2, rows, KV_HEADS * HEAD)
    query_own = project(me, normed_low, query_pieces)
    query_scaled = small_call(
        partial(query_body, 1.0 / math.sqrt(HEAD)),
        jax.ShapeDtypeStruct((rows, HEADS * HEAD), low),
        query_own,
        query_gain_row,
        cosine,
        sine_part,
    )
    attended, inverse = attend(span, jnp.transpose(window), query_scaled, pair_all)
    out_pieces, _, _ = gather_weight(
        out_weight, pairs, row_total, False, kv_first, query_last, attended
    )
    attention_out = contract(me, attended, out_pieces)
    laurel_mid = product(normed_low, laurel_down_all).astype(low)
    laurel_out = product_t(laurel_mid, laurel_up_all)
    (mixed, feed_in), mix_pull = jax.vjp(
        residual_mix,
        inputs,
        attention_out,
        normed_low.astype(wide),
        laurel_out,
        gain_list[1],
        gain_list[2],
        gain_list[3],
    )
    feed_low = feed_in.astype(low)
    feed_pieces = xor_gather(
        jnp.concatenate([gate_weight, up_weight], axis=1), ROW, row_total, feed_low
    )
    layer_own = jnp.concatenate([per_layer_gate, per_layer_projection], axis=1)
    feed_all = jnp.concatenate(feed_pieces, axis=0)
    halves = 2
    part_rows = rows // halves
    feed_tokens, hidden_pulls, hidden_lows, down_outs = [], [], [], []
    done = None
    for h in range(halves):
        tokens = lax.all_gather(
            feed_low[h * part_rows : (h + 1) * part_rows], COL, axis=0, tiled=True
        )
        tokens = tokens if done is None else after(tokens, done)
        gate_up = product(tokens, feed_all).astype(low)
        if h == 0:
            down_pieces = xor_gather(down_weight, ROW, row_total, gate_up)
            down_all = jnp.concatenate(down_pieces, axis=0)
        hidden, hidden_pull = jax.vjp(
            geglu, gate_up[:, :feed_width].astype(wide), gate_up[:, feed_width:].astype(wide)
        )
        hidden_low = hidden.astype(low)
        done = product_t(hidden_low, down_all).astype(low)
        down_outs.append(lax.psum_scatter(done, COL, scatter_dimension=0, tiled=True))
        feed_tokens.append(tokens)
        hidden_pulls.append(hidden_pull)
        hidden_lows.append(hidden_low)
    layer_group = over_col(me, after(layer_own, done), pairs)
    layer_pieces = direct_gather(layer_group, ROW, row_total)
    layer_all = jnp.concatenate([one.reshape(-1, 2 * embed) for one in layer_pieces], axis=0)
    layer_gate_all = layer_all[:, :embed]
    layer_proj_all = layer_all[:, embed:]
    down_out = jnp.concatenate(down_outs, axis=0).astype(wide)
    after_feed, feed_pull = jax.vjp(feed_mix, mixed, down_out, gain_list[4])
    after_low = after_feed.astype(low)
    per_pre = product(after_low, layer_gate_all)
    per_hidden, per_pull = jax.vjp(geglu, per_pre, per_layer_input.astype(wide))
    per_low = per_hidden.astype(low)
    per_out = product_t(per_low, layer_proj_all)
    output, final_pull = jax.vjp(final_mix, after_feed, per_out, gain_list[5])
    after_grad, per_out_grad, final_gain_grad = final_pull(cotangent)
    per_out_low = per_out_grad.astype(low)
    per_hidden_grad = product(per_out_low, layer_proj_all)
    layer_proj_grad = product_tn(per_out_low, per_low)
    per_pre_grad, embed_grad = per_pull(per_hidden_grad)
    per_pre_low = per_pre_grad.astype(low)
    after_grad = after_grad + product_t(per_pre_low, layer_gate_all)
    layer_gate_grad = product_tn(after_low, per_pre_low)
    mixed_grad, down_grad, post_gain_grad = feed_pull(after_grad)
    down_low = down_grad.astype(low)
    layer_grad = scatter_small(
        me,
        after(jnp.concatenate([layer_gate_grad, layer_proj_grad], axis=1).astype(low), down_low),
        row_total,
        col_total,
    )
    attended_pair = pair_columns(me, after(attended, down_low), col_total)
    normed_pair = pair_rows(after(normed_low, down_low))
    feed_in_grads = []
    done = None
    for h in range(halves):
        tokens = lax.all_gather(
            down_low[h * part_rows : (h + 1) * part_rows], COL, axis=0, tiled=True
        )
        if done is None:
            tokens, layer_grad, attended_pair, normed_pair = lax.optimization_barrier(
                (tokens, layer_grad, attended_pair, normed_pair)
            )
        else:
            tokens = after(tokens, done, down_first, feed_first)
        hidden_grad = product(tokens, down_all)
        gate_grad, up_grad = hidden_pulls[h](hidden_grad)
        feed_grad_low = jnp.concatenate([gate_grad.astype(low), up_grad.astype(low)], axis=1)
        done = product_t(feed_grad_low, feed_all).astype(low)
        feed_in_grads.append(lax.psum_scatter(done, COL, scatter_dimension=0, tiled=True))
        if h == 0:
            down_first = product_tn(after(tokens, done), hidden_lows[0]).astype(low)
            feed_first = product_tn(after(feed_tokens[0], down_first), feed_grad_low).astype(low)
    feed_in_grad = jnp.concatenate(feed_in_grads, axis=0).astype(wide)
    down_total = product_tn(after(tokens, done), hidden_lows[1]) + down_first.astype(wide)
    down_total = down_total.astype(low)
    feed_total = product_tn(after(feed_tokens[1], down_total), feed_grad_low)
    feed_total = (feed_total + feed_first.astype(wide)).astype(low)
    (
        inputs_grad,
        attention_grad,
        normed_grad,
        laurel_out_grad,
        attention_gain_grad,
        laurel_gain_grad,
        pre_gain_grad,
    ) = mix_pull((mixed_grad, feed_in_grad))
    attention_low = attention_grad.astype(low)
    attended_grad = project(me, attention_low, out_pieces)
    query_rot_grad, pair_parts = attend_back(
        span, window, query_scaled, pair_all, attended_grad, attended, inverse
    )
    pair_sum = lax.psum_scatter(
        pair_parts.reshape(2 * col_total, rows, KV_HEADS * HEAD),
        COL,
        scatter_dimension=0,
        tiled=True,
    )
    attention_pair = pair_rows(attention_low)
    out_total = product_tn(after(attention_pair, pair_parts), attended_pair).astype(low)
    query_rot_grad = after(query_rot_grad, out_total)
    gain_row = jax.ShapeDtypeStruct((1, HEAD), wide)
    query_low, query_gain_grad = small_call(
        query_back_body,
        (jax.ShapeDtypeStruct((rows, HEADS * HEAD), low), gain_row),
        query_own,
        query_rot_grad,
        query_gain_row,
        cosine,
        sine_part,
    )
    query_total = product_tn(
        after(normed_pair, out_total), pair_columns(me, query_low, col_total)
    ).astype(low)
    query_part = contract(me, after(query_low, query_total), query_pieces)

    laurel_out_low = after(laurel_out_grad.astype(low), query_total)
    laurel_mid_grad = product(laurel_out_low, laurel_up_all)
    laurel_up_grad = product_tn(laurel_out_low, laurel_mid)
    laurel_mid_low = laurel_mid_grad.astype(low)
    laurel_down_grad = product_tn(normed_low, laurel_mid_low)
    small_total = jnp.concatenate([laurel_down_grad, laurel_up_grad], axis=1)
    normed_grad = normed_grad + product_t(laurel_mid_low, laurel_down_all) + query_part
    pair_sum = after(pair_sum, normed_grad, small_total)
    kv_grad, key_gain_grad = small_call(
        partial(pair_back_body, col_total),
        (jax.ShapeDtypeStruct(kv_own.shape, low), gain_row),
        kv_own,
        pair_sum,
        key_gain_row,
        cosine,
        sine_part,
    )
    kv_total = product_tn(normed_pair, pair_columns(me, kv_grad, col_total)).astype(low)
    marks = []
    normed_grad = normed_grad + contract(me, after(kv_grad, kv_total), kv_pieces)
    kv_weight_grad = scatter_cols(kv_total, row_total, pairs, normed_grad, None, marks)
    mark = marks[0]
    query_marks = []
    query_weight_grad = scatter_cols(query_total, row_total, pairs, mark, mark, query_marks)
    out_weight_grad = scatter_cols(out_total, row_total, pairs, query_part, normed_grad)
    down_weight_grad = scatter_rows(down_total, row_total, feed_total, query_marks[0])
    feed_weight_grad = scatter_rows(feed_total, row_total, pair_parts, marks[-1])
    input_part, input_gain_grad = input_pull(after(normed_grad, mark))
    input_total = xor_blocks((inputs_grad + input_part).astype(low), me_row, row_total)

    wide_gains = jnp.stack(
        [
            input_gain_grad,
            attention_gain_grad,
            laurel_gain_grad,
            pre_gain_grad,
            post_gain_grad,
            final_gain_grad,
        ]
    ).reshape(6, row_total, col_total, small_rows)
    wide_gains = jnp.transpose(wide_gains, (1, 2, 0, 3)).reshape(row_total, col_total, -1)
    both_gains = jnp.concatenate([query_gain_grad, key_gain_grad], axis=0)
    both_gains = xor_blocks(both_gains, me_row, row_total)
    both_gains = both_gains.reshape(2, row_total, col_total, head_part)
    both_gains = jnp.transpose(both_gains, (1, 2, 0, 3)).reshape(row_total, col_total, -1)
    gain_sums = jnp.concatenate([wide_gains, both_gains], axis=2)
    gain_sums = jnp.pad(gain_sums, ((0, 0), (0, 0), (0, gain_lines * line - gain_total)))
    gain_sums = gain_sums.reshape(row_total, col_total, gain_lines, line)
    laurel_parts = small_total.reshape(row_total, col_total, small_rows, line)
    sums = after(jnp.concatenate([laurel_parts, gain_sums], axis=2), query_marks[0])
    sums = sums[0] + sum(hop(sums[j], ROW, j) for j in range(1, row_total))
    sums = lax.all_to_all(sums, COL, 0, 0, tiled=True)
    sums = jnp.sum(after(sums, query_marks[-1]), axis=0)
    laurel_grad = sums[:small_rows]
    gain_sums = sums[small_rows:].reshape(-1)
    gain_out = [gain_sums[i * small_rows : (i + 1) * small_rows] for i in range(6)]
    head_out = gain_sums[6 * small_rows : gain_total]
    return (
        xor_blocks(output.astype(low), me_row, row_total),
        input_total,
        embed_grad.astype(low),
        query_weight_grad,
        kv_weight_grad[:, :kv_width],
        kv_weight_grad[:, kv_width:],
        out_weight_grad,
        feed_weight_grad[:, :feed_width],
        feed_weight_grad[:, feed_width:],
        down_weight_grad,
        laurel_grad[:, :rank],
        laurel_grad[:, rank:],
        layer_grad[:, :embed],
        layer_grad[:, embed:],
        gain_out[0],
        head_out[:head_part],
        head_out[head_part:],
        gain_out[1],
        gain_out[2],
        gain_out[3],
        gain_out[4],
        gain_out[5],
    )


def solution(mesh):
    in_specs = (
        P((ROW, COL), None),
        P((ROW, COL), None),
        P((ROW, COL), None),
        P(ROW, None),
        P(ROW, COL),
        P(ROW, COL),
        P(ROW, COL),
        P(ROW, COL),
        P(ROW, COL),
        P(ROW, COL),
        P(ROW, COL),
        P((ROW, COL), None),
        P((ROW, COL), None),
        P((ROW, COL), None),
        P((ROW, COL), None),
        P((ROW, COL)),
        P((ROW, COL)),
        P((ROW, COL)),
        P((ROW, COL)),
        P((ROW, COL)),
        P((ROW, COL)),
        P((ROW, COL)),
        P((ROW, COL)),
    )
    out_specs = (
        P((ROW, COL), None),
        P((ROW, COL), None),
        P((ROW, COL), None),
        P(ROW, COL),
        P(ROW, COL),
        P(ROW, COL),
        P(ROW, COL),
        P(ROW, COL),
        P(ROW, COL),
        P(ROW, COL),
        P((ROW, COL), None),
        P((ROW, COL), None),
        P((ROW, COL), None),
        P((ROW, COL), None),
        P((ROW, COL)),
        P((ROW, COL)),
        P((ROW, COL)),
        P((ROW, COL)),
        P((ROW, COL)),
        P((ROW, COL)),
        P((ROW, COL)),
        P((ROW, COL)),
    )

    return jax.shard_map(local, mesh=mesh, in_specs=in_specs, out_specs=out_specs, check_vma=False)
```

```python
from functools import partial
import math

import jax
import jax.numpy as jnp
from jax import lax
from jax.experimental import pallas as pl
from jax.experimental.pallas import tpu as pltpu
from jax.sharding import PartitionSpec as P


HEADS = 8
KV_HEADS = 2
HEAD = 256
BLOCK = 256
ROW = "row"
COL = "col"


NORM_EPS = 1e-06
ROOT_HALF = 0.7071067811865476
ROPE_THETA = 1000000.0


def rms_scale(values, scale_gain):
    return (
        values
        * lax.rsqrt(jnp.mean(values * values, axis=-1, keepdims=True) + NORM_EPS)
        * scale_gain
    )


def angles(position):
    half_width = HEAD // 2
    steps_up = jnp.arange(half_width, dtype=jnp.float32)
    frequency = jnp.exp(steps_up * (-2.0 * math.log(ROPE_THETA) / HEAD))
    angle_grid = position.astype(jnp.float32)[:, None] * frequency[None, :]
    return (jnp.cos(angle_grid), jnp.sin(angle_grid))


def turn(values, cosine, sine_part):
    half_width = HEAD // 2
    first_half = values[:, :half_width]
    second_half = values[:, half_width:]
    return jnp.concatenate(
        [
            first_half * cosine - second_half * sine_part,
            second_half * cosine + first_half * sine_part,
        ],
        axis=1,
    )


def inverse_rms(values):
    return lax.rsqrt(jnp.mean(values * values, axis=1, keepdims=True) + NORM_EPS)


def norm_back(values, inverse, grad):
    return inverse * (
        grad - values * (inverse * inverse * jnp.mean(grad * values, axis=1, keepdims=True))
    )


def query_body(scale, query_ref, gain_ref, cosine_ref, sine_ref, out_ref):
    for head in range(query_ref.shape[1] // HEAD):
        span = slice(head * HEAD, (head + 1) * HEAD)
        values = query_ref[:, span].astype(jnp.float32)
        normed = values * inverse_rms(values) * gain_ref[...]
        turned = turn(normed, cosine_ref[...], sine_ref[...]).astype(jnp.bfloat16)
        out_ref[:, span] = turned * jnp.bfloat16(scale)


def query_back_body(query_ref, grad_ref, gain_ref, cosine_ref, sine_ref, out_ref, gain_grad_ref):
    total = jnp.zeros((1, HEAD), jnp.float32)
    for head in range(query_ref.shape[1] // HEAD):
        span = slice(head * HEAD, (head + 1) * HEAD)
        values = query_ref[:, span].astype(jnp.float32)
        inverse = inverse_rms(values)
        grad = turn(grad_ref[:, span], cosine_ref[...], -sine_ref[...])
        total = total + jnp.sum(grad * values * inverse, axis=0, keepdims=True)
        out_ref[:, span] = norm_back(values, inverse, grad * gain_ref[...]).astype(jnp.bfloat16)
    gain_grad_ref[...] = total


def head_of(columns, head, kind, count):
    width = columns.shape[1] // count // 2
    per_head = HEAD // width
    parts = [
        columns[:, (2 * c + kind) * width : (2 * c + kind + 1) * width]
        for c in range(head * per_head, (head + 1) * per_head)
    ]
    return jnp.concatenate(parts, axis=1)


def pair_body(count, columns_ref, gain_ref, cosine_ref, sine_ref, out_ref):
    columns = columns_ref[...].astype(jnp.float32)
    for head in range(KV_HEADS):
        span = slice(head * HEAD, (head + 1) * HEAD)
        keys = head_of(columns, head, 0, count)
        normed = keys * inverse_rms(keys) * gain_ref[...]
        out_ref[0, :, span] = turn(normed, cosine_ref[...], sine_ref[...]).astype(jnp.bfloat16)
        values = head_of(columns, head, 1, count)
        out_ref[1, :, span] = (values * inverse_rms(values)).astype(jnp.bfloat16)


def pair_back_body(
    count, columns_ref, grad_ref, gain_ref, cosine_ref, sine_ref, out_ref, gain_grad_ref
):
    columns = columns_ref[...].astype(jnp.float32)
    width = columns.shape[1] // count // 2
    total = jnp.zeros((1, HEAD), jnp.float32)
    pieces = []
    for head in range(KV_HEADS):
        span = slice(head * HEAD, (head + 1) * HEAD)
        keys = head_of(columns, head, 0, count)
        inverse = inverse_rms(keys)
        grad = grad_ref[0, :, span].astype(jnp.float32)
        grad = turn(grad, cosine_ref[...], -sine_ref[...])
        total = total + jnp.sum(grad * keys * inverse, axis=0, keepdims=True)
        key_grad = norm_back(keys, inverse, grad * gain_ref[...])
        values = head_of(columns, head, 1, count)
        value_grad = norm_back(
            values, inverse_rms(values), grad_ref[1, :, span].astype(jnp.float32)
        )
        for c in range(HEAD // width):
            pieces.append(key_grad[:, c * width : (c + 1) * width])
            pieces.append(value_grad[:, c * width : (c + 1) * width])
    out_ref[...] = jnp.concatenate(pieces, axis=1).astype(jnp.bfloat16)
    gain_grad_ref[...] = total


def small_call(body, shapes, *operands):
    size = 4 * sum(one.size for one in operands)
    return pl.pallas_call(
        body,
        out_shape=shapes,
        cost_estimate=pl.CostEstimate(flops=4 * size, transcendentals=0, bytes_accessed=size),
    )(*operands)


def placement_info(lengths, tokens_at):
    finish = jnp.cumsum(lengths)
    begins = finish - lengths
    segment = jnp.sum((tokens_at[:, None] >= finish[None, :]).astype(jnp.int32), axis=1)
    chosen = segment[:, None] == jnp.arange(lengths.shape[0], dtype=jnp.int32)[None, :]
    begin = jnp.sum(jnp.where(chosen, begins[None, :], 0), axis=1)
    end = jnp.sum(jnp.where(chosen, finish[None, :], 0), axis=1)
    position = tokens_at - begin
    reach = jnp.minimum(end, begin + (position // BLOCK + 1) * BLOCK)
    return (position, begin, reach)


def geglu(gate_in, up_in):
    return jax.nn.gelu(gate_in, approximate=True) * up_in


def residual_mix(inputs, attention_out, normed, laurel_out, attention_gain, laurel_gain, pre_gain):
    mixed = (
        inputs
        + rms_scale(attention_out, attention_gain)
        + normed
        + rms_scale(laurel_out, laurel_gain)
    ) * ROOT_HALF
    return (mixed, rms_scale(mixed, pre_gain))


def feed_mix(mixed, down_out, post_gain):
    return mixed + rms_scale(down_out, post_gain)


def final_mix(after_feed, per_out, final_gain):
    return after_feed + rms_scale(per_out, final_gain)


def product(left, right):
    return jnp.dot(left, right, preferred_element_type=jnp.float32)


def product_t(left, right):
    return lax.dot_general(
        left, right, (((1,), (1,)), ((), ())), preferred_element_type=jnp.float32
    )


def product_tn(left, right):
    return lax.dot_general(
        left, right, (((0,), (0,)), ((), ())), preferred_element_type=jnp.float32
    )


def hop(values, axis, mask):
    size = lax.axis_size(axis)
    return lax.ppermute(values, axis, [(i, i ^ mask) for i in range(size)])


def split_hop(values, even_mask, odd_mask):
    size = lax.axis_size(ROW) * lax.axis_size(COL)
    pairs = [(i, i ^ (odd_mask if i % 2 else even_mask)) for i in range(size)]
    return lax.ppermute(values, (ROW, COL), pairs)


def after(values, *others):
    return lax.optimization_barrier((values,) + others)[0]


def xor_blocks(values, me, count):
    width = values.shape[-1] // count
    blocks = [values[..., i * width : (i + 1) * width] for i in range(count)]
    bit = 1
    while bit < count:
        flip = (me & bit) != 0
        blocks = [jnp.where(flip, blocks[i ^ bit], blocks[i]) for i in range(count)]
        bit *= 2
    return jnp.concatenate(blocks, axis=-1)


def unit_of(axis):
    return lax.axis_size(COL) if axis == ROW else 2


def direct_gather(piece, axis, count):
    unit = 1 if axis == ROW else 2
    return [piece] + [hop(piece, axis, j * unit) for j in range(1, count)]


def xor_gather(piece, axis, count, middle=None):
    unit = 1 if axis == ROW else 2
    if count == 4:
        near = hop(piece, axis, unit)
        far = hop(piece, axis, 2 * unit)
        odd = lax.axis_index(COL) % 2 == 1
        flat = unit_of(axis)
        chosen_far, chosen_near = far, near
        if middle is not None:
            chosen_far, chosen_near = after(far, middle), after(near, middle)
        across = split_hop(jnp.where(odd, chosen_far, chosen_near), 2 * flat, flat)
        return [piece, near, far, across]
    pieces = [piece]
    bit = 1
    while bit < count:
        pieces = pieces + [hop(one, axis, bit * unit) for one in pieces]
        bit *= 2
    return pieces


def add_low(left, right):
    return (left.astype(jnp.float32) + right.astype(jnp.float32)).astype(jnp.bfloat16)


def xor_scatter(parts, axis, late=None, last=None, marks=None):
    count = parts.shape[0]
    unit = 1 if axis == ROW else 2
    if marks is not None and count != 4:
        marks.append(parts[0])
    if count == 4:
        odd = lax.axis_index(COL) % 2 == 1
        flat = unit_of(axis)
        across = split_hop(parts[3], 2 * flat, flat)
        early = split_hop(jnp.where(odd, parts[1], parts[2]), 2 * flat, flat)
        if late is not None:
            across = after(across, late)
        rest = add_low(jnp.where(odd, parts[2], parts[1]), across)
        if marks is not None:
            marks.append(rest)
        rest = split_hop(rest, flat, 2 * flat)
        if last is not None:
            rest = after(rest, last)
            early = after(early, last)
        return parts[0].astype(jnp.float32) + early.astype(jnp.float32) + rest.astype(jnp.float32)
    parts = [parts[j] for j in range(count)]
    bit = count // 2
    while bit > 0:
        parts = [add_low(parts[j], hop(parts[j + bit], axis, bit * unit)) for j in range(bit)]
        bit //= 2
    return parts[0].astype(jnp.float32)


def scatter_rows(total, row_total, late=None, last=None, marks=None):
    parts = total.reshape(row_total, -1, total.shape[1])
    return xor_scatter(parts, ROW, late, last, marks)


def scatter_cols(total, row_total, pairs, late=None, last=None, marks=None):
    mine = scatter_rows(total, row_total, late, last, marks).astype(jnp.bfloat16)
    width = mine.shape[1] // pairs
    parts = jnp.stack([mine[:, z * width : (z + 1) * width] for z in range(pairs)])
    return xor_scatter(parts, COL, None, None, marks)


def deal_rows_body(pairs, me_ref, block_ref, keep_ref, give_ref):
    for z in range(pairs):
        keep_ref[z] = block_ref[lax.bitwise_xor(me_ref[0], 2 * z)]
        give_ref[z] = block_ref[lax.bitwise_xor(me_ref[0], 2 * z + 1)]


def scatter_small(me, total, row_total, col_total):
    pairs = col_total // 2
    width = total.shape[1]
    blocks = total.reshape(row_total, col_total, -1, width)
    height = blocks.shape[2]
    half = jax.ShapeDtypeStruct((row_total, pairs, height, width), total.dtype)
    out_block = pl.BlockSpec((None, pairs, height, width), lambda r, s: (r, 0, 0, 0))
    keep, give = pl.pallas_call(
        partial(deal_rows_body, pairs),
        out_shape=(half, half),
        grid_spec=pltpu.PrefetchScalarGridSpec(
            num_scalar_prefetch=1,
            grid=(row_total,),
            in_specs=[
                pl.BlockSpec((None, col_total, height, width), lambda r, s: (r, 0, 0, 0))
            ],
            out_specs=(out_block, out_block),
        ),
        cost_estimate=pl.CostEstimate(
            flops=0, transcendentals=0, bytes_accessed=4 * total.size
        ),
    )(me, blocks)
    both = add_low(keep, hop(give, COL, 1)).reshape(row_total, pairs * height, width)
    mine = xor_scatter(both, ROW).astype(jnp.bfloat16)
    return xor_scatter(mine.reshape(pairs, height, width), COL)


def stack_body(*refs):
    for i, ref in enumerate(refs[:-1]):
        refs[-1][i] = ref[...]


def stack_pieces(pieces):
    shape = (len(pieces),) + pieces[0].shape
    return pl.pallas_call(
        stack_body,
        out_shape=jax.ShapeDtypeStruct(shape, pieces[0].dtype),
        cost_estimate=pl.CostEstimate(
            flops=0, transcendentals=0, bytes_accessed=4 * math.prod(shape)
        ),
    )(*pieces)


def gather_weight(shard, pairs, row_total, direct, first=None, second=None, middle=None):
    along = direct_gather(shard if first is None else after(shard, first), COL, pairs)
    stacked = stack_pieces(along)
    if second is not None:
        stacked = after(stacked, second)
    if direct:
        mine = direct_gather(stacked, ROW, row_total)
    else:
        mine = xor_gather(stacked, ROW, row_total, middle)
    other = [hop(one, COL, 1) for one in mine]
    return (mine, other), along[-1], mine[-1]


def place_body(pairs, me_ref, own_ref, other_ref, out_ref):
    for z in range(pairs):
        out_ref[lax.bitwise_xor(me_ref[0], 2 * z)] = own_ref[z]
        out_ref[lax.bitwise_xor(me_ref[0], 2 * z + 1)] = other_ref[z]


def over_col(me, own, pairs):
    stacked = stack_pieces(direct_gather(own, COL, pairs))
    other = hop(stacked, COL, 1)
    vmem = pl.BlockSpec(memory_space=pltpu.VMEM)
    return pl.pallas_call(
        partial(place_body, pairs),
        out_shape=jax.ShapeDtypeStruct((2 * pairs,) + own.shape, own.dtype),
        in_specs=[pl.BlockSpec(memory_space=pltpu.SMEM), vmem, vmem],
    )(me, stacked, other)


def block_of(ref, index, width):
    if len(ref.shape) == 3:
        return ref.at[index]
    return ref.at[:, pl.ds(pl.multiple_of(index * width, 128), width)]


def blocked(values, count):
    rows = values.shape[0]
    width = values.shape[1] // count
    if width % 128 == 0:
        return values
    return jnp.transpose(values.reshape(rows, count, width), (1, 0, 2))


def project_body(me_ref, left_ref, *refs):
    pieces, out_ref = refs[:-1], refs[-1]
    row_total = len(pieces) // 2
    pairs, height, width = pieces[0].shape
    for z in range(pairs):
        for core in range(2):
            total = None
            for r in range(row_total):
                part = jnp.dot(
                    left_ref[:, r * height : (r + 1) * height],
                    pieces[core * row_total + r][z],
                    preferred_element_type=jnp.float32,
                )
                total = part if total is None else total + part
            out = block_of(out_ref, lax.bitwise_xor(me_ref[0], 2 * z + core), width)
            out[...] = total.astype(out_ref.dtype)


def contract_body(me_ref, left_ref, *refs):
    pieces, out_ref = refs[:-1], refs[-1]
    row_total = len(pieces) // 2
    pairs, height, width = pieces[0].shape
    for r in range(row_total):
        total = None
        for z in range(pairs):
            for core in range(2):
                block = block_of(left_ref, lax.bitwise_xor(me_ref[0], 2 * z + core), width)
                part = lax.dot_general(
                    block[...],
                    pieces[core * row_total + r][z],
                    (((1,), (1,)), ((), ())),
                    preferred_element_type=jnp.float32,
                )
                total = part if total is None else total + part
        out_ref[:, r * height : (r + 1) * height] = total


def whole_call(body, shape, dtype, flops, me, left, pieces):
    mine, other = pieces
    operands = [left, *mine, *other]
    size = sum(one.size for one in operands) * 2
    vmem = pl.BlockSpec(memory_space=pltpu.VMEM)
    return pl.pallas_call(
        body,
        out_shape=jax.ShapeDtypeStruct(shape, dtype),
        in_specs=[pl.BlockSpec(memory_space=pltpu.SMEM)] + [vmem] * len(operands),
        out_specs=vmem,
        cost_estimate=pl.CostEstimate(flops=flops, transcendentals=0, bytes_accessed=size),
    )(me, *operands)


def project(me, left, pieces):
    pairs, _, width = pieces[0][0].shape
    rows = left.shape[0]
    shape = (rows, 2 * pairs * width) if width % 128 == 0 else (2 * pairs, rows, width)
    flops = 4 * rows * left.shape[1] * pairs * width
    out = whole_call(project_body, shape, jnp.bfloat16, flops, me, left, pieces)
    if len(shape) == 3:
        out = jnp.transpose(out, (1, 0, 2)).reshape(rows, 2 * pairs * width)
    return out


def contract(me, left, pieces):
    pairs, height, _ = pieces[0][0].shape
    shape = (left.shape[0], len(pieces[0]) * height)
    flops = 2 * left.size * shape[1]
    left = blocked(left, 2 * pairs)
    return whole_call(contract_body, shape, jnp.float32, flops, me, left, pieces)


def deal_body(pairs, me_ref, columns_ref, keep_ref, give_ref):
    width = keep_ref.shape[1] // pairs
    for z in range(pairs):
        span = slice(z * width, (z + 1) * width)
        for core, out_ref in enumerate((keep_ref, give_ref)):
            index = lax.bitwise_xor(me_ref[0], 2 * z + core)
            out_ref[:, span] = block_of(columns_ref, index, width)[...]


def pair_columns(me, columns, count):
    rows, width = columns.shape
    half = jax.ShapeDtypeStruct((rows, width // 2), columns.dtype)
    values = blocked(columns, count)
    keep, give = pl.pallas_call(
        partial(deal_body, count // 2),
        out_shape=(half, half),
        in_specs=[
            pl.BlockSpec(memory_space=pltpu.SMEM),
            pl.BlockSpec(memory_space=pltpu.VMEM),
        ],
        cost_estimate=pl.CostEstimate(
            flops=0, transcendentals=0, bytes_accessed=4 * rows * width
        ),
    )(me, values)
    return jnp.concatenate([keep, hop(give, COL, 1)], axis=0)


def pair_rows(own):
    return jnp.concatenate([own, hop(own, COL, 1)], axis=0)


def attend_body(span_ref, window_ref, query_ref, key_ref, value_ref, out_ref, inverse_ref, sums, weights):
    rows = query_ref.shape[0]
    low_edge = window_ref[:, 0:1]
    high_edge = window_ref[:, 1:2]
    query = query_ref[...]
    sums[...] = jnp.zeros_like(sums)
    weights[...] = jnp.zeros_like(weights)

    def one_tile(tile, carry):
        scores = lax.dot_general(
            query, key_ref[tile], (((1,), (1,)), ((), ())), preferred_element_type=jnp.float32
        )
        place = tile * rows + lax.broadcasted_iota(jnp.int32, scores.shape, 1)
        exps = jnp.where((place >= low_edge) & (place < high_edge), jnp.exp(scores), 0.0)
        part = exps[:, :128]
        for start in range(128, rows, 128):
            part = part + exps[:, start : start + 128]
        weights[...] += part
        sums[...] += jnp.dot(
            exps.astype(jnp.bfloat16), value_ref[tile], preferred_element_type=jnp.float32
        )
        return carry

    lax.fori_loop(span_ref[0], span_ref[1], one_tile, 0)
    inverse = 1.0 / jnp.sum(weights[...], axis=1, keepdims=True)
    out_ref[...] = (sums[...] * inverse).astype(jnp.bfloat16)
    inverse_ref[...] = jnp.broadcast_to(inverse, inverse_ref.shape)


def attend(span, window, query, gathered):
    rows, width = query.shape
    tiles = gathered.shape[0]
    groups = HEADS // KV_HEADS
    half = pl.BlockSpec((rows, HEAD), lambda h, s: (0, h))
    flops = 4 * rows * rows * tiles * width
    return pl.pallas_call(
        attend_body,
        out_shape=(
            jax.ShapeDtypeStruct((rows, width), jnp.bfloat16),
            jax.ShapeDtypeStruct((rows, HEADS * 128), jnp.float32),
        ),
        grid_spec=pltpu.PrefetchScalarGridSpec(
            num_scalar_prefetch=1,
            grid=(HEADS,),
            in_specs=[
                pl.BlockSpec((rows, 2), lambda h, s: (0, 0)),
                half,
                pl.BlockSpec((tiles, None, rows, HEAD), lambda h, s: (0, 0, 0, h // groups)),
                pl.BlockSpec((tiles, None, rows, HEAD), lambda h, s: (0, 1, 0, h // groups)),
            ],
            out_specs=(half, pl.BlockSpec((rows, 128), lambda h, s: (0, h))),
            scratch_shapes=[
                pltpu.VMEM((rows, HEAD), jnp.float32),
                pltpu.VMEM((rows, 128), jnp.float32),
            ],
        ),
        cost_estimate=pl.CostEstimate(
            flops=flops, transcendentals=rows * rows * tiles * HEADS, bytes_accessed=8 * rows * width
        ),
    )(span, window, query, gathered, gathered)


def attend_back_body(
    span_ref, window_ref, query_ref, key_ref, value_ref, grad_ref, out_ref, inverse_ref,
    query_grad_ref, pair_grad_ref, query_sum, key_sum, value_sum,
):
    rows = query_ref.shape[0]
    groups = HEADS // KV_HEADS
    head = pl.program_id(0)
    low_edge = window_ref[0:1, :]
    high_edge = window_ref[1:2, :]
    query = query_ref[...]
    grad_wide = grad_ref[...].astype(jnp.float32)
    inverse = inverse_ref[:, 0:1]
    delta = jnp.sum(grad_wide * out_ref[...].astype(jnp.float32), axis=1, keepdims=True) * inverse
    delta_row = jnp.transpose(jnp.broadcast_to(delta, (rows, 128)))[0:1, :]
    grad_scaled = (grad_wide * inverse).astype(jnp.bfloat16)
    query_sum[...] = jnp.zeros_like(query_sum)

    @pl.when(lax.rem(head, groups) == 0)
    def _():
        key_sum[...] = jnp.zeros_like(key_sum)
        value_sum[...] = jnp.zeros_like(value_sum)

    def one_tile(tile, carry):
        keys = key_ref[tile]
        contract_last = (((1,), (1,)), ((), ()))
        scores = lax.dot_general(keys, query, contract_last, preferred_element_type=jnp.float32)
        place = tile * rows + lax.broadcasted_iota(jnp.int32, scores.shape, 0)
        exps = jnp.where((place >= low_edge) & (place < high_edge), jnp.exp(scores), 0.0)
        prob_grad = lax.dot_general(
            value_ref[tile], grad_scaled, contract_last, preferred_element_type=jnp.float32
        )
        score_grad = (exps * (prob_grad - delta_row)).astype(jnp.bfloat16)
        key_sum[tile] += jnp.dot(score_grad, query, preferred_element_type=jnp.float32)
        value_sum[tile] += jnp.dot(
            exps.astype(jnp.bfloat16), grad_scaled, preferred_element_type=jnp.float32
        )
        query_sum[...] += lax.dot_general(
            score_grad, keys, (((0,), (0,)), ((), ())), preferred_element_type=jnp.float32
        )
        return carry

    lax.fori_loop(span_ref[0], span_ref[1], one_tile, 0)
    query_grad_ref[...] = query_sum[...] * (1.0 / math.sqrt(HEAD))

    @pl.when(lax.rem(head, groups) == groups - 1)
    def _():
        pair_grad_ref[:, 0] = key_sum[...].astype(jnp.bfloat16)
        pair_grad_ref[:, 1] = value_sum[...].astype(jnp.bfloat16)


def attend_back(span, window, query, gathered, grad, out, inverse):
    rows, width = query.shape
    tiles = gathered.shape[0]
    groups = HEADS // KV_HEADS
    half = pl.BlockSpec((rows, HEAD), lambda h, s: (0, h))
    return pl.pallas_call(
        attend_back_body,
        out_shape=(
            jax.ShapeDtypeStruct((rows, width), jnp.float32),
            jax.ShapeDtypeStruct(gathered.shape, jnp.bfloat16),
        ),
        grid_spec=pltpu.PrefetchScalarGridSpec(
            num_scalar_prefetch=1,
            grid=(HEADS,),
            in_specs=[
                pl.BlockSpec((2, rows), lambda h, s: (0, 0)),
                half,
                pl.BlockSpec((tiles, None, rows, HEAD), lambda h, s: (0, 0, 0, h // groups)),
                pl.BlockSpec((tiles, None, rows, HEAD), lambda h, s: (0, 1, 0, h // groups)),
                half,
                half,
                pl.BlockSpec((rows, 128), lambda h, s: (0, h)),
            ],
            out_specs=(
                half,
                pl.BlockSpec((tiles, 2, rows, HEAD), lambda h, s: (0, 0, 0, h // groups)),
            ),
            scratch_shapes=[
                pltpu.VMEM((rows, HEAD), jnp.float32),
                pltpu.VMEM((tiles, rows, HEAD), jnp.float32),
                pltpu.VMEM((tiles, rows, HEAD), jnp.float32),
            ],
        ),
        cost_estimate=pl.CostEstimate(
            flops=10 * rows * rows * tiles * width,
            transcendentals=rows * rows * tiles * HEADS,
            bytes_accessed=16 * rows * width,
        ),
    )(span, window, query, gathered, gathered, grad, out, inverse)


def local(
    layer_input,
    per_layer_input,
    out_cotangent,
    seq_lengths,
    query_weight,
    key_weight,
    value_weight,
    out_weight,
    gate_weight,
    up_weight,
    down_weight,
    laurel_down,
    laurel_up,
    per_layer_gate,
    per_layer_projection,
    input_gain,
    query_gain,
    key_gain,
    attention_gain,
    laurel_gain,
    pre_feed_gain,
    post_feed_gain,
    per_layer_gain,
):
    rows, width = layer_input.shape
    row_total = lax.axis_size(ROW)
    col_total = lax.axis_size(COL)
    pairs = col_total // 2
    me_row = lax.axis_index(ROW)
    me_col = lax.axis_index(COL)
    rank = laurel_down.shape[1]
    embed = per_layer_gate.shape[1]
    kv_width = key_weight.shape[1]
    feed_width = gate_weight.shape[1]
    low = jnp.bfloat16
    wide = jnp.float32

    me = me_col.astype(jnp.int32).reshape(1)
    small_rows = laurel_down.shape[0]
    head_part = query_gain.shape[0]

    gains_own = jnp.concatenate(
        [
            input_gain,
            attention_gain,
            laurel_gain,
            pre_feed_gain,
            post_feed_gain,
            per_layer_gain,
            query_gain,
            key_gain,
        ]
    )
    gain_total = gains_own.shape[0]
    laurel_own = jnp.concatenate([laurel_down, laurel_up], axis=1)
    line = laurel_own.shape[1]
    gain_lines = -(-gain_total // line)
    gains_block = jnp.pad(gains_own, (0, gain_lines * line - gain_total)).reshape(gain_lines, line)
    first_own = jnp.concatenate(
        [laurel_own, jnp.pad(gains_block, ((0, 16 - gain_lines), (0, 0)))], axis=0
    )

    spread = jnp.broadcast_to(first_own[None], (col_total,) + first_own.shape)
    first_group = lax.all_to_all(spread, COL, 0, 0, tiled=True)
    first_all = jnp.stack(direct_gather(first_group, ROW, row_total))
    laurel_all = first_all[:, :, :small_rows].reshape(-1, line)
    laurel_down_all = laurel_all[:, :rank]
    laurel_up_all = laurel_all[:, rank:]
    gain_rows = first_all[:, :, small_rows : small_rows + gain_lines].astype(wide)
    gain_rows = gain_rows.reshape(row_total, col_total, gain_lines * line)
    gains = gain_rows[:, :, : 6 * small_rows].reshape(row_total, col_total, 6, small_rows)
    gains = jnp.transpose(gains, (2, 0, 1, 3)).reshape(6, width)
    gain_list = [gains[i] for i in range(6)]
    head_gains = []
    for i in range(2):
        start = 6 * small_rows + i * head_part
        rel = gain_rows[:, :, start : start + head_part].reshape(-1)
        head_gains.append(xor_blocks(rel, me_row, row_total))

    kv_pieces, kv_first, kv_last = gather_weight(
        jnp.concatenate([key_weight, value_weight], axis=1), pairs, row_total, True
    )
    query_pieces, _, query_last = gather_weight(
        query_weight, pairs, row_total, False, kv_first, kv_last
    )
    tokens_at = me_col * rows + jnp.arange(rows, dtype=jnp.int32)
    position, begin, reach = placement_info(seq_lengths[0], tokens_at)
    window = jnp.stack([begin, reach])
    span = jnp.stack([jnp.min(begin) // rows, (jnp.max(reach) + rows - 1) // rows])
    inputs = xor_blocks(layer_input, me_row, row_total).astype(wide)
    cotangent = xor_blocks(out_cotangent, me_row, row_total).astype(wide)
    normed, input_pull = jax.vjp(rms_scale, inputs, gain_list[0])
    normed_low = normed.astype(low)
    cosine, sine_part = angles(position)
    query_gain_row = head_gains[0].reshape(1, HEAD)
    key_gain_row = head_gains[1].reshape(1, HEAD)
    kv_own = project(me, normed_low, kv_pieces)
    pair_own = small_call(
        partial(pair_body, col_total),
        jax.ShapeDtypeStruct((2, rows, KV_HEADS * HEAD), low),
        kv_own,
        key_gain_row,
        cosine,
        sine_part,
    )
    pair_all = lax.all_gather(pair_own, COL, axis=0, tiled=True)
    pair_all = pair_all.reshape(col_total, 2, rows, KV_HEADS * HEAD)
    query_own = project(me, normed_low, query_pieces)
    query_scaled = small_call(
        partial(query_body, 1.0 / math.sqrt(HEAD)),
        jax.ShapeDtypeStruct((rows, HEADS * HEAD), low),
        query_own,
        query_gain_row,
        cosine,
        sine_part,
    )
    attended, inverse = attend(span, jnp.transpose(window), query_scaled, pair_all)
    out_pieces, _, out_last = gather_weight(
        out_weight, pairs, row_total, False, kv_first, query_last, attended
    )
    attention_out = contract(me, attended, out_pieces)
    laurel_mid = product(normed_low, laurel_down_all).astype(low)
    laurel_out = product_t(laurel_mid, laurel_up_all)
    (mixed, feed_in), mix_pull = jax.vjp(
        residual_mix,
        inputs,
        attention_out,
        normed_low.astype(wide),
        laurel_out,
        gain_list[1],
        gain_list[2],
        gain_list[3],
    )
    feed_low = feed_in.astype(low)
    feed_pieces = xor_gather(
        after(jnp.concatenate([gate_weight, up_weight], axis=1), out_last), ROW, row_total, feed_low
    )
    layer_own = jnp.concatenate([per_layer_gate, per_layer_projection], axis=1)
    feed_all = jnp.concatenate(feed_pieces, axis=0)
    halves = 2
    part_rows = rows // halves
    feed_tokens, hidden_pulls, hidden_lows, down_outs = [], [], [], []
    done = None
    for h in range(halves):
        tokens = lax.all_gather(
            feed_low[h * part_rows : (h + 1) * part_rows], COL, axis=0, tiled=True
        )
        tokens = tokens if done is None else after(tokens, done)
        gate_up = product(tokens, feed_all).astype(low)
        if h == 0:
            down_pieces = xor_gather(down_weight, ROW, row_total, feed_low)
            down_all = jnp.concatenate(down_pieces, axis=0)
        hidden, hidden_pull = jax.vjp(
            geglu, gate_up[:, :feed_width].astype(wide), gate_up[:, feed_width:].astype(wide)
        )
        hidden_low = hidden.astype(low)
        done = product_t(hidden_low, down_all).astype(low)
        down_outs.append(lax.psum_scatter(done, COL, scatter_dimension=0, tiled=True))
        feed_tokens.append(tokens)
        hidden_pulls.append(hidden_pull)
        hidden_lows.append(hidden_low)
    layer_group = over_col(me, after(layer_own, done), pairs)
    layer_pieces = direct_gather(layer_group, ROW, row_total)
    layer_all = jnp.concatenate([one.reshape(-1, 2 * embed) for one in layer_pieces], axis=0)
    layer_gate_all = layer_all[:, :embed]
    layer_proj_all = layer_all[:, embed:]
    down_out = jnp.concatenate(down_outs, axis=0).astype(wide)
    after_feed, feed_pull = jax.vjp(feed_mix, mixed, down_out, gain_list[4])
    after_low = after_feed.astype(low)
    per_pre = product(after_low, layer_gate_all)
    per_hidden, per_pull = jax.vjp(geglu, per_pre, per_layer_input.astype(wide))
    per_low = per_hidden.astype(low)
    per_out = product_t(per_low, layer_proj_all)
    output, final_pull = jax.vjp(final_mix, after_feed, per_out, gain_list[5])
    after_grad, per_out_grad, final_gain_grad = final_pull(cotangent)
    per_out_low = per_out_grad.astype(low)
    per_hidden_grad = product(per_out_low, layer_proj_all)
    layer_proj_grad = product_tn(per_out_low, per_low)
    per_pre_grad, embed_grad = per_pull(per_hidden_grad)
    per_pre_low = per_pre_grad.astype(low)
    after_grad = after_grad + product_t(per_pre_low, layer_gate_all)
    layer_gate_grad = product_tn(after_low, per_pre_low)
    mixed_grad, down_grad, post_gain_grad = feed_pull(after_grad)
    down_low = down_grad.astype(low)
    layer_grad = scatter_small(
        me,
        after(jnp.concatenate([layer_gate_grad, layer_proj_grad], axis=1).astype(low), down_low),
        row_total,
        col_total,
    )
    attended_pair = pair_columns(me, after(attended, down_low), col_total)
    normed_pair = pair_rows(after(normed_low, down_low))
    feed_in_grads = []
    done = None
    for h in range(halves):
        tokens = lax.all_gather(
            down_low[h * part_rows : (h + 1) * part_rows], COL, axis=0, tiled=True
        )
        if done is None:
            tokens, layer_grad, attended_pair, normed_pair = lax.optimization_barrier(
                (tokens, layer_grad, attended_pair, normed_pair)
            )
        else:
            tokens = after(tokens, done, down_first, *feed_first)
        hidden_grad = product(tokens, down_all)
        gate_grad, up_grad = hidden_pulls[h](hidden_grad)
        feed_grad_low = jnp.concatenate([gate_grad.astype(low), up_grad.astype(low)], axis=1)
        done = product_t(feed_grad_low, feed_all).astype(low)
        feed_in_grads.append(lax.psum_scatter(done, COL, scatter_dimension=0, tiled=True))
        if h == 0:
            down_first = product_tn(after(tokens, done), hidden_lows[0]).astype(low)
            feed_first = [
                product_tn(after(feed_tokens[0], down_first), one.astype(low)).astype(low)
                for one in (gate_grad, up_grad)
            ]
    feed_in_grad = jnp.concatenate(feed_in_grads, axis=0).astype(wide)
    down_total = product_tn(after(tokens, done), hidden_lows[1]) + down_first.astype(wide)
    down_total = down_total.astype(low)
    gate_total = product_tn(after(feed_tokens[1], down_total), gate_grad.astype(low))
    gate_total = (gate_total + feed_first[0].astype(wide)).astype(low)
    up_total = product_tn(after(feed_tokens[1], gate_total), up_grad.astype(low))
    up_total = (up_total + feed_first[1].astype(wide)).astype(low)
    (
        inputs_grad,
        attention_grad,
        normed_grad,
        laurel_out_grad,
        attention_gain_grad,
        laurel_gain_grad,
        pre_gain_grad,
    ) = mix_pull((mixed_grad, feed_in_grad))
    attention_low = attention_grad.astype(low)
    attended_grad = project(me, attention_low, out_pieces)
    query_rot_grad, pair_parts = attend_back(
        span, window, query_scaled, pair_all, attended_grad, attended, inverse
    )
    pair_sum = lax.psum_scatter(
        pair_parts.reshape(2 * col_total, rows, KV_HEADS * HEAD),
        COL,
        scatter_dimension=0,
        tiled=True,
    )
    attention_pair = pair_rows(attention_low)
    out_total = product_tn(after(attention_pair, pair_parts), attended_pair).astype(low)
    query_rot_grad = after(query_rot_grad, out_total)
    gain_row = jax.ShapeDtypeStruct((1, HEAD), wide)
    query_low, query_gain_grad = small_call(
        query_back_body,
        (jax.ShapeDtypeStruct((rows, HEADS * HEAD), low), gain_row),
        query_own,
        query_rot_grad,
        query_gain_row,
        cosine,
        sine_part,
    )
    query_total = product_tn(
        after(normed_pair, out_total), pair_columns(me, query_low, col_total)
    ).astype(low)
    query_part = contract(me, after(query_low, query_total), query_pieces)

    laurel_out_low = after(laurel_out_grad.astype(low), query_total)
    laurel_mid_grad = product(laurel_out_low, laurel_up_all)
    laurel_up_grad = product_tn(laurel_out_low, laurel_mid)
    laurel_mid_low = laurel_mid_grad.astype(low)
    laurel_down_grad = product_tn(normed_low, laurel_mid_low)
    small_total = jnp.concatenate([laurel_down_grad, laurel_up_grad], axis=1)
    normed_grad = normed_grad + product_t(laurel_mid_low, laurel_down_all) + query_part
    pair_sum = after(pair_sum, normed_grad, small_total)
    kv_grad, key_gain_grad = small_call(
        partial(pair_back_body, col_total),
        (jax.ShapeDtypeStruct(kv_own.shape, low), gain_row),
        kv_own,
        pair_sum,
        key_gain_row,
        cosine,
        sine_part,
    )
    kv_total = product_tn(normed_pair, pair_columns(me, kv_grad, col_total)).astype(low)
    marks = []
    normed_grad = normed_grad + contract(me, after(kv_grad, kv_total), kv_pieces)
    kv_weight_grad = scatter_cols(kv_total, row_total, pairs, normed_grad, None, marks)
    mark = marks[0]
    query_marks = []
    query_weight_grad = scatter_cols(query_total, row_total, pairs, mark, mark, query_marks)
    out_weight_grad = scatter_cols(out_total, row_total, pairs, query_part, normed_grad)
    down_weight_grad = scatter_rows(down_total, row_total, up_total, query_marks[0])
    gate_weight_grad = scatter_rows(gate_total, row_total, up_total, marks[-1])
    up_weight_grad = scatter_rows(up_total, row_total, pair_parts, marks[-1])
    input_part, input_gain_grad = input_pull(after(normed_grad, mark))
    input_total = xor_blocks((inputs_grad + input_part).astype(low), me_row, row_total)

    wide_gains = jnp.stack(
        [
            input_gain_grad,
            attention_gain_grad,
            laurel_gain_grad,
            pre_gain_grad,
            post_gain_grad,
            final_gain_grad,
        ]
    ).reshape(6, row_total, col_total, small_rows)
    wide_gains = jnp.transpose(wide_gains, (1, 2, 0, 3)).reshape(row_total, col_total, -1)
    both_gains = jnp.concatenate([query_gain_grad, key_gain_grad], axis=0)
    both_gains = xor_blocks(both_gains, me_row, row_total)
    both_gains = both_gains.reshape(2, row_total, col_total, head_part)
    both_gains = jnp.transpose(both_gains, (1, 2, 0, 3)).reshape(row_total, col_total, -1)
    gain_sums = jnp.concatenate([wide_gains, both_gains], axis=2)
    gain_sums = jnp.pad(gain_sums, ((0, 0), (0, 0), (0, gain_lines * line - gain_total)))
    gain_sums = gain_sums.reshape(row_total, col_total, gain_lines, line)
    laurel_parts = small_total.reshape(row_total, col_total, small_rows, line)
    sums = after(jnp.concatenate([laurel_parts, gain_sums], axis=2), query_marks[0])
    sums = sums[0] + sum(hop(sums[j], ROW, j) for j in range(1, row_total))
    sums = lax.all_to_all(sums, COL, 0, 0, tiled=True)
    sums = jnp.sum(after(sums, query_marks[-1]), axis=0)
    laurel_grad = sums[:small_rows]
    gain_sums = sums[small_rows:].reshape(-1)
    gain_out = [gain_sums[i * small_rows : (i + 1) * small_rows] for i in range(6)]
    head_out = gain_sums[6 * small_rows : gain_total]
    return (
        xor_blocks(output.astype(low), me_row, row_total),
        input_total,
        embed_grad.astype(low),
        query_weight_grad,
        kv_weight_grad[:, :kv_width],
        kv_weight_grad[:, kv_width:],
        out_weight_grad,
        gate_weight_grad,
        up_weight_grad,
        down_weight_grad,
        laurel_grad[:, :rank],
        laurel_grad[:, rank:],
        layer_grad[:, :embed],
        layer_grad[:, embed:],
        gain_out[0],
        head_out[:head_part],
        head_out[head_part:],
        gain_out[1],
        gain_out[2],
        gain_out[3],
        gain_out[4],
        gain_out[5],
    )


def solution(mesh):
    in_specs = (
        P((ROW, COL), None),
        P((ROW, COL), None),
        P((ROW, COL), None),
        P(ROW, None),
        P(ROW, COL),
        P(ROW, COL),
        P(ROW, COL),
        P(ROW, COL),
        P(ROW, COL),
        P(ROW, COL),
        P(ROW, COL),
        P((ROW, COL), None),
        P((ROW, COL), None),
        P((ROW, COL), None),
        P((ROW, COL), None),
        P((ROW, COL)),
        P((ROW, COL)),
        P((ROW, COL)),
        P((ROW, COL)),
        P((ROW, COL)),
        P((ROW, COL)),
        P((ROW, COL)),
        P((ROW, COL)),
    )
    out_specs = (
        P((ROW, COL), None),
        P((ROW, COL), None),
        P((ROW, COL), None),
        P(ROW, COL),
        P(ROW, COL),
        P(ROW, COL),
        P(ROW, COL),
        P(ROW, COL),
        P(ROW, COL),
        P(ROW, COL),
        P((ROW, COL), None),
        P((ROW, COL), None),
        P((ROW, COL), None),
        P((ROW, COL), None),
        P((ROW, COL)),
        P((ROW, COL)),
        P((ROW, COL)),
        P((ROW, COL)),
        P((ROW, COL)),
        P((ROW, COL)),
        P((ROW, COL)),
        P((ROW, COL)),
    )

    return jax.shard_map(local, mesh=mesh, in_specs=in_specs, out_specs=out_specs, check_vma=False)
```

```python
from functools import partial
import math

import jax
import jax.numpy as jnp
from jax import lax
from jax.experimental import pallas as pl
from jax.experimental.pallas import tpu as pltpu
from jax.sharding import PartitionSpec as P


HEADS = 8
KV_HEADS = 2
HEAD = 256
BLOCK = 256
ROW = "row"
COL = "col"


NORM_EPS = 1e-06
ROOT_HALF = 0.7071067811865476
ROPE_THETA = 1000000.0


def rms_scale(values, scale_gain):
    return (
        values
        * lax.rsqrt(jnp.mean(values * values, axis=-1, keepdims=True) + NORM_EPS)
        * scale_gain
    )


def angles(position):
    half_width = HEAD // 2
    steps_up = jnp.arange(half_width, dtype=jnp.float32)
    frequency = jnp.exp(steps_up * (-2.0 * math.log(ROPE_THETA) / HEAD))
    angle_grid = position.astype(jnp.float32)[:, None] * frequency[None, :]
    return (jnp.cos(angle_grid), jnp.sin(angle_grid))


def turn(values, cosine, sine_part):
    half_width = HEAD // 2
    first_half = values[:, :half_width]
    second_half = values[:, half_width:]
    return jnp.concatenate(
        [
            first_half * cosine - second_half * sine_part,
            second_half * cosine + first_half * sine_part,
        ],
        axis=1,
    )


def inverse_rms(values):
    return lax.rsqrt(jnp.mean(values * values, axis=1, keepdims=True) + NORM_EPS)


def norm_back(values, inverse, grad):
    return inverse * (
        grad - values * (inverse * inverse * jnp.mean(grad * values, axis=1, keepdims=True))
    )


def query_body(scale, query_ref, gain_ref, cosine_ref, sine_ref, out_ref):
    for head in range(query_ref.shape[1] // HEAD):
        span = slice(head * HEAD, (head + 1) * HEAD)
        values = query_ref[:, span].astype(jnp.float32)
        normed = values * inverse_rms(values) * gain_ref[...]
        turned = turn(normed, cosine_ref[...], sine_ref[...]).astype(jnp.bfloat16)
        out_ref[:, span] = turned * jnp.bfloat16(scale)


def query_back_body(query_ref, grad_ref, gain_ref, cosine_ref, sine_ref, out_ref, gain_grad_ref):
    total = jnp.zeros((1, HEAD), jnp.float32)
    for head in range(query_ref.shape[1] // HEAD):
        span = slice(head * HEAD, (head + 1) * HEAD)
        values = query_ref[:, span].astype(jnp.float32)
        inverse = inverse_rms(values)
        grad = turn(grad_ref[:, span], cosine_ref[...], -sine_ref[...])
        total = total + jnp.sum(grad * values * inverse, axis=0, keepdims=True)
        out_ref[:, span] = norm_back(values, inverse, grad * gain_ref[...]).astype(jnp.bfloat16)
    gain_grad_ref[...] = total


def head_of(columns, head, kind, count):
    width = columns.shape[1] // count // 2
    per_head = HEAD // width
    parts = [
        columns[:, (2 * c + kind) * width : (2 * c + kind + 1) * width]
        for c in range(head * per_head, (head + 1) * per_head)
    ]
    return jnp.concatenate(parts, axis=1)


def pair_body(count, columns_ref, gain_ref, cosine_ref, sine_ref, out_ref):
    columns = columns_ref[...].astype(jnp.float32)
    for head in range(KV_HEADS):
        span = slice(head * HEAD, (head + 1) * HEAD)
        keys = head_of(columns, head, 0, count)
        normed = keys * inverse_rms(keys) * gain_ref[...]
        out_ref[0, :, span] = turn(normed, cosine_ref[...], sine_ref[...]).astype(jnp.bfloat16)
        values = head_of(columns, head, 1, count)
        out_ref[1, :, span] = (values * inverse_rms(values)).astype(jnp.bfloat16)


def pair_back_body(
    count, columns_ref, grad_ref, gain_ref, cosine_ref, sine_ref, out_ref, gain_grad_ref
):
    columns = columns_ref[...].astype(jnp.float32)
    width = columns.shape[1] // count // 2
    total = jnp.zeros((1, HEAD), jnp.float32)
    pieces = []
    for head in range(KV_HEADS):
        span = slice(head * HEAD, (head + 1) * HEAD)
        keys = head_of(columns, head, 0, count)
        inverse = inverse_rms(keys)
        grad = grad_ref[0, :, span].astype(jnp.float32)
        grad = turn(grad, cosine_ref[...], -sine_ref[...])
        total = total + jnp.sum(grad * keys * inverse, axis=0, keepdims=True)
        key_grad = norm_back(keys, inverse, grad * gain_ref[...])
        values = head_of(columns, head, 1, count)
        value_grad = norm_back(
            values, inverse_rms(values), grad_ref[1, :, span].astype(jnp.float32)
        )
        for c in range(HEAD // width):
            pieces.append(key_grad[:, c * width : (c + 1) * width])
            pieces.append(value_grad[:, c * width : (c + 1) * width])
    out_ref[...] = jnp.concatenate(pieces, axis=1).astype(jnp.bfloat16)
    gain_grad_ref[...] = total


def small_call(body, shapes, *operands):
    size = 4 * sum(one.size for one in operands)
    return pl.pallas_call(
        body,
        out_shape=shapes,
        cost_estimate=pl.CostEstimate(flops=4 * size, transcendentals=0, bytes_accessed=size),
    )(*operands)


def placement_info(lengths, tokens_at):
    finish = jnp.cumsum(lengths)
    begins = finish - lengths
    segment = jnp.sum((tokens_at[:, None] >= finish[None, :]).astype(jnp.int32), axis=1)
    chosen = segment[:, None] == jnp.arange(lengths.shape[0], dtype=jnp.int32)[None, :]
    begin = jnp.sum(jnp.where(chosen, begins[None, :], 0), axis=1)
    end = jnp.sum(jnp.where(chosen, finish[None, :], 0), axis=1)
    position = tokens_at - begin
    reach = jnp.minimum(end, begin + (position // BLOCK + 1) * BLOCK)
    return (position, begin, reach)


def geglu(gate_in, up_in):
    return jax.nn.gelu(gate_in, approximate=True) * up_in


def residual_mix(inputs, attention_out, normed, laurel_out, attention_gain, laurel_gain, pre_gain):
    mixed = (
        inputs
        + rms_scale(attention_out, attention_gain)
        + normed
        + rms_scale(laurel_out, laurel_gain)
    ) * ROOT_HALF
    return (mixed, rms_scale(mixed, pre_gain))


def feed_mix(mixed, down_out, post_gain):
    return mixed + rms_scale(down_out, post_gain)


def final_mix(after_feed, per_out, final_gain):
    return after_feed + rms_scale(per_out, final_gain)


def product(left, right):
    return jnp.dot(left, right, preferred_element_type=jnp.float32)


def product_t(left, right):
    return lax.dot_general(
        left, right, (((1,), (1,)), ((), ())), preferred_element_type=jnp.float32
    )


def product_tn(left, right):
    return lax.dot_general(
        left, right, (((0,), (0,)), ((), ())), preferred_element_type=jnp.float32
    )


def hop(values, axis, mask):
    size = lax.axis_size(axis)
    return lax.ppermute(values, axis, [(i, i ^ mask) for i in range(size)])


def split_hop(values, even_mask, odd_mask):
    size = lax.axis_size(ROW) * lax.axis_size(COL)
    pairs = [(i, i ^ (odd_mask if i % 2 else even_mask)) for i in range(size)]
    return lax.ppermute(values, (ROW, COL), pairs)


def after(values, *others):
    return lax.optimization_barrier((values,) + others)[0]


def xor_blocks(values, me, count):
    width = values.shape[-1] // count
    blocks = [values[..., i * width : (i + 1) * width] for i in range(count)]
    bit = 1
    while bit < count:
        flip = (me & bit) != 0
        blocks = [jnp.where(flip, blocks[i ^ bit], blocks[i]) for i in range(count)]
        bit *= 2
    return jnp.concatenate(blocks, axis=-1)


def unit_of(axis):
    return lax.axis_size(COL) if axis == ROW else 2


def direct_gather(piece, axis, count):
    unit = 1 if axis == ROW else 2
    return [piece] + [hop(piece, axis, j * unit) for j in range(1, count)]


def xor_gather(piece, axis, count, middle=None):
    unit = 1 if axis == ROW else 2
    if count == 4:
        near = hop(piece, axis, unit)
        far = hop(piece, axis, 2 * unit)
        odd = lax.axis_index(COL) % 2 == 1
        flat = unit_of(axis)
        chosen_far, chosen_near = far, near
        if middle is not None:
            chosen_far, chosen_near = after(far, middle), after(near, middle)
        across = split_hop(jnp.where(odd, chosen_far, chosen_near), 2 * flat, flat)
        return [piece, near, far, across]
    pieces = [piece]
    bit = 1
    while bit < count:
        pieces = pieces + [hop(one, axis, bit * unit) for one in pieces]
        bit *= 2
    return pieces


def add_low(left, right):
    return (left.astype(jnp.float32) + right.astype(jnp.float32)).astype(jnp.bfloat16)


def xor_scatter(parts, axis, late=None, last=None, marks=None):
    count = parts.shape[0]
    unit = 1 if axis == ROW else 2
    if marks is not None and count != 4:
        marks.append(parts[0])
    if count == 4:
        odd = lax.axis_index(COL) % 2 == 1
        flat = unit_of(axis)
        across = split_hop(parts[3], 2 * flat, flat)
        early = split_hop(jnp.where(odd, parts[1], parts[2]), 2 * flat, flat)
        if late is not None:
            across = after(across, late)
        rest = add_low(jnp.where(odd, parts[2], parts[1]), across)
        if marks is not None:
            marks.append(rest)
        rest = split_hop(rest, flat, 2 * flat)
        if last is not None:
            rest = after(rest, last)
            early = after(early, last)
        return parts[0].astype(jnp.float32) + early.astype(jnp.float32) + rest.astype(jnp.float32)
    parts = [parts[j] for j in range(count)]
    bit = count // 2
    while bit > 0:
        parts = [add_low(parts[j], hop(parts[j + bit], axis, bit * unit)) for j in range(bit)]
        bit //= 2
    return parts[0].astype(jnp.float32)


def scatter_rows(total, row_total, late=None, last=None, marks=None):
    parts = total.reshape(row_total, -1, total.shape[1])
    return xor_scatter(parts, ROW, late, last, marks)


def scatter_cols(total, row_total, pairs, late=None, last=None, marks=None):
    mine = scatter_rows(total, row_total, late, last, marks).astype(jnp.bfloat16)
    width = mine.shape[1] // pairs
    parts = jnp.stack([mine[:, z * width : (z + 1) * width] for z in range(pairs)])
    return xor_scatter(parts, COL, None, None, marks)


def deal_rows_body(pairs, me_ref, block_ref, keep_ref, give_ref):
    for z in range(pairs):
        keep_ref[z] = block_ref[lax.bitwise_xor(me_ref[0], 2 * z)]
        give_ref[z] = block_ref[lax.bitwise_xor(me_ref[0], 2 * z + 1)]


def scatter_small(me, total, row_total, col_total):
    pairs = col_total // 2
    width = total.shape[1]
    blocks = total.reshape(row_total, col_total, -1, width)
    height = blocks.shape[2]
    half = jax.ShapeDtypeStruct((row_total, pairs, height, width), total.dtype)
    out_block = pl.BlockSpec((None, pairs, height, width), lambda r, s: (r, 0, 0, 0))
    deal = pl.pallas_call(
        partial(deal_rows_body, pairs),
        out_shape=(half, half),
        grid_spec=pltpu.PrefetchScalarGridSpec(
            num_scalar_prefetch=1,
            grid=(row_total,),
            in_specs=[
                pl.BlockSpec((None, col_total, height, width), lambda r, s: (r, 0, 0, 0))
            ],
            out_specs=(out_block, out_block),
        ),
        cost_estimate=pl.CostEstimate(
            flops=0, transcendentals=0, bytes_accessed=4 * total.size
        ),
    )
    keep, give = deal(me, blocks)
    both = add_low(keep, hop(give, COL, 1)).reshape(row_total, pairs * height, width)
    mine = xor_scatter(both, ROW).astype(jnp.bfloat16)
    return xor_scatter(mine.reshape(pairs, height, width), COL)


def stack_body(*refs):
    for i, ref in enumerate(refs[:-1]):
        refs[-1][i] = ref[...]


def stack_pieces(pieces):
    shape = (len(pieces),) + pieces[0].shape
    return pl.pallas_call(
        stack_body,
        out_shape=jax.ShapeDtypeStruct(shape, pieces[0].dtype),
        cost_estimate=pl.CostEstimate(
            flops=0, transcendentals=0, bytes_accessed=4 * math.prod(shape)
        ),
    )(*pieces)


def gather_weight(shard, pairs, row_total, direct, first=None, second=None, middle=None):
    along = direct_gather(shard if first is None else after(shard, first), COL, pairs)
    stacked = stack_pieces(along)
    if second is not None:
        stacked = after(stacked, second)
    if direct:
        mine = direct_gather(stacked, ROW, row_total)
    else:
        mine = xor_gather(stacked, ROW, row_total, middle)
    other = [hop(one, COL, 1) for one in mine]
    return (mine, other), along[-1], mine[-1]


def place_body(pairs, me_ref, own_ref, other_ref, out_ref):
    for z in range(pairs):
        out_ref[lax.bitwise_xor(me_ref[0], 2 * z)] = own_ref[z]
        out_ref[lax.bitwise_xor(me_ref[0], 2 * z + 1)] = other_ref[z]


def over_col(me, own, pairs):
    stacked = stack_pieces(direct_gather(own, COL, pairs))
    other = hop(stacked, COL, 1)
    vmem = pl.BlockSpec(memory_space=pltpu.VMEM)
    return pl.pallas_call(
        partial(place_body, pairs),
        out_shape=jax.ShapeDtypeStruct((2 * pairs,) + own.shape, own.dtype),
        in_specs=[pl.BlockSpec(memory_space=pltpu.SMEM), vmem, vmem],
    )(me, stacked, other)


def join_body(me_ref, own_ref, other_ref, out_ref):
    parity = lax.bitwise_and(me_ref[0], 1)
    out_ref[parity] = own_ref[...]
    out_ref[1 - parity] = other_ref[...]


def join_pair(me, pieces, j, dones):
    piece = pieces[j]
    rows, width = piece.shape
    if j > 1 and j == len(pieces) - 1:
        piece = after(piece, dones[j - 2])
    other = hop(piece, COL, 1)
    if j > 0:
        other = after(other, dones[j - 1])
    vmem = pl.BlockSpec(memory_space=pltpu.VMEM)
    both = pl.pallas_call(
        join_body,
        out_shape=jax.ShapeDtypeStruct((2, rows, width), piece.dtype),
        in_specs=[pl.BlockSpec(memory_space=pltpu.SMEM), vmem, vmem],
        out_specs=vmem,
        cost_estimate=pl.CostEstimate(flops=0, transcendentals=0, bytes_accessed=8 * rows * width),
    )(me, piece, other)
    return both.reshape(2 * rows, width)


def block_of(ref, index, width):
    if len(ref.shape) == 3:
        return ref.at[index]
    return ref.at[:, pl.ds(pl.multiple_of(index * width, 128), width)]


def blocked(values, count):
    rows = values.shape[0]
    width = values.shape[1] // count
    if width % 128 == 0:
        return values
    return jnp.transpose(values.reshape(rows, count, width), (1, 0, 2))


def project_body(me_ref, left_ref, *refs):
    pieces, out_ref = refs[:-1], refs[-1]
    row_total = len(pieces) // 2
    pairs, height, width = pieces[0].shape
    for z in range(pairs):
        for core in range(2):
            total = None
            for r in range(row_total):
                part = jnp.dot(
                    left_ref[:, r * height : (r + 1) * height],
                    pieces[core * row_total + r][z],
                    preferred_element_type=jnp.float32,
                )
                total = part if total is None else total + part
            out = block_of(out_ref, lax.bitwise_xor(me_ref[0], 2 * z + core), width)
            out[...] = total.astype(out_ref.dtype)


def contract_body(me_ref, left_ref, *refs):
    pieces, out_ref = refs[:-1], refs[-1]
    row_total = len(pieces) // 2
    pairs, height, width = pieces[0].shape
    for r in range(row_total):
        total = None
        for z in range(pairs):
            for core in range(2):
                block = block_of(left_ref, lax.bitwise_xor(me_ref[0], 2 * z + core), width)
                part = lax.dot_general(
                    block[...],
                    pieces[core * row_total + r][z],
                    (((1,), (1,)), ((), ())),
                    preferred_element_type=jnp.float32,
                )
                total = part if total is None else total + part
        out_ref[:, r * height : (r + 1) * height] = total


def whole_call(body, shape, dtype, flops, me, left, pieces):
    mine, other = pieces
    operands = [left, *mine, *other]
    size = sum(one.size for one in operands) * 2
    vmem = pl.BlockSpec(memory_space=pltpu.VMEM)
    return pl.pallas_call(
        body,
        out_shape=jax.ShapeDtypeStruct(shape, dtype),
        in_specs=[pl.BlockSpec(memory_space=pltpu.SMEM)] + [vmem] * len(operands),
        out_specs=vmem,
        cost_estimate=pl.CostEstimate(flops=flops, transcendentals=0, bytes_accessed=size),
    )(me, *operands)


def project(me, left, pieces):
    pairs, _, width = pieces[0][0].shape
    rows = left.shape[0]
    shape = (rows, 2 * pairs * width) if width % 128 == 0 else (2 * pairs, rows, width)
    flops = 4 * rows * left.shape[1] * pairs * width
    out = whole_call(project_body, shape, jnp.bfloat16, flops, me, left, pieces)
    if len(shape) == 3:
        out = jnp.transpose(out, (1, 0, 2)).reshape(rows, 2 * pairs * width)
    return out


def contract(me, left, pieces):
    pairs, height, _ = pieces[0][0].shape
    shape = (left.shape[0], len(pieces[0]) * height)
    flops = 2 * left.size * shape[1]
    left = blocked(left, 2 * pairs)
    return whole_call(contract_body, shape, jnp.float32, flops, me, left, pieces)


def deal_body(pairs, me_ref, columns_ref, keep_ref, give_ref):
    width = keep_ref.shape[1] // pairs
    for z in range(pairs):
        span = slice(z * width, (z + 1) * width)
        for core, out_ref in enumerate((keep_ref, give_ref)):
            index = lax.bitwise_xor(me_ref[0], 2 * z + core)
            out_ref[:, span] = block_of(columns_ref, index, width)[...]


def pair_columns(me, columns, count):
    rows, width = columns.shape
    half = jax.ShapeDtypeStruct((rows, width // 2), columns.dtype)
    values = blocked(columns, count)
    keep, give = pl.pallas_call(
        partial(deal_body, count // 2),
        out_shape=(half, half),
        in_specs=[
            pl.BlockSpec(memory_space=pltpu.SMEM),
            pl.BlockSpec(memory_space=pltpu.VMEM),
        ],
        cost_estimate=pl.CostEstimate(
            flops=0, transcendentals=0, bytes_accessed=4 * rows * width
        ),
    )(me, values)
    return jnp.concatenate([keep, hop(give, COL, 1)], axis=0)


def pair_rows(own):
    return jnp.concatenate([own, hop(own, COL, 1)], axis=0)


def attend_body(span_ref, window_ref, query_ref, key_ref, value_ref, out_ref, inverse_ref, sums, weights):
    rows = query_ref.shape[0]
    low_edge = window_ref[:, 0:1]
    high_edge = window_ref[:, 1:2]
    query = query_ref[...]
    sums[...] = jnp.zeros_like(sums)
    weights[...] = jnp.zeros_like(weights)

    def one_tile(tile, carry):
        scores = lax.dot_general(
            query, key_ref[tile], (((1,), (1,)), ((), ())), preferred_element_type=jnp.float32
        )
        place = tile * rows + lax.broadcasted_iota(jnp.int32, scores.shape, 1)
        exps = jnp.where((place >= low_edge) & (place < high_edge), jnp.exp(scores), 0.0)
        part = exps[:, :128]
        for start in range(128, rows, 128):
            part = part + exps[:, start : start + 128]
        weights[...] += part
        sums[...] += jnp.dot(
            exps.astype(jnp.bfloat16), value_ref[tile], preferred_element_type=jnp.float32
        )
        return carry

    lax.fori_loop(span_ref[0], span_ref[1], one_tile, 0)
    inverse = 1.0 / jnp.sum(weights[...], axis=1, keepdims=True)
    out_ref[...] = (sums[...] * inverse).astype(jnp.bfloat16)
    inverse_ref[...] = jnp.broadcast_to(inverse, inverse_ref.shape)


def attend(span, window, query, gathered):
    rows, width = query.shape
    tiles = gathered.shape[0]
    groups = HEADS // KV_HEADS
    half = pl.BlockSpec((rows, HEAD), lambda h, s: (0, h))
    flops = 4 * rows * rows * tiles * width
    return pl.pallas_call(
        attend_body,
        out_shape=(
            jax.ShapeDtypeStruct((rows, width), jnp.bfloat16),
            jax.ShapeDtypeStruct((rows, HEADS * 128), jnp.float32),
        ),
        grid_spec=pltpu.PrefetchScalarGridSpec(
            num_scalar_prefetch=1,
            grid=(HEADS,),
            in_specs=[
                pl.BlockSpec((rows, 2), lambda h, s: (0, 0)),
                half,
                pl.BlockSpec((tiles, None, rows, HEAD), lambda h, s: (0, 0, 0, h // groups)),
                pl.BlockSpec((tiles, None, rows, HEAD), lambda h, s: (0, 1, 0, h // groups)),
            ],
            out_specs=(half, pl.BlockSpec((rows, 128), lambda h, s: (0, h))),
            scratch_shapes=[
                pltpu.VMEM((rows, HEAD), jnp.float32),
                pltpu.VMEM((rows, 128), jnp.float32),
            ],
        ),
        cost_estimate=pl.CostEstimate(
            flops=flops, transcendentals=rows * rows * tiles * HEADS, bytes_accessed=8 * rows * width
        ),
    )(span, window, query, gathered, gathered)


def attend_back_body(
    span_ref, window_ref, query_ref, key_ref, value_ref, grad_ref, out_ref, inverse_ref,
    query_grad_ref, pair_grad_ref, query_sum, key_sum, value_sum,
):
    rows = query_ref.shape[0]
    groups = HEADS // KV_HEADS
    head = pl.program_id(0)
    low_edge = window_ref[0:1, :]
    high_edge = window_ref[1:2, :]
    query = query_ref[...]
    grad_wide = grad_ref[...].astype(jnp.float32)
    inverse = inverse_ref[:, 0:1]
    delta = jnp.sum(grad_wide * out_ref[...].astype(jnp.float32), axis=1, keepdims=True) * inverse
    delta_row = jnp.transpose(jnp.broadcast_to(delta, (rows, 128)))[0:1, :]
    grad_scaled = (grad_wide * inverse).astype(jnp.bfloat16)
    query_sum[...] = jnp.zeros_like(query_sum)

    @pl.when(lax.rem(head, groups) == 0)
    def _():
        key_sum[...] = jnp.zeros_like(key_sum)
        value_sum[...] = jnp.zeros_like(value_sum)

    def one_tile(tile, carry):
        keys = key_ref[tile]
        contract_last = (((1,), (1,)), ((), ()))
        scores = lax.dot_general(keys, query, contract_last, preferred_element_type=jnp.float32)
        place = tile * rows + lax.broadcasted_iota(jnp.int32, scores.shape, 0)
        exps = jnp.where((place >= low_edge) & (place < high_edge), jnp.exp(scores), 0.0)
        prob_grad = lax.dot_general(
            value_ref[tile], grad_scaled, contract_last, preferred_element_type=jnp.float32
        )
        score_grad = (exps * (prob_grad - delta_row)).astype(jnp.bfloat16)
        key_sum[tile] += jnp.dot(score_grad, query, preferred_element_type=jnp.float32)
        value_sum[tile] += jnp.dot(
            exps.astype(jnp.bfloat16), grad_scaled, preferred_element_type=jnp.float32
        )
        query_sum[...] += lax.dot_general(
            score_grad, keys, (((0,), (0,)), ((), ())), preferred_element_type=jnp.float32
        )
        return carry

    lax.fori_loop(span_ref[0], span_ref[1], one_tile, 0)
    query_grad_ref[...] = query_sum[...] * (1.0 / math.sqrt(HEAD))

    @pl.when(lax.rem(head, groups) == groups - 1)
    def _():
        pair_grad_ref[:, 0] = key_sum[...].astype(jnp.bfloat16)
        pair_grad_ref[:, 1] = value_sum[...].astype(jnp.bfloat16)


def attend_back(span, window, query, gathered, grad, out, inverse):
    rows, width = query.shape
    tiles = gathered.shape[0]
    groups = HEADS // KV_HEADS
    half = pl.BlockSpec((rows, HEAD), lambda h, s: (0, h))
    return pl.pallas_call(
        attend_back_body,
        out_shape=(
            jax.ShapeDtypeStruct((rows, width), jnp.float32),
            jax.ShapeDtypeStruct(gathered.shape, jnp.bfloat16),
        ),
        grid_spec=pltpu.PrefetchScalarGridSpec(
            num_scalar_prefetch=1,
            grid=(HEADS,),
            in_specs=[
                pl.BlockSpec((2, rows), lambda h, s: (0, 0)),
                half,
                pl.BlockSpec((tiles, None, rows, HEAD), lambda h, s: (0, 0, 0, h // groups)),
                pl.BlockSpec((tiles, None, rows, HEAD), lambda h, s: (0, 1, 0, h // groups)),
                half,
                half,
                pl.BlockSpec((rows, 128), lambda h, s: (0, h)),
            ],
            out_specs=(
                half,
                pl.BlockSpec((tiles, 2, rows, HEAD), lambda h, s: (0, 0, 0, h // groups)),
            ),
            scratch_shapes=[
                pltpu.VMEM((rows, HEAD), jnp.float32),
                pltpu.VMEM((tiles, rows, HEAD), jnp.float32),
                pltpu.VMEM((tiles, rows, HEAD), jnp.float32),
            ],
        ),
        cost_estimate=pl.CostEstimate(
            flops=10 * rows * rows * tiles * width,
            transcendentals=rows * rows * tiles * HEADS,
            bytes_accessed=16 * rows * width,
        ),
    )(span, window, query, gathered, gathered, grad, out, inverse)


def local(
    layer_input,
    per_layer_input,
    out_cotangent,
    seq_lengths,
    query_weight,
    key_weight,
    value_weight,
    out_weight,
    gate_weight,
    up_weight,
    down_weight,
    laurel_down,
    laurel_up,
    per_layer_gate,
    per_layer_projection,
    input_gain,
    query_gain,
    key_gain,
    attention_gain,
    laurel_gain,
    pre_feed_gain,
    post_feed_gain,
    per_layer_gain,
):
    rows, width = layer_input.shape
    row_total = lax.axis_size(ROW)
    col_total = lax.axis_size(COL)
    pairs = col_total // 2
    me_row = lax.axis_index(ROW)
    me_col = lax.axis_index(COL)
    rank = laurel_down.shape[1]
    embed = per_layer_gate.shape[1]
    kv_width = key_weight.shape[1]
    feed_width = gate_weight.shape[1]
    low = jnp.bfloat16
    wide = jnp.float32

    me = me_col.astype(jnp.int32).reshape(1)
    small_rows = laurel_down.shape[0]
    head_part = query_gain.shape[0]

    gains_own = jnp.concatenate(
        [
            input_gain,
            attention_gain,
            laurel_gain,
            pre_feed_gain,
            post_feed_gain,
            per_layer_gain,
            query_gain,
            key_gain,
        ]
    )
    gain_total = gains_own.shape[0]
    laurel_own = jnp.concatenate([laurel_down, laurel_up], axis=1)
    line = laurel_own.shape[1]
    gain_lines = -(-gain_total // line)
    gains_block = jnp.pad(gains_own, (0, gain_lines * line - gain_total)).reshape(gain_lines, line)
    first_own = jnp.concatenate(
        [laurel_own, jnp.pad(gains_block, ((0, 16 - gain_lines), (0, 0)))], axis=0
    )

    spread = jnp.broadcast_to(first_own[None], (col_total,) + first_own.shape)
    first_group = lax.all_to_all(spread, COL, 0, 0, tiled=True)
    first_all = jnp.stack(direct_gather(first_group, ROW, row_total))
    laurel_all = first_all[:, :, :small_rows].reshape(-1, line)
    laurel_down_all = laurel_all[:, :rank]
    laurel_up_all = laurel_all[:, rank:]
    gain_rows = first_all[:, :, small_rows : small_rows + gain_lines].astype(wide)
    gain_rows = gain_rows.reshape(row_total, col_total, gain_lines * line)
    gains = gain_rows[:, :, : 6 * small_rows].reshape(row_total, col_total, 6, small_rows)
    gains = jnp.transpose(gains, (2, 0, 1, 3)).reshape(6, width)
    gain_list = [gains[i] for i in range(6)]
    head_gains = []
    for i in range(2):
        start = 6 * small_rows + i * head_part
        rel = gain_rows[:, :, start : start + head_part].reshape(-1)
        head_gains.append(xor_blocks(rel, me_row, row_total))

    kv_pieces, kv_first, kv_last = gather_weight(
        jnp.concatenate([key_weight, value_weight], axis=1), pairs, row_total, True
    )
    query_pieces, _, query_last = gather_weight(
        query_weight, pairs, row_total, False, kv_first, kv_last
    )
    tokens_at = me_col * rows + jnp.arange(rows, dtype=jnp.int32)
    position, begin, reach = placement_info(seq_lengths[0], tokens_at)
    window = jnp.stack([begin, reach])
    span = jnp.stack([jnp.min(begin) // rows, (jnp.max(reach) + rows - 1) // rows])
    inputs = xor_blocks(layer_input, me_row, row_total).astype(wide)
    cotangent = xor_blocks(out_cotangent, me_row, row_total).astype(wide)
    normed, input_pull = jax.vjp(rms_scale, inputs, gain_list[0])
    normed_low = normed.astype(low)
    cosine, sine_part = angles(position)
    query_gain_row = head_gains[0].reshape(1, HEAD)
    key_gain_row = head_gains[1].reshape(1, HEAD)
    kv_own = project(me, normed_low, kv_pieces)
    pair_own = small_call(
        partial(pair_body, col_total),
        jax.ShapeDtypeStruct((2, rows, KV_HEADS * HEAD), low),
        kv_own,
        key_gain_row,
        cosine,
        sine_part,
    )
    pair_all = lax.all_gather(pair_own, COL, axis=0, tiled=True)
    pair_all = pair_all.reshape(col_total, 2, rows, KV_HEADS * HEAD)
    query_own = project(me, normed_low, query_pieces)
    query_scaled = small_call(
        partial(query_body, 1.0 / math.sqrt(HEAD)),
        jax.ShapeDtypeStruct((rows, HEADS * HEAD), low),
        query_own,
        query_gain_row,
        cosine,
        sine_part,
    )
    attended, inverse = attend(span, jnp.transpose(window), query_scaled, pair_all)
    out_pieces, _, out_last = gather_weight(
        out_weight, pairs, row_total, False, kv_first, query_last, attended
    )
    attention_out = contract(me, attended, out_pieces)
    laurel_mid = product(normed_low, laurel_down_all).astype(low)
    laurel_out = product_t(laurel_mid, laurel_up_all)
    (mixed, feed_in), mix_pull = jax.vjp(
        residual_mix,
        inputs,
        attention_out,
        normed_low.astype(wide),
        laurel_out,
        gain_list[1],
        gain_list[2],
        gain_list[3],
    )
    feed_low = feed_in.astype(low)
    feed_pieces = xor_gather(
        after(jnp.concatenate([gate_weight, up_weight], axis=1), out_last), ROW, row_total, feed_low
    )
    layer_own = jnp.concatenate([per_layer_gate, per_layer_projection], axis=1)
    feed_all = jnp.concatenate(feed_pieces, axis=0)
    down_pieces = xor_gather(down_weight, ROW, row_total, feed_low)
    down_all = jnp.concatenate(down_pieces, axis=0)
    feed_pieces = xor_gather(feed_low, COL, pairs)
    feed_pairs, dones = [], []
    chip = me_col // 2
    hidden_pulls, hidden_lows = [], []
    down_part = jnp.zeros((2 * pairs * rows, width), low)
    for j in range(pairs):
        tokens = join_pair(me, feed_pieces, j, dones)
        feed_pairs.append(tokens)
        gate_up = product(tokens, feed_all).astype(low)
        hidden, hidden_pull = jax.vjp(
            geglu, gate_up[:, :feed_width].astype(wide), gate_up[:, feed_width:].astype(wide)
        )
        hidden_low = hidden.astype(low)
        done = product_t(hidden_low, down_all).astype(low)
        place = (lax.bitwise_xor(chip, j) * (2 * rows), 0)
        down_part = lax.dynamic_update_slice(down_part, done, place)
        dones.append(done)
        hidden_pulls.append(hidden_pull)
        hidden_lows.append(hidden_low)
    down_out = lax.psum_scatter(down_part, COL, scatter_dimension=0, tiled=True).astype(wide)
    layer_group = over_col(me, after(layer_own, done), pairs)
    layer_pieces = direct_gather(layer_group, ROW, row_total)
    layer_all = jnp.concatenate([one.reshape(-1, 2 * embed) for one in layer_pieces], axis=0)
    layer_gate_all = layer_all[:, :embed]
    layer_proj_all = layer_all[:, embed:]
    after_feed, feed_pull = jax.vjp(feed_mix, mixed, down_out, gain_list[4])
    after_low = after_feed.astype(low)
    per_pre = product(after_low, layer_gate_all)
    per_hidden, per_pull = jax.vjp(geglu, per_pre, per_layer_input.astype(wide))
    per_low = per_hidden.astype(low)
    per_out = product_t(per_low, layer_proj_all)
    output, final_pull = jax.vjp(final_mix, after_feed, per_out, gain_list[5])
    after_grad, per_out_grad, final_gain_grad = final_pull(cotangent)
    per_out_low = per_out_grad.astype(low)
    per_hidden_grad = product(per_out_low, layer_proj_all)
    layer_proj_grad = product_tn(per_out_low, per_low)
    per_pre_grad, embed_grad = per_pull(per_hidden_grad)
    per_pre_low = per_pre_grad.astype(low)
    after_grad = after_grad + product_t(per_pre_low, layer_gate_all)
    layer_gate_grad = product_tn(after_low, per_pre_low)
    mixed_grad, down_grad, post_gain_grad = feed_pull(after_grad)
    down_low = down_grad.astype(low)
    layer_grad = scatter_small(
        me,
        after(jnp.concatenate([layer_gate_grad, layer_proj_grad], axis=1).astype(low), down_low),
        row_total,
        col_total,
    )
    attended_pair = pair_columns(me, after(attended, down_low), col_total)
    normed_pair = pair_rows(after(normed_low, down_low))
    down_pieces = [down_low]
    down_pairs, dones = [], []
    feed_in_part = jnp.zeros((2 * pairs * rows, width), low)
    feed_grads = []
    for j in range(pairs):
        if j == 1:
            down_pieces = xor_gather(down_low, COL, pairs, dones[0])
        tokens = join_pair(me, down_pieces, j, dones)
        if j == pairs - 1:
            tokens, layer_grad, attended_pair, normed_pair = lax.optimization_barrier(
                (tokens, layer_grad, attended_pair, normed_pair)
            )
        down_pairs.append(tokens)
        hidden_grad = product(tokens, down_all)
        gate_grad, up_grad = [one.astype(low) for one in hidden_pulls[j](hidden_grad)]
        feed_grad_low = jnp.concatenate([gate_grad, up_grad], axis=1)
        done = product_t(feed_grad_low, feed_all).astype(low)
        place = (lax.bitwise_xor(chip, j) * (2 * rows), 0)
        feed_in_part = lax.dynamic_update_slice(feed_in_part, done, place)
        dones.append(done)
        feed_grads.append((gate_grad, up_grad))
    feed_in_grad = lax.psum_scatter(
        feed_in_part, COL, scatter_dimension=0, tiled=True
    ).astype(wide)

    def over_chips(lefts, rights, marker):
        total = None
        for j in range(pairs):
            part = product_tn(after(lefts[j], marker), rights[j])
            total = (part if total is None else part + total.astype(wide)).astype(low)
        return total

    down_total = over_chips(down_pairs, hidden_lows, done)
    gate_total = over_chips(feed_pairs, [one[0] for one in feed_grads], down_total)
    up_total = over_chips(feed_pairs, [one[1] for one in feed_grads], gate_total)
    (
        inputs_grad,
        attention_grad,
        normed_grad,
        laurel_out_grad,
        attention_gain_grad,
        laurel_gain_grad,
        pre_gain_grad,
    ) = mix_pull((mixed_grad, feed_in_grad))
    attention_low = attention_grad.astype(low)
    attended_grad = project(me, attention_low, out_pieces)
    query_rot_grad, pair_parts = attend_back(
        span, window, query_scaled, pair_all, attended_grad, attended, inverse
    )
    pair_sum = lax.psum_scatter(
        pair_parts.reshape(2 * col_total, rows, KV_HEADS * HEAD),
        COL,
        scatter_dimension=0,
        tiled=True,
    )
    attention_pair = pair_rows(attention_low)
    out_total = product_tn(after(attention_pair, pair_parts), attended_pair).astype(low)
    query_rot_grad = after(query_rot_grad, out_total)
    gain_row = jax.ShapeDtypeStruct((1, HEAD), wide)
    query_low, query_gain_grad = small_call(
        query_back_body,
        (jax.ShapeDtypeStruct((rows, HEADS * HEAD), low), gain_row),
        query_own,
        query_rot_grad,
        query_gain_row,
        cosine,
        sine_part,
    )
    query_total = product_tn(
        after(normed_pair, out_total), pair_columns(me, query_low, col_total)
    ).astype(low)
    query_part = contract(me, after(query_low, query_total), query_pieces)

    laurel_out_low = after(laurel_out_grad.astype(low), query_total)
    laurel_mid_grad = product(laurel_out_low, laurel_up_all)
    laurel_up_grad = product_tn(laurel_out_low, laurel_mid)
    laurel_mid_low = laurel_mid_grad.astype(low)
    laurel_down_grad = product_tn(normed_low, laurel_mid_low)
    small_total = jnp.concatenate([laurel_down_grad, laurel_up_grad], axis=1)
    normed_grad = normed_grad + product_t(laurel_mid_low, laurel_down_all) + query_part
    pair_sum = after(pair_sum, normed_grad, small_total)
    kv_grad, key_gain_grad = small_call(
        partial(pair_back_body, col_total),
        (jax.ShapeDtypeStruct(kv_own.shape, low), gain_row),
        kv_own,
        pair_sum,
        key_gain_row,
        cosine,
        sine_part,
    )
    kv_total = product_tn(normed_pair, pair_columns(me, kv_grad, col_total)).astype(low)
    marks = []
    normed_grad = normed_grad + contract(me, after(kv_grad, kv_total), kv_pieces)
    kv_weight_grad = scatter_cols(kv_total, row_total, pairs, normed_grad, None, marks)
    mark = marks[0]
    query_marks = []
    query_weight_grad = scatter_cols(query_total, row_total, pairs, mark, mark, query_marks)
    out_weight_grad = scatter_cols(out_total, row_total, pairs, query_part, normed_grad)
    down_weight_grad = scatter_rows(down_total, row_total, up_total, query_marks[0])
    gate_weight_grad = scatter_rows(gate_total, row_total, up_total, marks[-1])
    up_weight_grad = scatter_rows(up_total, row_total, pair_parts, marks[-1])
    input_part, input_gain_grad = input_pull(after(normed_grad, mark))
    input_total = xor_blocks((inputs_grad + input_part).astype(low), me_row, row_total)

    wide_gains = jnp.stack(
        [
            input_gain_grad,
            attention_gain_grad,
            laurel_gain_grad,
            pre_gain_grad,
            post_gain_grad,
            final_gain_grad,
        ]
    ).reshape(6, row_total, col_total, small_rows)
    wide_gains = jnp.transpose(wide_gains, (1, 2, 0, 3)).reshape(row_total, col_total, -1)
    both_gains = jnp.concatenate([query_gain_grad, key_gain_grad], axis=0)
    both_gains = xor_blocks(both_gains, me_row, row_total)
    both_gains = both_gains.reshape(2, row_total, col_total, head_part)
    both_gains = jnp.transpose(both_gains, (1, 2, 0, 3)).reshape(row_total, col_total, -1)
    gain_sums = jnp.concatenate([wide_gains, both_gains], axis=2)
    gain_sums = jnp.pad(gain_sums, ((0, 0), (0, 0), (0, gain_lines * line - gain_total)))
    gain_sums = gain_sums.reshape(row_total, col_total, gain_lines, line)
    laurel_parts = small_total.reshape(row_total, col_total, small_rows, line)
    sums = after(jnp.concatenate([laurel_parts, gain_sums], axis=2), query_marks[0])
    sums = sums[0] + sum(hop(sums[j], ROW, j) for j in range(1, row_total))
    sums = lax.all_to_all(sums, COL, 0, 0, tiled=True)
    sums = jnp.sum(after(sums, query_marks[-1]), axis=0)
    laurel_grad = sums[:small_rows]
    gain_sums = sums[small_rows:].reshape(-1)
    gain_out = [gain_sums[i * small_rows : (i + 1) * small_rows] for i in range(6)]
    head_out = gain_sums[6 * small_rows : gain_total]
    return (
        xor_blocks(output.astype(low), me_row, row_total),
        input_total,
        embed_grad.astype(low),
        query_weight_grad,
        kv_weight_grad[:, :kv_width],
        kv_weight_grad[:, kv_width:],
        out_weight_grad,
        gate_weight_grad,
        up_weight_grad,
        down_weight_grad,
        laurel_grad[:, :rank],
        laurel_grad[:, rank:],
        layer_grad[:, :embed],
        layer_grad[:, embed:],
        gain_out[0],
        head_out[:head_part],
        head_out[head_part:],
        gain_out[1],
        gain_out[2],
        gain_out[3],
        gain_out[4],
        gain_out[5],
    )


def solution(mesh):
    in_specs = (
        P((ROW, COL), None),
        P((ROW, COL), None),
        P((ROW, COL), None),
        P(ROW, None),
        P(ROW, COL),
        P(ROW, COL),
        P(ROW, COL),
        P(ROW, COL),
        P(ROW, COL),
        P(ROW, COL),
        P(ROW, COL),
        P((ROW, COL), None),
        P((ROW, COL), None),
        P((ROW, COL), None),
        P((ROW, COL), None),
        P((ROW, COL)),
        P((ROW, COL)),
        P((ROW, COL)),
        P((ROW, COL)),
        P((ROW, COL)),
        P((ROW, COL)),
        P((ROW, COL)),
        P((ROW, COL)),
    )
    out_specs = (
        P((ROW, COL), None),
        P((ROW, COL), None),
        P((ROW, COL), None),
        P(ROW, COL),
        P(ROW, COL),
        P(ROW, COL),
        P(ROW, COL),
        P(ROW, COL),
        P(ROW, COL),
        P(ROW, COL),
        P((ROW, COL), None),
        P((ROW, COL), None),
        P((ROW, COL), None),
        P((ROW, COL), None),
        P((ROW, COL)),
        P((ROW, COL)),
        P((ROW, COL)),
        P((ROW, COL)),
        P((ROW, COL)),
        P((ROW, COL)),
        P((ROW, COL)),
        P((ROW, COL)),
    )

    return jax.shard_map(local, mesh=mesh, in_specs=in_specs, out_specs=out_specs, check_vma=False)
```

```python
from functools import partial
import math

import jax
import jax.numpy as jnp
from jax import lax
from jax.experimental import pallas as pl
from jax.experimental.pallas import tpu as pltpu
from jax.sharding import PartitionSpec as P


HEADS = 8
KV_HEADS = 2
HEAD = 256
BLOCK = 256
ROW = "row"
COL = "col"


NORM_EPS = 1e-06
ROOT_HALF = 0.7071067811865476
ROPE_THETA = 1000000.0


def rms_scale(values, scale_gain):
    return (
        values
        * lax.rsqrt(jnp.mean(values * values, axis=-1, keepdims=True) + NORM_EPS)
        * scale_gain
    )


def angles(position):
    half_width = HEAD // 2
    steps_up = jnp.arange(half_width, dtype=jnp.float32)
    frequency = jnp.exp(steps_up * (-2.0 * math.log(ROPE_THETA) / HEAD))
    angle_grid = position.astype(jnp.float32)[:, None] * frequency[None, :]
    return (jnp.cos(angle_grid), jnp.sin(angle_grid))


def turn(values, cosine, sine_part):
    half_width = HEAD // 2
    first_half = values[:, :half_width]
    second_half = values[:, half_width:]
    return jnp.concatenate(
        [
            first_half * cosine - second_half * sine_part,
            second_half * cosine + first_half * sine_part,
        ],
        axis=1,
    )


def inverse_rms(values):
    return lax.rsqrt(jnp.mean(values * values, axis=1, keepdims=True) + NORM_EPS)


def norm_back(values, inverse, grad):
    return inverse * (
        grad - values * (inverse * inverse * jnp.mean(grad * values, axis=1, keepdims=True))
    )


def query_body(scale, query_ref, gain_ref, cosine_ref, sine_ref, out_ref):
    for head in range(query_ref.shape[1] // HEAD):
        span = slice(head * HEAD, (head + 1) * HEAD)
        values = query_ref[:, span].astype(jnp.float32)
        normed = values * inverse_rms(values) * gain_ref[...]
        turned = turn(normed, cosine_ref[...], sine_ref[...]).astype(jnp.bfloat16)
        out_ref[:, span] = turned * jnp.bfloat16(scale)


def query_back_body(query_ref, grad_ref, gain_ref, cosine_ref, sine_ref, out_ref, gain_grad_ref):
    total = jnp.zeros((1, HEAD), jnp.float32)
    for head in range(query_ref.shape[1] // HEAD):
        span = slice(head * HEAD, (head + 1) * HEAD)
        values = query_ref[:, span].astype(jnp.float32)
        inverse = inverse_rms(values)
        grad = turn(grad_ref[:, span], cosine_ref[...], -sine_ref[...])
        total = total + jnp.sum(grad * values * inverse, axis=0, keepdims=True)
        out_ref[:, span] = norm_back(values, inverse, grad * gain_ref[...]).astype(jnp.bfloat16)
    gain_grad_ref[...] = total


def head_of(columns, head, kind, count):
    width = columns.shape[1] // count // 2
    per_head = HEAD // width
    parts = [
        columns[:, (2 * c + kind) * width : (2 * c + kind + 1) * width]
        for c in range(head * per_head, (head + 1) * per_head)
    ]
    return jnp.concatenate(parts, axis=1)


def pair_body(count, columns_ref, gain_ref, cosine_ref, sine_ref, out_ref):
    columns = columns_ref[...].astype(jnp.float32)
    for head in range(KV_HEADS):
        span = slice(head * HEAD, (head + 1) * HEAD)
        keys = head_of(columns, head, 0, count)
        normed = keys * inverse_rms(keys) * gain_ref[...]
        out_ref[0, :, span] = turn(normed, cosine_ref[...], sine_ref[...]).astype(jnp.bfloat16)
        values = head_of(columns, head, 1, count)
        out_ref[1, :, span] = (values * inverse_rms(values)).astype(jnp.bfloat16)


def pair_back_body(
    count, columns_ref, grad_ref, gain_ref, cosine_ref, sine_ref, out_ref, gain_grad_ref
):
    columns = columns_ref[...].astype(jnp.float32)
    width = columns.shape[1] // count // 2
    total = jnp.zeros((1, HEAD), jnp.float32)
    pieces = []
    for head in range(KV_HEADS):
        span = slice(head * HEAD, (head + 1) * HEAD)
        keys = head_of(columns, head, 0, count)
        inverse = inverse_rms(keys)
        grad = grad_ref[0, :, span].astype(jnp.float32)
        grad = turn(grad, cosine_ref[...], -sine_ref[...])
        total = total + jnp.sum(grad * keys * inverse, axis=0, keepdims=True)
        key_grad = norm_back(keys, inverse, grad * gain_ref[...])
        values = head_of(columns, head, 1, count)
        value_grad = norm_back(
            values, inverse_rms(values), grad_ref[1, :, span].astype(jnp.float32)
        )
        for c in range(HEAD // width):
            pieces.append(key_grad[:, c * width : (c + 1) * width])
            pieces.append(value_grad[:, c * width : (c + 1) * width])
    out_ref[...] = jnp.concatenate(pieces, axis=1).astype(jnp.bfloat16)
    gain_grad_ref[...] = total


def small_call(body, shapes, *operands):
    size = 4 * sum(one.size for one in operands)
    return pl.pallas_call(
        body,
        out_shape=shapes,
        cost_estimate=pl.CostEstimate(flops=4 * size, transcendentals=0, bytes_accessed=size),
    )(*operands)


def placement_info(lengths, tokens_at):
    finish = jnp.cumsum(lengths)
    begins = finish - lengths
    segment = jnp.sum((tokens_at[:, None] >= finish[None, :]).astype(jnp.int32), axis=1)
    chosen = segment[:, None] == jnp.arange(lengths.shape[0], dtype=jnp.int32)[None, :]
    begin = jnp.sum(jnp.where(chosen, begins[None, :], 0), axis=1)
    end = jnp.sum(jnp.where(chosen, finish[None, :], 0), axis=1)
    position = tokens_at - begin
    reach = jnp.minimum(end, begin + (position // BLOCK + 1) * BLOCK)
    return (position, begin, reach)


def geglu(gate_in, up_in):
    return jax.nn.gelu(gate_in, approximate=True) * up_in


def residual_mix(inputs, attention_out, normed, laurel_out, attention_gain, laurel_gain, pre_gain):
    mixed = (
        inputs
        + rms_scale(attention_out, attention_gain)
        + normed
        + rms_scale(laurel_out, laurel_gain)
    ) * ROOT_HALF
    return (mixed, rms_scale(mixed, pre_gain))


def feed_mix(mixed, down_out, post_gain):
    return mixed + rms_scale(down_out, post_gain)


def final_mix(after_feed, per_out, final_gain):
    return after_feed + rms_scale(per_out, final_gain)


def product(left, right):
    return jnp.dot(left, right, preferred_element_type=jnp.float32)


def product_t(left, right):
    return lax.dot_general(
        left, right, (((1,), (1,)), ((), ())), preferred_element_type=jnp.float32
    )


def product_tn(left, right):
    return lax.dot_general(
        left, right, (((0,), (0,)), ((), ())), preferred_element_type=jnp.float32
    )


def hop(values, axis, mask):
    size = lax.axis_size(axis)
    return lax.ppermute(values, axis, [(i, i ^ mask) for i in range(size)])


def split_hop(values, even_mask, odd_mask):
    size = lax.axis_size(ROW) * lax.axis_size(COL)
    pairs = [(i, i ^ (odd_mask if i % 2 else even_mask)) for i in range(size)]
    return lax.ppermute(values, (ROW, COL), pairs)


def after(values, *others):
    return lax.optimization_barrier((values,) + others)[0]


def xor_blocks(values, me, count):
    width = values.shape[-1] // count
    blocks = [values[..., i * width : (i + 1) * width] for i in range(count)]
    bit = 1
    while bit < count:
        flip = (me & bit) != 0
        blocks = [jnp.where(flip, blocks[i ^ bit], blocks[i]) for i in range(count)]
        bit *= 2
    return jnp.concatenate(blocks, axis=-1)


def unit_of(axis):
    return lax.axis_size(COL) if axis == ROW else 2


def direct_gather(piece, axis, count):
    unit = 1 if axis == ROW else 2
    return [piece] + [hop(piece, axis, j * unit) for j in range(1, count)]


def xor_gather(piece, axis, count, middle=None):
    unit = 1 if axis == ROW else 2
    if count == 4:
        near = hop(piece, axis, unit)
        far = hop(piece, axis, 2 * unit)
        odd = lax.axis_index(COL) % 2 == 1
        flat = unit_of(axis)
        chosen_far, chosen_near = far, near
        if middle is not None:
            chosen_far, chosen_near = after(far, middle), after(near, middle)
        across = split_hop(jnp.where(odd, chosen_far, chosen_near), 2 * flat, flat)
        return [piece, near, far, across]
    pieces = [piece]
    bit = 1
    while bit < count:
        pieces = pieces + [hop(one, axis, bit * unit) for one in pieces]
        bit *= 2
    return pieces


def add_low(left, right):
    return (left.astype(jnp.float32) + right.astype(jnp.float32)).astype(jnp.bfloat16)


def xor_scatter(parts, axis, late=None, last=None, marks=None):
    count = parts.shape[0]
    unit = 1 if axis == ROW else 2
    if marks is not None and count != 4:
        marks.append(parts[0])
    if count == 4:
        odd = lax.axis_index(COL) % 2 == 1
        flat = unit_of(axis)
        across = split_hop(parts[3], 2 * flat, flat)
        early = split_hop(jnp.where(odd, parts[1], parts[2]), 2 * flat, flat)
        if late is not None:
            across = after(across, late)
        rest = add_low(jnp.where(odd, parts[2], parts[1]), across)
        if marks is not None:
            marks.append(rest)
        rest = split_hop(rest, flat, 2 * flat)
        if last is not None:
            rest = after(rest, last)
            early = after(early, last)
        return parts[0].astype(jnp.float32) + early.astype(jnp.float32) + rest.astype(jnp.float32)
    parts = [parts[j] for j in range(count)]
    bit = count // 2
    while bit > 0:
        parts = [add_low(parts[j], hop(parts[j + bit], axis, bit * unit)) for j in range(bit)]
        bit //= 2
    return parts[0].astype(jnp.float32)


def scatter_rows(total, row_total, late=None, last=None, marks=None):
    parts = total.reshape(row_total, -1, total.shape[1])
    return xor_scatter(parts, ROW, late, last, marks)


def scatter_cols(total, row_total, pairs, late=None, last=None, marks=None):
    mine = scatter_rows(total, row_total, late, last, marks).astype(jnp.bfloat16)
    width = mine.shape[1] // pairs
    parts = jnp.stack([mine[:, z * width : (z + 1) * width] for z in range(pairs)])
    return xor_scatter(parts, COL, None, None, marks)


def deal_rows_body(pairs, me_ref, block_ref, keep_ref, give_ref):
    for z in range(pairs):
        keep_ref[z] = block_ref[lax.bitwise_xor(me_ref[0], 2 * z)]
        give_ref[z] = block_ref[lax.bitwise_xor(me_ref[0], 2 * z + 1)]


def scatter_small(me, total, row_total, col_total):
    pairs = col_total // 2
    width = total.shape[1]
    blocks = total.reshape(row_total, col_total, -1, width)
    height = blocks.shape[2]
    half = jax.ShapeDtypeStruct((row_total, pairs, height, width), total.dtype)
    out_block = pl.BlockSpec((None, pairs, height, width), lambda r, s: (r, 0, 0, 0))
    keep, give = pl.pallas_call(
        partial(deal_rows_body, pairs),
        out_shape=(half, half),
        grid_spec=pltpu.PrefetchScalarGridSpec(
            num_scalar_prefetch=1,
            grid=(row_total,),
            in_specs=[
                pl.BlockSpec((None, col_total, height, width), lambda r, s: (r, 0, 0, 0))
            ],
            out_specs=(out_block, out_block),
        ),
        cost_estimate=pl.CostEstimate(
            flops=0, transcendentals=0, bytes_accessed=4 * total.size
        ),
    )(me, blocks)
    both = add_low(keep, hop(give, COL, 1)).reshape(row_total, pairs * height, width)
    mine = xor_scatter(both, ROW).astype(jnp.bfloat16)
    return xor_scatter(mine.reshape(pairs, height, width), COL)


def stack_body(*refs):
    for i, ref in enumerate(refs[:-1]):
        refs[-1][i] = ref[...]


def stack_pieces(pieces):
    shape = (len(pieces),) + pieces[0].shape
    return pl.pallas_call(
        stack_body,
        out_shape=jax.ShapeDtypeStruct(shape, pieces[0].dtype),
        cost_estimate=pl.CostEstimate(
            flops=0, transcendentals=0, bytes_accessed=4 * math.prod(shape)
        ),
    )(*pieces)


def gather_weight(shard, pairs, row_total, direct, first=None, second=None, middle=None):
    along = direct_gather(shard if first is None else after(shard, first), COL, pairs)
    stacked = stack_pieces(along)
    if second is not None:
        stacked = after(stacked, second)
    if direct:
        mine = direct_gather(stacked, ROW, row_total)
    else:
        mine = xor_gather(stacked, ROW, row_total, middle)
    other = [hop(one, COL, 1) for one in mine]
    return (mine, other), along[-1], mine[-1]


def place_body(pairs, me_ref, own_ref, other_ref, out_ref):
    for z in range(pairs):
        out_ref[lax.bitwise_xor(me_ref[0], 2 * z)] = own_ref[z]
        out_ref[lax.bitwise_xor(me_ref[0], 2 * z + 1)] = other_ref[z]


def over_col(me, own, pairs):
    stacked = stack_pieces(direct_gather(own, COL, pairs))
    other = hop(stacked, COL, 1)
    vmem = pl.BlockSpec(memory_space=pltpu.VMEM)
    return pl.pallas_call(
        partial(place_body, pairs),
        out_shape=jax.ShapeDtypeStruct((2 * pairs,) + own.shape, own.dtype),
        in_specs=[pl.BlockSpec(memory_space=pltpu.SMEM), vmem, vmem],
    )(me, stacked, other)


def block_of(ref, index, width):
    if len(ref.shape) == 3:
        return ref.at[index]
    return ref.at[:, pl.ds(pl.multiple_of(index * width, 128), width)]


def blocked(values, count):
    rows = values.shape[0]
    width = values.shape[1] // count
    if width % 128 == 0:
        return values
    return jnp.transpose(values.reshape(rows, count, width), (1, 0, 2))


def project_body(me_ref, left_ref, *refs):
    pieces, out_ref = refs[:-1], refs[-1]
    row_total = len(pieces) // 2
    pairs, height, width = pieces[0].shape
    for z in range(pairs):
        for core in range(2):
            total = None
            for r in range(row_total):
                part = jnp.dot(
                    left_ref[:, r * height : (r + 1) * height],
                    pieces[core * row_total + r][z],
                    preferred_element_type=jnp.float32,
                )
                total = part if total is None else total + part
            out = block_of(out_ref, lax.bitwise_xor(me_ref[0], 2 * z + core), width)
            out[...] = total.astype(out_ref.dtype)


def contract_body(me_ref, left_ref, *refs):
    pieces, out_ref = refs[:-1], refs[-1]
    row_total = len(pieces) // 2
    pairs, height, width = pieces[0].shape
    for r in range(row_total):
        total = None
        for z in range(pairs):
            for core in range(2):
                block = block_of(left_ref, lax.bitwise_xor(me_ref[0], 2 * z + core), width)
                part = lax.dot_general(
                    block[...],
                    pieces[core * row_total + r][z],
                    (((1,), (1,)), ((), ())),
                    preferred_element_type=jnp.float32,
                )
                total = part if total is None else total + part
        out_ref[:, r * height : (r + 1) * height] = total


def whole_call(body, shape, dtype, flops, me, left, pieces):
    mine, other = pieces
    operands = [left, *mine, *other]
    size = sum(one.size for one in operands) * 2
    vmem = pl.BlockSpec(memory_space=pltpu.VMEM)
    return pl.pallas_call(
        body,
        out_shape=jax.ShapeDtypeStruct(shape, dtype),
        in_specs=[pl.BlockSpec(memory_space=pltpu.SMEM)] + [vmem] * len(operands),
        out_specs=vmem,
        cost_estimate=pl.CostEstimate(flops=flops, transcendentals=0, bytes_accessed=size),
    )(me, *operands)


def project(me, left, pieces):
    pairs, _, width = pieces[0][0].shape
    rows = left.shape[0]
    shape = (rows, 2 * pairs * width) if width % 128 == 0 else (2 * pairs, rows, width)
    flops = 4 * rows * left.shape[1] * pairs * width
    out = whole_call(project_body, shape, jnp.bfloat16, flops, me, left, pieces)
    if len(shape) == 3:
        out = jnp.transpose(out, (1, 0, 2)).reshape(rows, 2 * pairs * width)
    return out


def contract(me, left, pieces):
    pairs, height, _ = pieces[0][0].shape
    shape = (left.shape[0], len(pieces[0]) * height)
    flops = 2 * left.size * shape[1]
    left = blocked(left, 2 * pairs)
    return whole_call(contract_body, shape, jnp.float32, flops, me, left, pieces)


def deal_body(pairs, me_ref, columns_ref, keep_ref, give_ref):
    width = keep_ref.shape[1] // pairs
    for z in range(pairs):
        span = slice(z * width, (z + 1) * width)
        for core, out_ref in enumerate((keep_ref, give_ref)):
            index = lax.bitwise_xor(me_ref[0], 2 * z + core)
            out_ref[:, span] = block_of(columns_ref, index, width)[...]


def pair_columns(me, columns, count):
    rows, width = columns.shape
    half = jax.ShapeDtypeStruct((rows, width // 2), columns.dtype)
    values = blocked(columns, count)
    keep, give = pl.pallas_call(
        partial(deal_body, count // 2),
        out_shape=(half, half),
        in_specs=[
            pl.BlockSpec(memory_space=pltpu.SMEM),
            pl.BlockSpec(memory_space=pltpu.VMEM),
        ],
        cost_estimate=pl.CostEstimate(
            flops=0, transcendentals=0, bytes_accessed=4 * rows * width
        ),
    )(me, values)
    return jnp.concatenate([keep, hop(give, COL, 1)], axis=0)


def pair_rows(own):
    return jnp.concatenate([own, hop(own, COL, 1)], axis=0)


def attend_body(span_ref, window_ref, query_ref, key_ref, value_ref, out_ref, inverse_ref, sums, weights):
    rows = query_ref.shape[0]
    low_edge = window_ref[:, 0:1]
    high_edge = window_ref[:, 1:2]
    query = query_ref[...]
    sums[...] = jnp.zeros_like(sums)
    weights[...] = jnp.zeros_like(weights)

    def one_tile(tile, carry):
        scores = lax.dot_general(
            query, key_ref[tile], (((1,), (1,)), ((), ())), preferred_element_type=jnp.float32
        )
        place = tile * rows + lax.broadcasted_iota(jnp.int32, scores.shape, 1)
        exps = jnp.where((place >= low_edge) & (place < high_edge), jnp.exp(scores), 0.0)
        part = exps[:, :128]
        for start in range(128, rows, 128):
            part = part + exps[:, start : start + 128]
        weights[...] += part
        sums[...] += jnp.dot(
            exps.astype(jnp.bfloat16), value_ref[tile], preferred_element_type=jnp.float32
        )
        return carry

    lax.fori_loop(span_ref[0], span_ref[1], one_tile, 0)
    inverse = 1.0 / jnp.sum(weights[...], axis=1, keepdims=True)
    out_ref[...] = (sums[...] * inverse).astype(jnp.bfloat16)
    inverse_ref[...] = jnp.broadcast_to(inverse, inverse_ref.shape)


def attend(span, window, query, gathered):
    rows, width = query.shape
    tiles = gathered.shape[0]
    groups = HEADS // KV_HEADS
    half = pl.BlockSpec((rows, HEAD), lambda h, s: (0, h))
    flops = 4 * rows * rows * tiles * width
    return pl.pallas_call(
        attend_body,
        out_shape=(
            jax.ShapeDtypeStruct((rows, width), jnp.bfloat16),
            jax.ShapeDtypeStruct((rows, HEADS * 128), jnp.float32),
        ),
        grid_spec=pltpu.PrefetchScalarGridSpec(
            num_scalar_prefetch=1,
            grid=(HEADS,),
            in_specs=[
                pl.BlockSpec((rows, 2), lambda h, s: (0, 0)),
                half,
                pl.BlockSpec((tiles, None, rows, HEAD), lambda h, s: (0, 0, 0, h // groups)),
                pl.BlockSpec((tiles, None, rows, HEAD), lambda h, s: (0, 1, 0, h // groups)),
            ],
            out_specs=(half, pl.BlockSpec((rows, 128), lambda h, s: (0, h))),
            scratch_shapes=[
                pltpu.VMEM((rows, HEAD), jnp.float32),
                pltpu.VMEM((rows, 128), jnp.float32),
            ],
        ),
        cost_estimate=pl.CostEstimate(
            flops=flops, transcendentals=rows * rows * tiles * HEADS, bytes_accessed=8 * rows * width
        ),
    )(span, window, query, gathered, gathered)


def attend_back_body(
    span_ref, window_ref, query_ref, key_ref, value_ref, grad_ref, out_ref, inverse_ref,
    query_grad_ref, pair_grad_ref, query_sum, key_sum, value_sum,
):
    rows = query_ref.shape[0]
    groups = HEADS // KV_HEADS
    head = pl.program_id(0)
    low_edge = window_ref[0:1, :]
    high_edge = window_ref[1:2, :]
    query = query_ref[...]
    grad_wide = grad_ref[...].astype(jnp.float32)
    inverse = inverse_ref[:, 0:1]
    delta = jnp.sum(grad_wide * out_ref[...].astype(jnp.float32), axis=1, keepdims=True) * inverse
    delta_row = jnp.transpose(jnp.broadcast_to(delta, (rows, 128)))[0:1, :]
    grad_scaled = (grad_wide * inverse).astype(jnp.bfloat16)
    query_sum[...] = jnp.zeros_like(query_sum)

    @pl.when(lax.rem(head, groups) == 0)
    def _():
        key_sum[...] = jnp.zeros_like(key_sum)
        value_sum[...] = jnp.zeros_like(value_sum)

    def one_tile(tile, carry):
        keys = key_ref[tile]
        contract_last = (((1,), (1,)), ((), ()))
        scores = lax.dot_general(keys, query, contract_last, preferred_element_type=jnp.float32)
        place = tile * rows + lax.broadcasted_iota(jnp.int32, scores.shape, 0)
        exps = jnp.where((place >= low_edge) & (place < high_edge), jnp.exp(scores), 0.0)
        prob_grad = lax.dot_general(
            value_ref[tile], grad_scaled, contract_last, preferred_element_type=jnp.float32
        )
        score_grad = (exps * (prob_grad - delta_row)).astype(jnp.bfloat16)
        key_sum[tile] += jnp.dot(score_grad, query, preferred_element_type=jnp.float32)
        value_sum[tile] += jnp.dot(
            exps.astype(jnp.bfloat16), grad_scaled, preferred_element_type=jnp.float32
        )
        query_sum[...] += lax.dot_general(
            score_grad, keys, (((0,), (0,)), ((), ())), preferred_element_type=jnp.float32
        )
        return carry

    lax.fori_loop(span_ref[0], span_ref[1], one_tile, 0)
    query_grad_ref[...] = query_sum[...] * (1.0 / math.sqrt(HEAD))

    @pl.when(lax.rem(head, groups) == groups - 1)
    def _():
        pair_grad_ref[:, 0] = key_sum[...].astype(jnp.bfloat16)
        pair_grad_ref[:, 1] = value_sum[...].astype(jnp.bfloat16)


def attend_back(span, window, query, gathered, grad, out, inverse):
    rows, width = query.shape
    tiles = gathered.shape[0]
    groups = HEADS // KV_HEADS
    half = pl.BlockSpec((rows, HEAD), lambda h, s: (0, h))
    return pl.pallas_call(
        attend_back_body,
        out_shape=(
            jax.ShapeDtypeStruct((rows, width), jnp.float32),
            jax.ShapeDtypeStruct(gathered.shape, jnp.bfloat16),
        ),
        grid_spec=pltpu.PrefetchScalarGridSpec(
            num_scalar_prefetch=1,
            grid=(HEADS,),
            in_specs=[
                pl.BlockSpec((2, rows), lambda h, s: (0, 0)),
                half,
                pl.BlockSpec((tiles, None, rows, HEAD), lambda h, s: (0, 0, 0, h // groups)),
                pl.BlockSpec((tiles, None, rows, HEAD), lambda h, s: (0, 1, 0, h // groups)),
                half,
                half,
                pl.BlockSpec((rows, 128), lambda h, s: (0, h)),
            ],
            out_specs=(
                half,
                pl.BlockSpec((tiles, 2, rows, HEAD), lambda h, s: (0, 0, 0, h // groups)),
            ),
            scratch_shapes=[
                pltpu.VMEM((rows, HEAD), jnp.float32),
                pltpu.VMEM((tiles, rows, HEAD), jnp.float32),
                pltpu.VMEM((tiles, rows, HEAD), jnp.float32),
            ],
        ),
        cost_estimate=pl.CostEstimate(
            flops=10 * rows * rows * tiles * width,
            transcendentals=rows * rows * tiles * HEADS,
            bytes_accessed=16 * rows * width,
        ),
    )(span, window, query, gathered, gathered, grad, out, inverse)


def local(
    layer_input,
    per_layer_input,
    out_cotangent,
    seq_lengths,
    query_weight,
    key_weight,
    value_weight,
    out_weight,
    gate_weight,
    up_weight,
    down_weight,
    laurel_down,
    laurel_up,
    per_layer_gate,
    per_layer_projection,
    input_gain,
    query_gain,
    key_gain,
    attention_gain,
    laurel_gain,
    pre_feed_gain,
    post_feed_gain,
    per_layer_gain,
):
    rows, width = layer_input.shape
    row_total = lax.axis_size(ROW)
    col_total = lax.axis_size(COL)
    pairs = col_total // 2
    me_row = lax.axis_index(ROW)
    me_col = lax.axis_index(COL)
    rank = laurel_down.shape[1]
    embed = per_layer_gate.shape[1]
    kv_width = key_weight.shape[1]
    feed_width = gate_weight.shape[1]
    low = jnp.bfloat16
    wide = jnp.float32

    me = me_col.astype(jnp.int32).reshape(1)
    small_rows = laurel_down.shape[0]
    head_part = query_gain.shape[0]

    gains_own = jnp.concatenate(
        [
            input_gain,
            attention_gain,
            laurel_gain,
            pre_feed_gain,
            post_feed_gain,
            per_layer_gain,
            query_gain,
            key_gain,
        ]
    )
    gain_total = gains_own.shape[0]
    laurel_own = jnp.concatenate([laurel_down, laurel_up], axis=1)
    line = laurel_own.shape[1]
    gain_lines = -(-gain_total // line)
    gains_block = jnp.pad(gains_own, (0, gain_lines * line - gain_total)).reshape(gain_lines, line)
    first_own = jnp.concatenate(
        [laurel_own, jnp.pad(gains_block, ((0, 16 - gain_lines), (0, 0)))], axis=0
    )

    spread = jnp.broadcast_to(first_own[None], (col_total,) + first_own.shape)
    first_group = lax.all_to_all(spread, COL, 0, 0, tiled=True)
    first_all = jnp.stack(direct_gather(first_group, ROW, row_total))
    laurel_all = first_all[:, :, :small_rows].reshape(-1, line)
    laurel_down_all = laurel_all[:, :rank]
    laurel_up_all = laurel_all[:, rank:]
    gain_rows = first_all[:, :, small_rows : small_rows + gain_lines].astype(wide)
    gain_rows = gain_rows.reshape(row_total, col_total, gain_lines * line)
    gains = gain_rows[:, :, : 6 * small_rows].reshape(row_total, col_total, 6, small_rows)
    gains = jnp.transpose(gains, (2, 0, 1, 3)).reshape(6, width)
    gain_list = [gains[i] for i in range(6)]
    head_gains = []
    for i in range(2):
        start = 6 * small_rows + i * head_part
        rel = gain_rows[:, :, start : start + head_part].reshape(-1)
        head_gains.append(xor_blocks(rel, me_row, row_total))

    kv_pieces, kv_first, kv_last = gather_weight(
        jnp.concatenate([key_weight, value_weight], axis=1), pairs, row_total, True
    )
    query_pieces, _, query_last = gather_weight(
        query_weight, pairs, row_total, False, kv_first, kv_last
    )
    tokens_at = me_col * rows + jnp.arange(rows, dtype=jnp.int32)
    position, begin, reach = placement_info(seq_lengths[0], tokens_at)
    window = jnp.stack([begin, reach])
    span = jnp.stack([jnp.min(begin) // rows, (jnp.max(reach) + rows - 1) // rows])
    inputs = xor_blocks(layer_input, me_row, row_total).astype(wide)
    cotangent = xor_blocks(out_cotangent, me_row, row_total).astype(wide)
    normed, input_pull = jax.vjp(rms_scale, inputs, gain_list[0])
    normed_low = normed.astype(low)
    cosine, sine_part = angles(position)
    query_gain_row = head_gains[0].reshape(1, HEAD)
    key_gain_row = head_gains[1].reshape(1, HEAD)
    kv_own = project(me, normed_low, kv_pieces)
    pair_own = small_call(
        partial(pair_body, col_total),
        jax.ShapeDtypeStruct((2, rows, KV_HEADS * HEAD), low),
        kv_own,
        key_gain_row,
        cosine,
        sine_part,
    )
    pair_all = lax.all_gather(pair_own, COL, axis=0, tiled=True)
    pair_all = pair_all.reshape(col_total, 2, rows, KV_HEADS * HEAD)
    query_own = project(me, normed_low, query_pieces)
    query_scaled = small_call(
        partial(query_body, 1.0 / math.sqrt(HEAD)),
        jax.ShapeDtypeStruct((rows, HEADS * HEAD), low),
        query_own,
        query_gain_row,
        cosine,
        sine_part,
    )
    attended, inverse = attend(span, jnp.transpose(window), query_scaled, pair_all)
    out_pieces, _, out_last = gather_weight(
        out_weight, pairs, row_total, False, kv_first, query_last, attended
    )
    attention_out = contract(me, attended, out_pieces)
    laurel_mid = product(normed_low, laurel_down_all).astype(low)
    laurel_out = product_t(laurel_mid, laurel_up_all)
    (mixed, feed_in), mix_pull = jax.vjp(
        residual_mix,
        inputs,
        attention_out,
        normed_low.astype(wide),
        laurel_out,
        gain_list[1],
        gain_list[2],
        gain_list[3],
    )
    feed_low = feed_in.astype(low)
    feed_pieces = xor_gather(
        after(jnp.concatenate([gate_weight, up_weight], axis=1), out_last), ROW, row_total, feed_low
    )
    layer_own = jnp.concatenate([per_layer_gate, per_layer_projection], axis=1)
    feed_all = jnp.concatenate(feed_pieces, axis=0)
    halves = 2
    part_rows = rows // halves
    feed_tokens, hidden_pulls, hidden_lows, down_outs = [], [], [], []
    done = None
    for h in range(halves):
        tokens = lax.all_gather(
            feed_low[h * part_rows : (h + 1) * part_rows], COL, axis=0, tiled=True
        )
        tokens = tokens if done is None else after(tokens, done)
        gate_up = product(tokens, feed_all).astype(low)
        if h == 0:
            down_pieces = xor_gather(down_weight, ROW, row_total, feed_low)
            down_all = jnp.concatenate(down_pieces, axis=0)
        hidden, hidden_pull = jax.vjp(
            geglu, gate_up[:, :feed_width].astype(wide), gate_up[:, feed_width:].astype(wide)
        )
        hidden_low = hidden.astype(low)
        done = product_t(hidden_low, down_all).astype(low)
        down_outs.append(lax.psum_scatter(done, COL, scatter_dimension=0, tiled=True))
        feed_tokens.append(tokens)
        hidden_pulls.append(hidden_pull)
        hidden_lows.append(hidden_low)
    layer_group = over_col(me, after(layer_own, done), pairs)
    layer_pieces = direct_gather(layer_group, ROW, row_total)
    layer_all = jnp.concatenate([one.reshape(-1, 2 * embed) for one in layer_pieces], axis=0)
    layer_gate_all = layer_all[:, :embed]
    layer_proj_all = layer_all[:, embed:]
    down_out = jnp.concatenate(down_outs, axis=0).astype(wide)
    after_feed, feed_pull = jax.vjp(feed_mix, mixed, down_out, gain_list[4])
    after_low = after_feed.astype(low)
    per_pre = product(after_low, layer_gate_all)
    per_hidden, per_pull = jax.vjp(geglu, per_pre, per_layer_input.astype(wide))
    per_low = per_hidden.astype(low)
    per_out = product_t(per_low, layer_proj_all)
    output, final_pull = jax.vjp(final_mix, after_feed, per_out, gain_list[5])
    after_grad, per_out_grad, final_gain_grad = final_pull(cotangent)
    per_out_low = per_out_grad.astype(low)
    per_hidden_grad = product(per_out_low, layer_proj_all)
    layer_proj_grad = product_tn(per_out_low, per_low)
    per_pre_grad, embed_grad = per_pull(per_hidden_grad)
    per_pre_low = per_pre_grad.astype(low)
    after_grad = after_grad + product_t(per_pre_low, layer_gate_all)
    layer_gate_grad = product_tn(after_low, per_pre_low)
    mixed_grad, down_grad, post_gain_grad = feed_pull(after_grad)
    down_low = down_grad.astype(low)
    layer_grad = scatter_small(
        me,
        after(jnp.concatenate([layer_gate_grad, layer_proj_grad], axis=1).astype(low), down_low),
        row_total,
        col_total,
    )
    attended_pair = pair_columns(me, after(attended, down_low), col_total)
    normed_pair = pair_rows(after(normed_low, down_low))
    feed_in_grads = []
    done = None
    for h in range(halves):
        tokens = lax.all_gather(
            down_low[h * part_rows : (h + 1) * part_rows], COL, axis=0, tiled=True
        )
        if done is None:
            tokens, layer_grad, attended_pair, normed_pair = lax.optimization_barrier(
                (tokens, layer_grad, attended_pair, normed_pair)
            )
        else:
            tokens = after(tokens, done, down_first, *feed_first)
        hidden_grad = product(tokens, down_all)
        gate_grad, up_grad = hidden_pulls[h](hidden_grad)
        feed_grad_low = jnp.concatenate([gate_grad.astype(low), up_grad.astype(low)], axis=1)
        done = product_t(feed_grad_low, feed_all).astype(low)
        feed_in_grads.append(lax.psum_scatter(done, COL, scatter_dimension=0, tiled=True))
        if h == 0:
            down_first = product_tn(after(tokens, done), hidden_lows[0]).astype(low)
            feed_first = [
                product_tn(after(feed_tokens[0], down_first), one.astype(low)).astype(low)
                for one in (gate_grad, up_grad)
            ]
    feed_in_grad = jnp.concatenate(feed_in_grads, axis=0).astype(wide)
    down_total = product_tn(after(tokens, done), hidden_lows[1]) + down_first.astype(wide)
    down_total = down_total.astype(low)
    gate_total = product_tn(after(feed_tokens[1], down_total), gate_grad.astype(low))
    gate_total = (gate_total + feed_first[0].astype(wide)).astype(low)
    up_total = product_tn(after(feed_tokens[1], gate_total), up_grad.astype(low))
    up_total = (up_total + feed_first[1].astype(wide)).astype(low)
    (
        inputs_grad,
        attention_grad,
        normed_grad,
        laurel_out_grad,
        attention_gain_grad,
        laurel_gain_grad,
        pre_gain_grad,
    ) = mix_pull((mixed_grad, feed_in_grad))
    attention_low = attention_grad.astype(low)
    attended_grad = project(me, attention_low, out_pieces)
    query_rot_grad, pair_parts = attend_back(
        span, window, query_scaled, pair_all, attended_grad, attended, inverse
    )
    pair_sum = lax.psum_scatter(
        pair_parts.reshape(2 * col_total, rows, KV_HEADS * HEAD),
        COL,
        scatter_dimension=0,
        tiled=True,
    )
    attention_pair = pair_rows(attention_low)
    out_total = product_tn(after(attention_pair, pair_parts), attended_pair).astype(low)
    query_rot_grad = after(query_rot_grad, out_total)
    gain_row = jax.ShapeDtypeStruct((1, HEAD), wide)
    query_low, query_gain_grad = small_call(
        query_back_body,
        (jax.ShapeDtypeStruct((rows, HEADS * HEAD), low), gain_row),
        query_own,
        query_rot_grad,
        query_gain_row,
        cosine,
        sine_part,
    )
    query_total = product_tn(
        after(normed_pair, out_total), pair_columns(me, query_low, col_total)
    ).astype(low)
    query_part = contract(me, after(query_low, query_total), query_pieces)

    laurel_out_low = after(laurel_out_grad.astype(low), query_total)
    laurel_mid_grad = product(laurel_out_low, laurel_up_all)
    laurel_up_grad = product_tn(laurel_out_low, laurel_mid)
    laurel_mid_low = laurel_mid_grad.astype(low)
    laurel_down_grad = product_tn(normed_low, laurel_mid_low)
    small_total = jnp.concatenate([laurel_down_grad, laurel_up_grad], axis=1)
    normed_grad = normed_grad + product_t(laurel_mid_low, laurel_down_all) + query_part
    pair_sum = after(pair_sum, normed_grad, small_total)
    kv_grad, key_gain_grad = small_call(
        partial(pair_back_body, col_total),
        (jax.ShapeDtypeStruct(kv_own.shape, low), gain_row),
        kv_own,
        pair_sum,
        key_gain_row,
        cosine,
        sine_part,
    )
    kv_total = product_tn(normed_pair, pair_columns(me, kv_grad, col_total)).astype(low)
    marks = []
    normed_grad = normed_grad + contract(me, after(kv_grad, kv_total), kv_pieces)
    kv_weight_grad = scatter_cols(kv_total, row_total, pairs, normed_grad, None, marks)
    mark = marks[0]
    query_marks = []
    query_weight_grad = scatter_cols(query_total, row_total, pairs, mark, mark, query_marks)
    out_weight_grad = scatter_cols(out_total, row_total, pairs, query_part, query_marks[0])
    down_weight_grad = scatter_rows(down_total, row_total, up_total, query_marks[0])
    gate_weight_grad = scatter_rows(gate_total, row_total, up_total, query_marks[-1])
    up_weight_grad = scatter_rows(up_total, row_total, pair_parts, query_marks[-1])
    input_part, input_gain_grad = input_pull(after(normed_grad, mark))
    input_total = xor_blocks((inputs_grad + input_part).astype(low), me_row, row_total)

    wide_gains = jnp.stack(
        [
            input_gain_grad,
            attention_gain_grad,
            laurel_gain_grad,
            pre_gain_grad,
            post_gain_grad,
            final_gain_grad,
        ]
    ).reshape(6, row_total, col_total, small_rows)
    wide_gains = jnp.transpose(wide_gains, (1, 2, 0, 3)).reshape(row_total, col_total, -1)
    both_gains = jnp.concatenate([query_gain_grad, key_gain_grad], axis=0)
    both_gains = xor_blocks(both_gains, me_row, row_total)
    both_gains = both_gains.reshape(2, row_total, col_total, head_part)
    both_gains = jnp.transpose(both_gains, (1, 2, 0, 3)).reshape(row_total, col_total, -1)
    gain_sums = jnp.concatenate([wide_gains, both_gains], axis=2)
    gain_sums = jnp.pad(gain_sums, ((0, 0), (0, 0), (0, gain_lines * line - gain_total)))
    gain_sums = gain_sums.reshape(row_total, col_total, gain_lines, line)
    laurel_parts = small_total.reshape(row_total, col_total, small_rows, line)
    sums = after(jnp.concatenate([laurel_parts, gain_sums], axis=2), query_marks[0])
    sums = sums[0] + sum(hop(sums[j], ROW, j) for j in range(1, row_total))
    sums = lax.all_to_all(sums, COL, 0, 0, tiled=True)
    sums = jnp.sum(after(sums, query_marks[-1]), axis=0)
    laurel_grad = sums[:small_rows]
    gain_sums = sums[small_rows:].reshape(-1)
    gain_out = [gain_sums[i * small_rows : (i + 1) * small_rows] for i in range(6)]
    head_out = gain_sums[6 * small_rows : gain_total]
    return (
        xor_blocks(output.astype(low), me_row, row_total),
        input_total,
        embed_grad.astype(low),
        query_weight_grad,
        kv_weight_grad[:, :kv_width],
        kv_weight_grad[:, kv_width:],
        out_weight_grad,
        gate_weight_grad,
        up_weight_grad,
        down_weight_grad,
        laurel_grad[:, :rank],
        laurel_grad[:, rank:],
        layer_grad[:, :embed],
        layer_grad[:, embed:],
        gain_out[0],
        head_out[:head_part],
        head_out[head_part:],
        gain_out[1],
        gain_out[2],
        gain_out[3],
        gain_out[4],
        gain_out[5],
    )


def solution(mesh):
    in_specs = (
        P((ROW, COL), None),
        P((ROW, COL), None),
        P((ROW, COL), None),
        P(ROW, None),
        P(ROW, COL),
        P(ROW, COL),
        P(ROW, COL),
        P(ROW, COL),
        P(ROW, COL),
        P(ROW, COL),
        P(ROW, COL),
        P((ROW, COL), None),
        P((ROW, COL), None),
        P((ROW, COL), None),
        P((ROW, COL), None),
        P((ROW, COL)),
        P((ROW, COL)),
        P((ROW, COL)),
        P((ROW, COL)),
        P((ROW, COL)),
        P((ROW, COL)),
        P((ROW, COL)),
        P((ROW, COL)),
    )
    out_specs = (
        P((ROW, COL), None),
        P((ROW, COL), None),
        P((ROW, COL), None),
        P(ROW, COL),
        P(ROW, COL),
        P(ROW, COL),
        P(ROW, COL),
        P(ROW, COL),
        P(ROW, COL),
        P(ROW, COL),
        P((ROW, COL), None),
        P((ROW, COL), None),
        P((ROW, COL), None),
        P((ROW, COL), None),
        P((ROW, COL)),
        P((ROW, COL)),
        P((ROW, COL)),
        P((ROW, COL)),
        P((ROW, COL)),
        P((ROW, COL)),
        P((ROW, COL)),
        P((ROW, COL)),
    )

    return jax.shard_map(local, mesh=mesh, in_specs=in_specs, out_specs=out_specs, check_vma=False)
```
